256 devices in a mesh: node: 64 (over z, x, core), site: 4 (over y).
Axes of the slice: x: 4, y: 4, z: 8, core: 2. Of those that a mesh axis runs over, the one named last changes fastest.
Arguments:
- leaf_partials: float32 [4096, 4, 4096], P('node', None, 'site'), may hold values from 0.05 to 1
- dag_edges: int32 [3, 12288, 3], P(None, 'node'), may hold values from 0 to 4095, as said below
- weights: float32 [3, 12288], P(None, 'node'), may hold values from 0.25 to 4
- lengths: float32 [3, 12288], P(None, 'node'), may hold values from 0.02 to 2
- counts: int32 [4096], P('site'), may hold values from 1 to 9
- topo_nodes: int32 [256, 8], P('node'), may hold values from 0 to 4095
Outputs:
- topology_loglik: float32 [256], P('node')
- edge_gradient: float32 [12288], P('node')
The draws below stay inside these ranges and needn't reach their ends.
Inputs may be any that keep to these rules, and one draw needn't show every extreme that they name: `dag_edges`: in every level each subsplit is the child of exactly 3 edges, listed on the index of node that owns the child; subsplit n is owned by index n // 64. Column 1 is the parent in the next level, column 2 the rotation (0 or 1). Every parent has at least one edge of each rotation. Among the edges of one index of node, at most 4 have parents owned by any one index, and some index receives exactly 4 from every index.
All inputs are finite; a program needn't handle non-finite values.
Results may differ from the reference program's by a relative error of at most 0.0003.
Values sent between devices are 32-bit elements; how exact they have to be, the bound alone decides.
No kernel may reach another device: no remote copies, remote signals or barrier semaphores. Data moves between devices by JAX's collectives and lax.ppermute only.
A program may use at most 192 MiB of HBM per device.

```python
import math
import jax
import jax.numpy as jnp
from jax import lax

NODE_DEV = 64
LEVELS = 3
USE = 8
NODES = 4096
EDGES = 12288
SITES = 4096
TOPOS = 256
N_NODE = 64


def level_edges(key):
    owners = N_NODE
    node_count = NODE_DEV
    capacity = 4 * node_count // owners
    half_cap = capacity // 2
    busiest = jax.random.randint(jax.random.fold_in(key, 1), (), 0, owners)
    low_keys = jax.random.split(jax.random.fold_in(key, 2), owners)
    low_pairs = jax.vmap(lambda subkey: jax.random.permutation(subkey, 2 * node_count))(low_keys)
    low_pairs = low_pairs.reshape(owners, owners, half_cap).transpose(1, 0, 2)
    high_pairs = jax.random.randint(jax.random.fold_in(key, 3), (owners, owners, half_cap), 0, 2 * node_count)
    pair_table = jnp.concatenate([low_pairs, high_pairs], axis=2).reshape(owners, owners * capacity)
    slot_range = jnp.arange(owners * half_cap)
    high_dest = slot_range // half_cap
    high_slot = high_dest * capacity + half_cap + slot_range % half_cap
    low_slot = slot_range // half_cap * capacity + slot_range % half_cap

    def one_source(source_key, source):
        ranking = jax.random.permutation(jax.random.fold_in(source_key, 1), owners * half_cap)
        priority = ranking + (high_dest != busiest).astype(jnp.int32) * (owners * half_cap)
        picked_slots = jnp.argsort(priority)[:node_count]
        used_slots = jnp.concatenate([low_slot, high_slot[picked_slots]])
        pair_codes = pair_table[source][used_slots]
        destination = used_slots // capacity
        parents = destination * node_count + pair_codes // 2
        rotation = pair_codes % 2
        children = source * node_count + jax.random.permutation(jax.random.fold_in(source_key, 2), jnp.repeat(jnp.arange(node_count), 3))
        shuffle = jax.random.permutation(jax.random.fold_in(source_key, 3), 3 * node_count)
        return jnp.stack([children, parents[shuffle], rotation[shuffle]], axis=1)
    source_keys = jax.random.split(jax.random.fold_in(key, 4), owners)
    return jax.vmap(one_source)(source_keys, jnp.arange(owners)).reshape(owners * 3 * node_count, 3)


def draw_dag_edges(key, part):
    level_keys = jax.random.split(jax.random.fold_in(key, 7), LEVELS)
    return jax.vmap(level_edges)(level_keys).astype(jnp.int32)


def plant(drawn, own_key, low, top_value):
    extent = drawn.shape
    place = [jax.random.randint(jax.random.fold_in(own_key, axis), (), 0, extent[axis]) for axis in range(len(extent))]
    drawn = drawn.at[tuple(place)].set(low)
    longest = extent.index(max(extent))
    place[longest] = (place[longest] + 1) % extent[longest]
    return drawn.at[tuple(place)].set(top_value)


def level_of(key, extent, shards, least, high):
    def one(axis_at, parts):
        steps = jax.random.uniform(jax.random.fold_in(jax.random.fold_in(key, 6), axis_at), (parts,), jnp.float32, least / len(shards), high / len(shards))
        return jnp.repeat(jnp.exp(steps), extent[axis_at] // parts).reshape((-1,) + (1,) * (len(extent) - axis_at - 1))

    loudness = one(*shards[0])
    for cut in shards[1:]:
        loudness = loudness * one(*cut)
    return loudness


def setup_inputs(seed: int = 0) -> dict:
    key_list = jax.random.split(jax.random.key(seed), 7)
    leaf_partials = jnp.clip(0.05 + 0.95 * jax.random.uniform(key_list[0], (NODES, 4, SITES), jnp.float32) ** level_of(key_list[0], (NODES, 4, SITES), ((0, 64), (2, 4)), -0.2, 0.2), 0.05, 1.0)
    dag_edges = draw_dag_edges(jax.random.fold_in(key_list[6], 71), 0)
    weights = jnp.clip(jnp.exp(math.log(4.0) - 2.7725887 * jax.random.uniform(key_list[2], (LEVELS, EDGES), jnp.float32) ** level_of(key_list[2], (LEVELS, EDGES), ((1, 64),), -0.2, 0.2)), 0.25, 4.0)
    lengths = jnp.clip(jnp.exp(math.log(2.0) - 4.6051702 * jax.random.uniform(key_list[3], (LEVELS, EDGES), jnp.float32) ** level_of(key_list[3], (LEVELS, EDGES), ((1, 64),), -0.2, 0.2)), 0.02, 2.0)
    counts = plant(jax.random.randint(key_list[4], (SITES,), 1, 10), jax.random.fold_in(key_list[4], 1), 1, 9).astype(jnp.int32)
    topo_nodes = plant(jax.random.randint(key_list[5], (TOPOS, USE), 0, NODES), jax.random.fold_in(key_list[5], 1), 0, NODES - 1).astype(jnp.int32)
    return {"leaf_partials": leaf_partials, "dag_edges": dag_edges, "weights": weights, "lengths": lengths, "counts": counts, "topo_nodes": topo_nodes}


def transit(child_rows, branch):
    survival = jnp.exp(branch * (-4.0 / 3.0))[:, None, None]
    return survival * child_rows + (1.0 - survival) * 0.25 * jnp.sum(child_rows, axis=1, keepdims=True)


def block_terms(leaf_block, count_block, dag_edges, weights, lengths):
    current = leaf_block
    span = leaf_block.shape[2]
    for level_index in range(LEVELS):
        child_index = dag_edges[level_index, :, 0]
        pair_code = dag_edges[level_index, :, 1] * 2 + dag_edges[level_index, :, 2]
        message = transit(current[child_index], lengths[level_index])
        summed = jax.ops.segment_sum(weights[level_index][:, None, None] * message, pair_code, num_segments=2 * NODES)
        pair_sums = summed.reshape(NODES, 2, 4, span)
        current = pair_sums[:, 0] * pair_sums[:, 1]
    denominator = 0.25 * jnp.sum(current, axis=1)
    scaled = count_block.astype(jnp.float32) / SITES
    node_terms = jnp.sum(scaled[None, :] * jnp.log(denominator), axis=1)
    adjoint = pair_sums[:, ::-1] * (scaled[None, :] * 0.25 / denominator)[:, None, None, :]
    adjoint_rows = adjoint.reshape(2 * NODES, 4, span)[pair_code]
    edge_terms = jnp.sum(message * adjoint_rows, axis=(1, 2))
    return node_terms, edge_terms


def reference(leaf_partials, dag_edges, weights, lengths, counts, topo_nodes):
    site_block = math.gcd(SITES, 512)
    blocks = SITES // site_block
    leaf_blocks = jnp.moveaxis(leaf_partials.reshape(NODES, 4, blocks, site_block), 2, 0)
    count_blocks = counts.reshape(blocks, site_block)

    def one_block(inputs):
        return block_terms(inputs[0], inputs[1], dag_edges, weights, lengths)

    node_parts, edge_parts = lax.map(one_block, (leaf_blocks, count_blocks))
    node_scores = jnp.sum(node_parts, axis=0)
    edge_scores = jnp.sum(edge_parts, axis=0)
    multiplicity = jax.ops.segment_sum(jnp.ones((TOPOS * USE,), jnp.float32), topo_nodes.reshape(-1), num_segments=NODES)
    topology_loglik = jnp.sum(node_scores[topo_nodes], axis=1)
    edge_gradient = multiplicity[dag_edges[LEVELS - 1, :, 1]] * edge_scores
    return topology_loglik, edge_gradient
```

```python
import functools

import jax
import jax.numpy as jnp
from jax import lax
from jax.experimental import pallas as pl
from jax.experimental.pallas import tpu as pltpu
from jax.sharding import PartitionSpec as P

F32 = jnp.float32
BF16 = jnp.bfloat16
LANES = 128


def spread_kernel(leaf_ref, out_ref):
    states = leaf_ref.shape[1]
    for pair in range(states // 2):
        rows = jnp.concatenate([leaf_ref[:, 2 * pair, :], leaf_ref[:, 2 * pair + 1, :]], axis=0)
        out_ref[:, pair * LANES : (pair + 1) * LANES] = rows.T


def two_parts(value):
    high = value.astype(BF16)
    return high, (value - high.astype(F32)).astype(BF16)


def state_sum(value):
    value = value + pltpu.roll(value, 16, 1)
    return value + pltpu.roll(value, 32, 1)


def dag_kernel(
    leaf_ref, meta_ref, topo_ref, scaled_ref, out_ref,
    current_ref, slot_ref, table_ref, score_ref, mult_ref, term_ref,
    *, levels, owners, node_dev, site_own, states, fields,
):
    half = 2 * node_dev
    slots = 4 * owners
    meta_rows = fields * levels * 2
    left = lax.broadcasted_iota(jnp.int32, (LANES, LANES), 1) < LANES // 2
    left_nodes = left[:node_dev]

    def store_current(start, value, mask):
        high = value.astype(BF16).astype(F32)
        current_ref[pl.ds(start, value.shape[0]), :] = jnp.where(
            mask, high, value - high
        ).astype(BF16)

    for level in range(levels):
        for field in range(1, fields):
            for part in range(2):
                row = (field * levels + level) * 2 + part
                block = meta_ref[pl.ds(row, owners, stride=meta_rows), :].T
                table_ref[
                    pl.ds((level * (fields - 1) + field - 1) * owners, owners),
                    part * LANES : (part + 1) * LANES,
                ] = jnp.concatenate([block[:owners], block[owners:]], axis=1)

    def count_uses(chunk, total):
        entry = topo_ref[pl.ds(chunk, 1), :]
        owner_of = entry // node_dev
        local_of = entry - owner_of * node_dev
        owner_hot = (lax.broadcasted_iota(jnp.int32, (LANES, LANES), 0) == owner_of).astype(F32)
        local_hot = (lax.broadcasted_iota(jnp.int32, (node_dev, LANES), 0) == local_of).astype(F32)
        return total + lax.dot_general(
            local_hot.astype(BF16), owner_hot.astype(BF16), (((1,), (1,)), ((), ())),
            preferred_element_type=F32,
        )

    mult_ref[...] = lax.fori_loop(
        0, topo_ref.shape[0], count_uses, jnp.zeros((node_dev, LANES), F32)
    )

    def load_leaves(pair, carry):
        first = leaf_ref[pl.ds(pl.multiple_of(pair * 2 * site_own, 2 * site_own), site_own), :]
        second = leaf_ref[
            pl.ds(pl.multiple_of(pair * 2 * site_own, 2 * site_own) + site_own, site_own), :
        ]
        pieces = []
        for block in range(states // 2):
            a = first[:, block * LANES : (block + 1) * LANES]
            b = second[:, block * LANES : (block + 1) * LANES]
            pieces.append(jnp.where(left[:site_own], a, pltpu.roll(b, LANES // 2, 1)))
            pieces.append(jnp.where(left[:site_own], pltpu.roll(a, LANES // 2, 1), b))
        stacked = jnp.concatenate(pieces + pieces, axis=0)
        store_current(pl.multiple_of(pair * LANES, LANES), stacked.T, left)
        return carry

    lax.fori_loop(0, owners // 2, load_leaves, 0)

    node_row = lax.broadcasted_iota(jnp.int32, (node_dev, LANES), 0).astype(F32) + 1.0
    pair_row = lax.broadcasted_iota(jnp.int32, (half, slots), 0).astype(F32) + 1.0

    def spread(level):
        def body(source, carry):
            rows = current_ref[pl.ds(pl.multiple_of(source * node_dev, node_dev), node_dev), :]
            for part in range(2):
                child = meta_ref[pl.ds(source * meta_rows + level * 2 + part, 1), :]
                hot = (node_row == child).astype(F32).astype(BF16)
                picked = lax.dot_general(
                    hot, rows, (((0,), (0,)), ((), ())), preferred_element_type=F32
                )
                slot_ref[pl.ds(part * half * owners + source, half, stride=owners), :] = picked
            return carry

        lax.fori_loop(0, owners, body, 0, unroll=4)

    def gather(level, last):
        def body(dest, carry):
            pieces = [
                slot_ref[pl.ds(pl.multiple_of((rank * owners + dest) * owners, owners), owners), :]
                for rank in range(4)
            ]
            rows = jnp.concatenate(pieces, axis=0).astype(BF16)
            base = level * (fields - 1) * owners + dest
            code = table_ref[pl.ds(base, 1), :]
            weight = table_ref[pl.ds(base + owners, 1), :]
            survival = table_ref[pl.ds(base + 2 * owners, 1), :]
            spread_out = (1.0 - survival) * 0.25
            hit = pair_row == code

            def weighted(scale):
                high = scale.astype(BF16).astype(F32)
                low = scale - high
                return sum(
                    jnp.dot(
                        jnp.where(hit, piece, 0.0).astype(BF16), rows, preferred_element_type=F32
                    )
                    for piece in (high, low)
                )

            sums = weighted(weight * survival) + state_sum(weighted(weight * spread_out))
            sums = sums + pltpu.roll(sums, LANES // 2, 1)
            value = sums[:node_dev] * sums[node_dev:]
            if not last:
                store_current(pl.multiple_of(dest * node_dev, node_dev), value, left_nodes)
                return carry
            scaled = scaled_ref[...]
            likelihood = 0.25 * state_sum(value)
            lane = lax.broadcasted_iota(jnp.int32, (node_dev, LANES), 1)
            logs = scaled * jnp.log(likelihood)
            high = logs.astype(BF16).astype(F32)
            middle = (logs - high).astype(BF16).astype(F32)
            packed = jnp.where(
                lane < site_own, high,
                jnp.where(
                    lane < 2 * site_own, middle,
                    jnp.where(lane < 3 * site_own, logs - high - middle, 0.0),
                ),
            )
            score_ref[pl.ds(dest, 1), :] = lax.dot_general(
                jnp.ones((8, LANES), BF16), packed.astype(BF16), (((1,), (1,)), ((), ())),
                preferred_element_type=F32,
            )[:1]
            times = jnp.sum(jnp.where(lane == dest, mult_ref[...], 0.0), axis=1, keepdims=True)
            factor = scaled * 0.25 / likelihood * times
            adjoint = jnp.concatenate([sums[node_dev:] * factor, sums[:node_dev] * factor], axis=0)

            def against(value):
                return sum(
                    lax.dot_general(
                        piece, rows, (((1,), (1,)), ((), ())), preferred_element_type=F32
                    )
                    for piece in two_parts(value)
                )

            terms = survival * against(adjoint) + spread_out * against(state_sum(adjoint))
            edge = jnp.sum(jnp.where(hit, terms, 0.0), axis=0, keepdims=True)
            for part in range(2):
                piece = edge[:, part * LANES : (part + 1) * LANES]
                term_ref[pl.ds(2 * part * owners + dest, 1), :] = piece
                term_ref[pl.ds((2 * part + 1) * owners + dest, 1), :] = pltpu.roll(
                    piece, LANES // 2, 1
                )
            return carry

        lax.fori_loop(0, owners, body, 0, unroll=2)

    term_ref[pl.ds(slots, LANES), :] = jnp.zeros((LANES, LANES), F32)
    for level in range(levels):
        spread(level)
        gather(level, level == levels - 1)

    score = score_ref[...]
    score_high = score.astype(BF16)
    score_rest = score - score_high.astype(F32)
    score_middle = score_rest.astype(BF16)
    score_low = (score_rest - score_middle.astype(F32)).astype(BF16)
    totals = [jnp.zeros((1, LANES), F32), jnp.zeros((1, LANES), F32)]
    for chunk in range(topo_ref.shape[0]):
        entry = topo_ref[chunk : chunk + 1, :]
        owner_of = entry // node_dev
        local_of = entry - owner_of * node_dev
        row = lax.broadcasted_iota(jnp.int32, (node_dev, LANES), 0)
        owner_hot = (row == owner_of).astype(F32).astype(BF16)
        found = sum(
            lax.dot_general(piece, owner_hot, (((0,), (0,)), ((), ())), preferred_element_type=F32)
            for piece in (score_high, score_middle, score_low)
        )
        totals[chunk % 2] = totals[chunk % 2] + jnp.sum(
            jnp.where(row == local_of, found, 0.0), axis=0, keepdims=True
        )
    for part in range(2):
        term_ref[slots + 2 * part : slots + 2 * part + 1, :] = totals[part]
        term_ref[slots + 2 * part + 1 : slots + 2 * part + 2, :] = pltpu.roll(
            totals[part], LANES // 2, 1
        )
    for block in range(slots // LANES + 1):
        out_ref[:, block * LANES : (block + 1) * LANES] = term_ref[
            block * LANES : (block + 1) * LANES, :
        ].T[:owners]


def on_device(leaf_partials, dag_edges, weights, lengths, counts, topo_nodes):
    node_dev, states, site_dev = leaf_partials.shape
    levels, edge_dev, _ = dag_edges.shape
    owners = lax.axis_size("node")
    device = lax.axis_index("node")
    sites_all = site_dev * lax.axis_size("site")
    site_own = site_dev // owners
    ranks = 4
    slots = ranks * owners
    fields = 4
    topo_dev, use = topo_nodes.shape

    turned = pl.pallas_call(
        spread_kernel,
        grid=(site_dev // LANES,),
        in_specs=[pl.BlockSpec((node_dev, states, LANES), lambda step: (0, 0, step))],
        out_specs=pl.BlockSpec((LANES, states * node_dev), lambda step: (step, 0)),
        out_shape=jax.ShapeDtypeStruct((site_dev, states * node_dev), F32),
    )(leaf_partials)
    leaves = lax.all_to_all(
        turned.reshape(owners, site_own, states * node_dev), "node",
        split_axis=0, concat_axis=0, tiled=True,
    ).reshape(owners * site_own, states * node_dev)

    child = dag_edges[:, :, 0] - device * node_dev
    parents = dag_edges[:, :, 1]
    owner_of = parents // node_dev
    code = dag_edges[:, :, 2] * node_dev + parents - owner_of * node_dev
    earlier = jnp.arange(edge_dev)[:, None] < jnp.arange(edge_dev)[None, :]
    rank = jnp.sum(
        ((owner_of[:, :, None] == owner_of[:, None, :]) & earlier[None]).astype(jnp.int32), axis=1
    )
    slot = rank * owners + owner_of
    chosen = slot[:, None, :] == jnp.arange(slots)[None, :, None]
    values = jnp.stack(
        [
            (child + 1).astype(F32), (code + 1).astype(F32), weights,
            jnp.exp(lengths * (-4.0 / 3.0)),
        ]
    )
    by_slot = jnp.sum(jnp.where(chosen[None], values[:, :, None, :], 0.0), axis=3)
    meta = lax.all_gather(by_slot.reshape(fields * levels * 2, LANES), "node", axis=0, tiled=True)
    topo = lax.all_gather(topo_nodes, "node", axis=0, tiled=True)
    topo = topo.reshape(owners, topo_dev, use).transpose(2, 1, 0).reshape(-1, LANES)
    own_counts = lax.dynamic_slice_in_dim(counts, device * site_own, site_own)
    scaled = jnp.tile(own_counts.astype(F32) / sites_all, LANES // site_own)[None, :]

    partial = pl.pallas_call(
        functools.partial(
            dag_kernel, levels=levels, owners=owners, node_dev=node_dev, site_own=site_own,
            states=states, fields=fields,
        ),
        out_shape=jax.ShapeDtypeStruct((owners, slots + LANES), F32),
        scratch_shapes=[
            pltpu.VMEM((owners * node_dev, LANES), BF16),
            pltpu.VMEM((slots * owners, LANES), F32),
            pltpu.VMEM((levels * (fields - 1) * owners, slots), F32),
            pltpu.VMEM((owners, node_dev), F32),
            pltpu.VMEM((node_dev, LANES), F32),
            pltpu.VMEM((slots + LANES, LANES), F32),
        ],
        compiler_params=pltpu.CompilerParams(vmem_limit_bytes=48 * 1024 * 1024),
    )(leaves, meta, topo, scaled)
    mine = lax.psum_scatter(partial, "node", scatter_dimension=0, tiled=True)
    mine = lax.psum(mine[:, : slots + topo_dev], "site")[0]
    edge_gradient = jnp.sum(
        jnp.where(slot[levels - 1][:, None] == jnp.arange(slots)[None, :], mine[None, :slots], 0.0),
        axis=1,
    )
    return (mine[slots:], edge_gradient)


def solution(mesh):
    return jax.shard_map(
        on_device,
        mesh=mesh,
        in_specs=(
            P("node", None, "site"),
            P(None, "node", None),
            P(None, "node"),
            P(None, "node"),
            P("site"),
            P("node", None),
        ),
        out_specs=(P("node"), P("node")),
        check_vma=False,
    )
```

```python
import functools

import jax
import jax.numpy as jnp
from jax import lax
from jax.experimental import pallas as pl
from jax.experimental.pallas import tpu as pltpu
from jax.sharding import PartitionSpec as P

F32 = jnp.float32
BF16 = jnp.bfloat16
MASK = F32
SPREAD_UNROLL = 8
GATHER_UNROLL = 8
LAST_UNROLL = 4
LEAF_UNROLL = 4
LANES = 128


def pack_kernel(leaf_ref, tail_ref, out_ref, *, site_own, chunk):
    states = leaf_ref.shape[1]
    for pair in range(states // 2):
        rows = jnp.concatenate([leaf_ref[:, 2 * pair, :], leaf_ref[:, 2 * pair + 1, :]], axis=0).T
        for peer in range(LANES // site_own):
            out_ref[peer * chunk + pair * site_own : peer * chunk + (pair + 1) * site_own, :] = (
                rows[peer * site_own : (peer + 1) * site_own]
            )
    for peer in range(LANES // site_own):
        out_ref[peer * chunk + 2 * site_own : (peer + 1) * chunk, :] = tail_ref[...]


def two_parts(value):
    high = value.astype(BF16)
    return high, (value - high.astype(F32)).astype(BF16)


def state_sum(value):
    value = value + pltpu.roll(value, 16, 1)
    return value + pltpu.roll(value, 32, 1)


def dag_kernel(
    input_ref, scaled_ref, out_ref,
    current_ref, slot_ref, table_ref, topo_ref, score_ref, mult_ref, term_ref,
    *, levels, owners, node_dev, site_own, states, fields, chunk, out_rows,
):
    half = 2 * node_dev
    slots = 4 * owners
    meta_rows = fields * levels * 2
    meta_base = 2 * site_own
    left = lax.broadcasted_iota(jnp.int32, (LANES, LANES), 1) < LANES // 2
    left_nodes = left[:node_dev]

    def store_current(start, value, mask):
        high = value.astype(BF16).astype(F32)
        current_ref[pl.ds(start, value.shape[0]), :] = jnp.where(
            mask, high, value - high
        ).astype(BF16)

    for level in range(levels):
        for field in range(1, fields):
            for part in range(2):
                row = (field * levels + level) * 2 + part
                block = input_ref[pl.ds(meta_base + row, owners, stride=chunk), :].T
                table_ref[
                    pl.ds((level * (fields - 1) + field - 1) * owners, owners),
                    part * LANES : (part + 1) * LANES,
                ] = jnp.concatenate([block[:owners], block[owners:]], axis=1)

    block = input_ref[pl.ds(meta_base + meta_rows, owners, stride=chunk), :].T
    entries = topo_ref.shape[0]
    topo_ref[...] = jnp.concatenate(
        [block[:entries], block[entries : 2 * entries]], axis=1
    ).astype(jnp.int32)

    def count_uses(chunk, total):
        entry = topo_ref[pl.ds(chunk, 1), :]
        owner_of = entry // node_dev
        local_of = entry - owner_of * node_dev
        owner_hot = (lax.broadcasted_iota(jnp.int32, (LANES, LANES), 0) == owner_of).astype(F32)
        local_hot = (lax.broadcasted_iota(jnp.int32, (node_dev, LANES), 0) == local_of).astype(F32)
        return total + lax.dot_general(
            local_hot.astype(BF16), owner_hot.astype(BF16), (((1,), (1,)), ((), ())),
            preferred_element_type=F32,
        )

    mult_ref[...] = lax.fori_loop(
        0, topo_ref.shape[0], count_uses, jnp.zeros((node_dev, LANES), F32), unroll=True
    )

    def load_leaves(pair, carry):
        first = pl.multiple_of(pair * 2 * chunk, chunk)
        pieces = []
        for block in range(states // 2):
            a = input_ref[pl.ds(first + block * site_own, site_own), :]
            b = input_ref[pl.ds(first + chunk + block * site_own, site_own), :]
            pieces.append(jnp.where(left[:site_own], a, pltpu.roll(b, LANES // 2, 1)))
            pieces.append(jnp.where(left[:site_own], pltpu.roll(a, LANES // 2, 1), b))
        stacked = jnp.concatenate(pieces + pieces, axis=0)
        store_current(pl.multiple_of(pair * LANES, LANES), stacked.T, left)
        return carry

    lax.fori_loop(0, owners // 2, load_leaves, 0, unroll=LEAF_UNROLL)

    node_row = lax.broadcasted_iota(jnp.int32, (node_dev, LANES), 0).astype(F32) + 1.0
    pair_row = (lax.broadcasted_iota(jnp.int32, (half, slots), 0).astype(F32) + 1.0).astype(MASK)
    blank = jnp.zeros((node_dev, LANES), BF16)
    pair_wide = lax.broadcasted_iota(jnp.int32, (half, slots), 0).astype(F32) + 1.0

    def spread(level):
        def body(pair, carry):
            rows = current_ref[pl.ds(pl.multiple_of(pair * LANES, LANES), LANES), :]
            both = jnp.concatenate(
                [
                    jnp.concatenate([rows[:node_dev], blank], axis=0),
                    jnp.concatenate([blank, rows[node_dev:]], axis=0),
                ],
                axis=1,
            )
            for part in range(2):
                hot = jnp.concatenate(
                    [
                        node_row == input_ref[
                            pl.ds((2 * pair + side) * chunk + meta_base + level * 2 + part, 1), :
                        ]
                        for side in range(2)
                    ],
                    axis=0,
                )
                picked = lax.dot_general(
                    hot.astype(F32).astype(BF16), both, (((0,), (0,)), ((), ())),
                    preferred_element_type=F32,
                )
                for side in range(2):
                    slot_ref[
                        pl.ds(part * half * owners + 2 * pair + side, half, stride=owners), :
                    ] = picked[:, side * LANES : (side + 1) * LANES]
            return carry

        lax.fori_loop(0, owners // 2, body, 0, unroll=SPREAD_UNROLL)

    def gather(level, last):
        def body(dest, carry):
            pieces = [
                slot_ref[pl.ds(pl.multiple_of((rank * owners + dest) * owners, owners), owners), :]
                for rank in range(4)
            ]
            rows = jnp.concatenate(pieces, axis=0).astype(BF16)
            base = level * (fields - 1) * owners + dest
            code = table_ref[pl.ds(base, 1), :]
            weight = table_ref[pl.ds(base + owners, 1), :]
            survival = table_ref[pl.ds(base + 2 * owners, 1), :]
            spread_out = (1.0 - survival) * 0.25
            hit = pair_row == code.astype(MASK)
            scales = []
            for scale in (weight * survival, weight * spread_out):
                high = scale.astype(BF16).astype(F32)
                scales += [high, scale - high]
            chosen = jnp.concatenate(
                [
                    jnp.where(hit, scale.astype(MASK), jnp.zeros((), MASK)).astype(BF16)
                    for scale in scales
                ],
                axis=0,
            )
            product = jnp.dot(chosen, rows, preferred_element_type=F32)
            sums = (
                product[:half] + product[half : 2 * half]
                + state_sum(product[2 * half : 3 * half] + product[3 * half :])
            )
            sums = sums + pltpu.roll(sums, LANES // 2, 1)
            value = sums[:node_dev] * sums[node_dev:]
            if not last:
                store_current(pl.multiple_of(dest * node_dev, node_dev), value, left_nodes)
                return carry
            scaled = scaled_ref[...]
            likelihood = 0.25 * state_sum(value)
            lane = lax.broadcasted_iota(jnp.int32, (node_dev, LANES), 1)
            logs = scaled * jnp.log(likelihood)
            high = logs.astype(BF16).astype(F32)
            middle = (logs - high).astype(BF16).astype(F32)
            packed = jnp.where(
                lane < site_own, high,
                jnp.where(
                    lane < 2 * site_own, middle,
                    jnp.where(lane < 3 * site_own, logs - high - middle, 0.0),
                ),
            )
            score_ref[pl.ds(dest, 1), :] = lax.dot_general(
                jnp.ones((8, LANES), BF16), packed.astype(BF16), (((1,), (1,)), ((), ())),
                preferred_element_type=F32,
            )[:1]
            times = jnp.sum(jnp.where(lane == dest, mult_ref[...], 0.0), axis=1, keepdims=True)
            factor = scaled * 0.25 / likelihood * times
            adjoint = jnp.concatenate([sums[node_dev:] * factor, sums[:node_dev] * factor], axis=0)
            against = lax.dot_general(
                jnp.concatenate(
                    [
                        jnp.concatenate(two_parts(value), axis=1)
                        for value in (adjoint, state_sum(adjoint))
                    ],
                    axis=0,
                ),
                jnp.concatenate([rows, rows], axis=1),
                (((1,), (1,)), ((), ())), preferred_element_type=F32,
            )
            found = hit if MASK == F32 else pair_wide == code
            edge = survival * jnp.sum(
                jnp.where(found, against[:half], 0.0), axis=0, keepdims=True
            ) + spread_out * jnp.sum(jnp.where(found, against[half:], 0.0), axis=0, keepdims=True)
            for part in range(2):
                piece = edge[:, part * LANES : (part + 1) * LANES]
                term_ref[pl.ds(2 * part * owners + dest, 1), :] = piece
                term_ref[pl.ds((2 * part + 1) * owners + dest, 1), :] = pltpu.roll(
                    piece, LANES // 2, 1
                )
            return carry

        lax.fori_loop(0, owners, body, 0, unroll=LAST_UNROLL if last else GATHER_UNROLL)

    term_ref[pl.ds(slots, LANES), :] = jnp.zeros((LANES, LANES), F32)
    for level in range(levels):
        spread(level)
        gather(level, level == levels - 1)

    score = score_ref[...]
    score_high = score.astype(BF16)
    score_rest = score - score_high.astype(F32)
    score_middle = score_rest.astype(BF16)
    score_low = (score_rest - score_middle.astype(F32)).astype(BF16)
    totals = [jnp.zeros((1, LANES), F32), jnp.zeros((1, LANES), F32)]
    for chunk in range(topo_ref.shape[0]):
        entry = topo_ref[chunk : chunk + 1, :]
        owner_of = entry // node_dev
        local_of = entry - owner_of * node_dev
        row = lax.broadcasted_iota(jnp.int32, (node_dev, LANES), 0)
        owner_hot = (row == owner_of).astype(F32).astype(BF16)
        found = sum(
            lax.dot_general(piece, owner_hot, (((0,), (0,)), ((), ())), preferred_element_type=F32)
            for piece in (score_high, score_middle, score_low)
        )
        totals[chunk % 2] = totals[chunk % 2] + jnp.sum(
            jnp.where(row == local_of, found, 0.0), axis=0, keepdims=True
        )
    for part in range(2):
        term_ref[slots + 2 * part : slots + 2 * part + 1, :] = totals[part]
        term_ref[slots + 2 * part + 1 : slots + 2 * part + 2, :] = pltpu.roll(
            totals[part], LANES // 2, 1
        )
    for block in range(slots // LANES + 1):
        out_ref[pl.ds(block, owners, stride=out_rows), :] = term_ref[
            block * LANES : (block + 1) * LANES, :
        ].T[:owners]


def on_device(leaf_partials, dag_edges, weights, lengths, counts, topo_nodes):
    node_dev, states, site_dev = leaf_partials.shape
    levels, edge_dev, _ = dag_edges.shape
    owners = lax.axis_size("node")
    device = lax.axis_index("node")
    sites_all = site_dev * lax.axis_size("site")
    site_own = site_dev // owners
    ranks = 4
    slots = ranks * owners
    fields = 4
    topo_dev, use = topo_nodes.shape

    child = dag_edges[:, :, 0] - device * node_dev
    parents = dag_edges[:, :, 1]
    owner_of = parents // node_dev
    code = dag_edges[:, :, 2] * node_dev + parents - owner_of * node_dev
    earlier = jnp.arange(edge_dev)[:, None] < jnp.arange(edge_dev)[None, :]
    rank = jnp.sum(
        ((owner_of[:, :, None] == owner_of[:, None, :]) & earlier[None]).astype(jnp.int32), axis=1
    )
    slot = rank * owners + owner_of
    chosen = slot[:, None, :] == jnp.arange(slots)[None, :, None]
    values = jnp.stack(
        [
            (child + 1).astype(F32), (code + 1).astype(F32), weights,
            jnp.exp(lengths * (-4.0 / 3.0)),
        ]
    )
    by_slot = jnp.sum(jnp.where(chosen[None], values[:, :, None, :], 0.0), axis=3)
    halves = topo_dev // 2
    topo = topo_nodes.reshape(halves, 2, use).transpose(1, 2, 0).reshape(1, -1).astype(F32)
    meta = by_slot.reshape(fields * levels * 2, LANES)
    tail = -(-(meta.shape[0] + 1) // 8) * 8
    tail = jnp.concatenate(
        [meta, jnp.pad(topo, ((0, tail - meta.shape[0] - 1), (0, LANES - topo.shape[1])))], axis=0
    )
    chunk = 2 * site_own + tail.shape[0]
    peers = LANES // site_own
    packed = pl.pallas_call(
        functools.partial(pack_kernel, site_own=site_own, chunk=chunk),
        grid=(site_dev // LANES,),
        in_specs=[
            pl.BlockSpec((node_dev, states, LANES), lambda step: (0, 0, step)),
            pl.BlockSpec(tail.shape, lambda step: (0, 0)),
        ],
        out_specs=pl.BlockSpec((peers * chunk, LANES), lambda step: (step, 0)),
        out_shape=jax.ShapeDtypeStruct((owners * chunk, LANES), F32),
    )(leaf_partials, tail)
    received = lax.all_to_all(
        packed.reshape(owners, chunk, LANES), "node", split_axis=0, concat_axis=0, tiled=True
    ).reshape(owners * chunk, LANES)
    own_counts = lax.dynamic_slice_in_dim(counts, device * site_own, site_own)
    scaled = jnp.tile(own_counts.astype(F32) / sites_all, LANES // site_own)[None, :]

    out_rows = 8
    partial = pl.pallas_call(
        functools.partial(
            dag_kernel, levels=levels, owners=owners, node_dev=node_dev, site_own=site_own,
            states=states, fields=fields, chunk=chunk, out_rows=out_rows,
        ),
        out_shape=jax.ShapeDtypeStruct((owners * out_rows, LANES), F32),
        scratch_shapes=[
            pltpu.VMEM((owners * node_dev, LANES), BF16),
            pltpu.VMEM((slots * owners, LANES), F32),
            pltpu.VMEM((levels * (fields - 1) * owners, slots), F32),
            pltpu.VMEM((use * halves, LANES), jnp.int32),
            pltpu.VMEM((owners, node_dev), F32),
            pltpu.VMEM((node_dev, LANES), F32),
            pltpu.VMEM((slots + LANES, LANES), F32),
        ],
        compiler_params=pltpu.CompilerParams(vmem_limit_bytes=48 * 1024 * 1024),
    )(received, scaled)
    shares = lax.all_to_all(
        partial.reshape(owners, out_rows, LANES), "node", split_axis=0, concat_axis=0, tiled=True
    )
    mine = lax.psum(jnp.sum(shares[:, : slots // LANES + 1], axis=0), "site").reshape(-1)
    edge_gradient = jnp.sum(
        jnp.where(slot[levels - 1][:, None] == jnp.arange(slots)[None, :], mine[None, :slots], 0.0),
        axis=1,
    )
    return (mine[slots : slots + topo_dev], edge_gradient)


def solution(mesh):
    return jax.shard_map(
        on_device,
        mesh=mesh,
        in_specs=(
            P("node", None, "site"),
            P(None, "node", None),
            P(None, "node"),
            P(None, "node"),
            P("site"),
            P("node", None),
        ),
        out_specs=(P("node"), P("node")),
        check_vma=False,
    )
```

```python
import functools

import jax
import jax.numpy as jnp
from jax import lax
from jax.experimental import pallas as pl
from jax.experimental.pallas import tpu as pltpu
from jax.sharding import PartitionSpec as P

F32 = jnp.float32
BF16 = jnp.bfloat16
MASK = F32
SPREAD_UNROLL = 8
GATHER_UNROLL = 8
FINISH_UNROLL = 8
EDGE_UNROLL = 8
LEAF_UNROLL = 4
LANES = 128


def pack_kernel(leaf_ref, tail_ref, out_ref, *, site_own, chunk):
    states = leaf_ref.shape[1]
    for pair in range(states // 2):
        rows = jnp.concatenate([leaf_ref[:, 2 * pair, :], leaf_ref[:, 2 * pair + 1, :]], axis=0).T
        for peer in range(LANES // site_own):
            out_ref[peer * chunk + pair * site_own : peer * chunk + (pair + 1) * site_own, :] = (
                rows[peer * site_own : (peer + 1) * site_own]
            )
    for peer in range(LANES // site_own):
        out_ref[peer * chunk + 2 * site_own : (peer + 1) * chunk, :] = tail_ref[...]


def two_parts(value):
    high = value.astype(BF16)
    return high, (value - high.astype(F32)).astype(BF16)


def both_parts(value):
    return jnp.concatenate(two_parts(value), axis=1)


def dag_kernel(
    input_ref, scaled_ref, out_ref,
    current_ref, slot_ref, table_ref, topo_ref, score_ref, term_ref, sums_ref, adjoint_ref,
    *, levels, owners, node_dev, site_own, states, fields, chunk, out_rows,
):
    half = 2 * node_dev
    slots = 4 * owners
    meta_rows = fields * levels * 2
    meta_base = 2 * site_own
    left = lax.broadcasted_iota(jnp.int32, (LANES, LANES), 1) < LANES // 2
    left_nodes = left[:node_dev]

    def store_current(start, value, mask):
        high = value.astype(BF16).astype(F32)
        current_ref[pl.ds(start, value.shape[0]), :] = jnp.where(
            mask, high, value - high
        ).astype(BF16)

    apart = jnp.abs(
        lax.broadcasted_iota(jnp.int32, (LANES, LANES), 0)
        - lax.broadcasted_iota(jnp.int32, (LANES, LANES), 1)
    )
    fold = (apart % (site_own * states) == 0).astype(F32).astype(BF16)
    over_states = (apart % site_own == 0).astype(F32).astype(BF16)
    over_states_twice = jnp.concatenate([over_states, over_states], axis=0)
    settle = jnp.concatenate([fold, fold, over_states_twice], axis=0)

    for level in range(levels):
        for field in range(1, fields):
            for part in range(2):
                row = (field * levels + level) * 2 + part
                block = input_ref[pl.ds(meta_base + row, owners, stride=chunk), :].T
                table_ref[
                    pl.ds((level * (fields - 1) + field - 1) * owners, owners),
                    part * LANES : (part + 1) * LANES,
                ] = jnp.concatenate([block[:owners], block[owners:]], axis=1)

    block = input_ref[pl.ds(meta_base + meta_rows, owners, stride=chunk), :].T
    entries = topo_ref.shape[0]
    topo_ref[...] = jnp.concatenate(
        [block[:entries], block[entries : 2 * entries]], axis=1
    ).astype(jnp.int32)

    def load_leaves(pair, carry):
        first = pl.multiple_of(pair * 2 * chunk, chunk)
        pieces = []
        for block in range(states // 2):
            a = input_ref[pl.ds(first + block * site_own, site_own), :]
            b = input_ref[pl.ds(first + chunk + block * site_own, site_own), :]
            pieces.append(jnp.where(left[:site_own], a, pltpu.roll(b, LANES // 2, 1)))
            pieces.append(jnp.where(left[:site_own], pltpu.roll(a, LANES // 2, 1), b))
        stacked = jnp.concatenate(pieces + pieces, axis=0)
        store_current(pl.multiple_of(pair * LANES, LANES), stacked.T, left)
        return carry

    lax.fori_loop(0, owners // 2, load_leaves, 0, unroll=LEAF_UNROLL)

    node_row = lax.broadcasted_iota(jnp.int32, (node_dev, LANES), 0).astype(F32) + 1.0
    pair_row = (lax.broadcasted_iota(jnp.int32, (half, slots), 0).astype(F32) + 1.0).astype(MASK)
    blank = jnp.zeros((node_dev, LANES), BF16)
    pair_wide = lax.broadcasted_iota(jnp.int32, (half, slots), 0).astype(F32) + 1.0

    def spread(level):
        def body(pair, carry):
            rows = current_ref[pl.ds(pl.multiple_of(pair * LANES, LANES), LANES), :]
            both = jnp.concatenate(
                [
                    jnp.concatenate([rows[:node_dev], blank], axis=0),
                    jnp.concatenate([blank, rows[node_dev:]], axis=0),
                ],
                axis=1,
            )
            for part in range(2):
                hot = jnp.concatenate(
                    [
                        node_row == input_ref[
                            pl.ds((2 * pair + side) * chunk + meta_base + level * 2 + part, 1), :
                        ]
                        for side in range(2)
                    ],
                    axis=0,
                )
                picked = lax.dot_general(
                    hot.astype(F32).astype(BF16), both, (((0,), (0,)), ((), ())),
                    preferred_element_type=F32,
                )
                for side in range(2):
                    slot_ref[
                        pl.ds(part * half * owners + 2 * pair + side, half, stride=owners), :
                    ] = picked[:, side * LANES : (side + 1) * LANES]
            return carry

        lax.fori_loop(0, owners // 2, body, 0, unroll=SPREAD_UNROLL)

    def slot_rows(dest):
        pieces = [
            slot_ref[pl.ds(pl.multiple_of((rank * owners + dest) * owners, owners), owners), :]
            for rank in range(4)
        ]
        return jnp.concatenate(pieces, axis=0).astype(BF16)

    def gather(level):
        def body(dest, carry):
            base = level * (fields - 1) * owners + dest
            code = table_ref[pl.ds(base, 1), :]
            weight = table_ref[pl.ds(base + owners, 1), :]
            survival = table_ref[pl.ds(base + 2 * owners, 1), :]
            hit = pair_row == code.astype(MASK)
            scales = []
            for scale in (weight * survival, weight * ((1.0 - survival) * 0.25)):
                high = scale.astype(BF16).astype(F32)
                scales += [high, scale - high]
            chosen = jnp.concatenate(
                [
                    jnp.where(hit, scale.astype(MASK), jnp.zeros((), MASK)).astype(BF16)
                    for scale in scales
                ],
                axis=0,
            )
            product = jnp.dot(chosen, slot_rows(dest), preferred_element_type=F32)
            start = pl.multiple_of(dest * half, half)
            sums_ref[pl.ds(start, half), : 2 * LANES] = both_parts(
                product[:half] + product[half : 2 * half]
            )
            sums_ref[pl.ds(start, half), 2 * LANES :] = both_parts(
                product[2 * half : 3 * half] + product[3 * half :]
            )
            return carry

        lax.fori_loop(0, owners, body, 0, unroll=GATHER_UNROLL)

    def pair_sums(dest):
        start = pl.multiple_of(dest * half, half)
        return jnp.dot(sums_ref[pl.ds(start, half), :], settle, preferred_element_type=F32)

    def finish():
        def body(dest, carry):
            sums = pair_sums(dest)
            store_current(
                pl.multiple_of(dest * node_dev, node_dev), sums[:node_dev] * sums[node_dev:],
                left_nodes,
            )
            return carry

        lax.fori_loop(0, owners, body, 0, unroll=FINISH_UNROLL)

    def finish_last():
        lane = lax.broadcasted_iota(jnp.int32, (node_dev, LANES), 1)

        def body(dest, carry):
            sums = pair_sums(dest)
            scaled = scaled_ref[...]
            likelihood = 0.125 * jnp.dot(
                both_parts(sums[:node_dev] * sums[node_dev:]), over_states_twice,
                preferred_element_type=F32,
            )
            logs = scaled * jnp.log(likelihood)
            high = logs.astype(BF16).astype(F32)
            middle = (logs - high).astype(BF16).astype(F32)
            packed = jnp.where(
                lane < site_own, high,
                jnp.where(
                    lane < 2 * site_own, middle,
                    jnp.where(lane < 3 * site_own, logs - high - middle, 0.0),
                ),
            )
            score_ref[pl.ds(dest, 1), :] = lax.dot_general(
                jnp.ones((8, LANES), BF16), packed.astype(BF16), (((1,), (1,)), ((), ())),
                preferred_element_type=F32,
            )[:1]
            factor = scaled * 0.25 / likelihood
            adjoint = jnp.concatenate([sums[node_dev:] * factor, sums[:node_dev] * factor], axis=0)
            start = pl.multiple_of(dest * 2 * half, 2 * half)
            parts = both_parts(adjoint)
            adjoint_ref[pl.ds(start, half), :] = parts
            adjoint_ref[pl.ds(start + half, half), :] = both_parts(
                0.5 * jnp.dot(parts, over_states_twice, preferred_element_type=F32)
            )
            return carry

        lax.fori_loop(0, owners, body, 0, unroll=FINISH_UNROLL)

    def edges(level):
        def body(dest, carry):
            base = level * (fields - 1) * owners + dest
            code = table_ref[pl.ds(base, 1), :]
            survival = table_ref[pl.ds(base + 2 * owners, 1), :]
            rows = slot_rows(dest)
            against = lax.dot_general(
                adjoint_ref[pl.ds(pl.multiple_of(dest * 2 * half, 2 * half), 2 * half), :],
                jnp.concatenate([rows, rows], axis=1),
                (((1,), (1,)), ((), ())), preferred_element_type=F32,
            )
            found = pair_wide == code
            edge = survival * jnp.sum(
                jnp.where(found, against[:half], 0.0), axis=0, keepdims=True
            ) + ((1.0 - survival) * 0.25) * jnp.sum(
                jnp.where(found, against[half:], 0.0), axis=0, keepdims=True
            )
            for part in range(2):
                term_ref[pl.ds(part * owners + dest, 1), :] = edge[
                    :, part * LANES : (part + 1) * LANES
                ]
            return carry

        lax.fori_loop(0, owners, body, 0, unroll=EDGE_UNROLL)

    for level in range(levels):
        spread(level)
        gather(level)
        if level < levels - 1:
            finish()
    finish_last()
    edges(levels - 1)

    score = score_ref[...]
    score_high = score.astype(BF16)
    score_rest = score - score_high.astype(F32)
    score_middle = score_rest.astype(BF16)
    score_low = (score_rest - score_middle.astype(F32)).astype(BF16)
    totals = [jnp.zeros((1, LANES), F32), jnp.zeros((1, LANES), F32)]
    for chunk in range(topo_ref.shape[0]):
        entry = topo_ref[chunk : chunk + 1, :]
        owner_of = entry // node_dev
        local_of = entry - owner_of * node_dev
        row = lax.broadcasted_iota(jnp.int32, (node_dev, LANES), 0)
        owner_hot = (row == owner_of).astype(F32).astype(BF16)
        found = sum(
            lax.dot_general(piece, owner_hot, (((0,), (0,)), ((), ())), preferred_element_type=F32)
            for piece in (score_high, score_middle, score_low)
        )
        totals[chunk % 2] = totals[chunk % 2] + jnp.sum(
            jnp.where(row == local_of, found, 0.0), axis=0, keepdims=True
        )
    def place(row, block):
        turned = block.T
        out_ref[pl.ds(row, owners, stride=out_rows), : 2 * block.shape[0]] = jnp.concatenate(
            [turned[:owners], turned[owners:]], axis=1
        )

    for part in range(2):
        place(part, term_ref[part * owners : (part + 1) * owners, :])
    place(2, jnp.concatenate(totals + [jnp.zeros((6, LANES), F32)], axis=0))


def on_device(leaf_partials, dag_edges, weights, lengths, counts, topo_nodes):
    node_dev, states, site_dev = leaf_partials.shape
    levels, edge_dev, _ = dag_edges.shape
    owners = lax.axis_size("node")
    device = lax.axis_index("node")
    sites_all = site_dev * lax.axis_size("site")
    site_own = site_dev // owners
    ranks = 4
    slots = ranks * owners
    fields = 4
    topo_dev, use = topo_nodes.shape

    child = dag_edges[:, :, 0] - device * node_dev
    parents = dag_edges[:, :, 1]
    owner_of = parents // node_dev
    code = dag_edges[:, :, 2] * node_dev + parents - owner_of * node_dev
    earlier = jnp.arange(edge_dev)[:, None] < jnp.arange(edge_dev)[None, :]
    rank = jnp.sum(
        ((owner_of[:, :, None] == owner_of[:, None, :]) & earlier[None]).astype(jnp.int32), axis=1
    )
    slot = rank * owners + owner_of
    chosen = slot[:, None, :] == jnp.arange(slots)[None, :, None]
    values = jnp.stack(
        [
            (child + 1).astype(F32), (code + 1).astype(F32), weights,
            jnp.exp(lengths * (-4.0 / 3.0)),
        ]
    )
    by_slot = jnp.sum(jnp.where(chosen[None], values[:, :, None, :], 0.0), axis=3)
    halves = topo_dev // 2
    topo = topo_nodes.reshape(halves, 2, use).transpose(1, 2, 0).reshape(1, -1).astype(F32)
    meta = by_slot.reshape(fields * levels * 2, LANES)
    tail = -(-(meta.shape[0] + 1) // 8) * 8
    tail = jnp.concatenate(
        [meta, jnp.pad(topo, ((0, tail - meta.shape[0] - 1), (0, LANES - topo.shape[1])))], axis=0
    )
    chunk = 2 * site_own + tail.shape[0]
    peers = LANES // site_own
    packed = pl.pallas_call(
        functools.partial(pack_kernel, site_own=site_own, chunk=chunk),
        grid=(site_dev // LANES,),
        in_specs=[
            pl.BlockSpec((node_dev, states, LANES), lambda step: (0, 0, step)),
            pl.BlockSpec(tail.shape, lambda step: (0, 0)),
        ],
        out_specs=pl.BlockSpec((peers * chunk, LANES), lambda step: (step, 0)),
        out_shape=jax.ShapeDtypeStruct((owners * chunk, LANES), F32),
    )(leaf_partials, tail)
    received = lax.all_to_all(
        packed.reshape(owners, chunk, LANES), "node", split_axis=0, concat_axis=0, tiled=True
    ).reshape(owners * chunk, LANES)
    own_counts = lax.dynamic_slice_in_dim(counts, device * site_own, site_own)
    scaled = jnp.tile(own_counts.astype(F32) / sites_all, LANES // site_own)[None, :]

    out_rows = 8
    partial = pl.pallas_call(
        functools.partial(
            dag_kernel, levels=levels, owners=owners, node_dev=node_dev, site_own=site_own,
            states=states, fields=fields, chunk=chunk, out_rows=out_rows,
        ),
        out_shape=jax.ShapeDtypeStruct((owners * out_rows, LANES), F32),
        scratch_shapes=[
            pltpu.VMEM((owners * node_dev, LANES), BF16),
            pltpu.VMEM((slots * owners, LANES), F32),
            pltpu.VMEM((levels * (fields - 1) * owners, slots), F32),
            pltpu.VMEM((use * halves, LANES), jnp.int32),
            pltpu.VMEM((owners, node_dev), F32),
            pltpu.VMEM((2 * owners, LANES), F32),
            pltpu.VMEM((2 * owners * node_dev, 4 * LANES), BF16),
            pltpu.VMEM((4 * owners * node_dev, 2 * LANES), BF16),
        ],
        compiler_params=pltpu.CompilerParams(vmem_limit_bytes=56 * 1024 * 1024),
    )(received, scaled)
    shares = lax.all_to_all(
        partial.reshape(owners, out_rows, LANES), "node", split_axis=0, concat_axis=0, tiled=True
    )
    mine = lax.psum(jnp.sum(shares[:, : slots // LANES + 1], axis=0), "site").reshape(-1)
    uses = received.reshape(owners, chunk, LANES)[:, 2 * site_own + meta.shape[0], : topo_dev * use]
    multiplicity = jnp.sum(
        (uses.reshape(-1)[None, :] == parents[levels - 1].astype(F32)[:, None]).astype(F32), axis=1
    )
    edge_gradient = multiplicity * jnp.sum(
        jnp.where(slot[levels - 1][:, None] == jnp.arange(slots)[None, :], mine[None, :slots], 0.0),
        axis=1,
    )
    topology = mine[slots : slots + 16].reshape(2, 8)[:, :halves].T.reshape(-1)
    return (topology, edge_gradient)


def solution(mesh):
    return jax.shard_map(
        on_device,
        mesh=mesh,
        in_specs=(
            P("node", None, "site"),
            P(None, "node", None),
            P(None, "node"),
            P(None, "node"),
            P("site"),
            P("node", None),
        ),
        out_specs=(P("node"), P("node")),
        check_vma=False,
    )
```

```python
import functools

import jax
import jax.numpy as jnp
from jax import lax
from jax.experimental import pallas as pl
from jax.experimental.pallas import tpu as pltpu
from jax.sharding import PartitionSpec as P

F32 = jnp.float32
BF16 = jnp.bfloat16
MASK = F32
SPREAD_UNROLL = 8
GATHER_UNROLL = 8
FINISH_UNROLL = 2
LAST_UNROLL = 2
EDGE_UNROLL = 8
LEAF_UNROLL = 4
LANES = 128
GROUP = 4


def pack_kernel(leaf_ref, tail_ref, out_ref, *, site_own, chunk):
    states = leaf_ref.shape[1]
    for pair in range(states // 2):
        rows = jnp.concatenate([leaf_ref[:, 2 * pair, :], leaf_ref[:, 2 * pair + 1, :]], axis=0).T
        for peer in range(LANES // site_own):
            out_ref[peer * chunk + pair * site_own : peer * chunk + (pair + 1) * site_own, :] = (
                rows[peer * site_own : (peer + 1) * site_own]
            )
    for peer in range(LANES // site_own):
        out_ref[peer * chunk + 2 * site_own : (peer + 1) * chunk, :] = tail_ref[...]


def two_parts(value):
    high = value.astype(BF16)
    return high, (value - high.astype(F32)).astype(BF16)


def both_parts(value):
    return jnp.concatenate(two_parts(value), axis=1)


def dag_kernel(
    input_ref, scaled_ref, out_ref,
    current_ref, slot_ref, table_ref, topo_ref, score_ref, term_ref, sums_ref, adjoint_ref,
    *, levels, owners, node_dev, site_own, states, fields, chunk, out_rows,
):
    half = 2 * node_dev
    slots = 4 * owners
    meta_rows = fields * levels * 2
    meta_base = 2 * site_own
    pitch = slot_ref.shape[0] // slots
    left = lax.broadcasted_iota(jnp.int32, (LANES, LANES), 1) < LANES // 2
    left_nodes = left[:node_dev]

    def store_current(start, value, mask):
        high = value.astype(BF16).astype(F32)
        current_ref[pl.ds(start, value.shape[0]), :] = jnp.where(
            mask, high, value - high
        ).astype(BF16)

    apart = jnp.abs(
        lax.broadcasted_iota(jnp.int32, (LANES, LANES), 0)
        - lax.broadcasted_iota(jnp.int32, (LANES, LANES), 1)
    )
    fold = (apart % (site_own * states) == 0).astype(F32).astype(BF16)
    over_states = (apart % site_own == 0).astype(F32).astype(BF16)
    over_states_twice = jnp.concatenate([over_states, over_states], axis=0)
    settle = jnp.concatenate([fold, fold, over_states_twice], axis=0)

    for level in range(levels):
        for field in range(1, fields):
            for part in range(2):
                row = (field * levels + level) * 2 + part
                block = input_ref[pl.ds(meta_base + row, owners, stride=chunk), :].T
                table_ref[
                    pl.ds((level * (fields - 1) + field - 1) * owners, owners),
                    part * LANES : (part + 1) * LANES,
                ] = jnp.concatenate([block[:owners], block[owners:]], axis=1)

    block = input_ref[pl.ds(meta_base + meta_rows, owners, stride=chunk), :].T
    entries = topo_ref.shape[0]
    topo_ref[...] = jnp.concatenate(
        [block[:entries], block[entries : 2 * entries]], axis=1
    ).astype(jnp.int32)

    def load_leaves(pair, carry):
        first = pl.multiple_of(pair * 2 * chunk, chunk)
        pieces = []
        for block in range(states // 2):
            a = input_ref[pl.ds(first + block * site_own, site_own), :]
            b = input_ref[pl.ds(first + chunk + block * site_own, site_own), :]
            pieces.append(jnp.where(left[:site_own], a, pltpu.roll(b, LANES // 2, 1)))
            pieces.append(jnp.where(left[:site_own], pltpu.roll(a, LANES // 2, 1), b))
        stacked = jnp.concatenate(pieces + pieces, axis=0)
        store_current(pl.multiple_of(pair * LANES, LANES), stacked.T, left)
        return carry

    lax.fori_loop(0, owners // 2, load_leaves, 0, unroll=LEAF_UNROLL)

    node_row = lax.broadcasted_iota(jnp.int32, (node_dev, LANES), 0).astype(F32) + 1.0
    pair_row = (lax.broadcasted_iota(jnp.int32, (half, slots), 0).astype(F32) + 1.0).astype(MASK)
    blank = jnp.zeros((node_dev, LANES), BF16)
    pair_wide = lax.broadcasted_iota(jnp.int32, (half, slots), 0).astype(F32) + 1.0

    def spread(level):
        def body(pair, carry):
            rows = current_ref[pl.ds(pl.multiple_of(pair * LANES, LANES), LANES), :]
            both = jnp.concatenate(
                [
                    jnp.concatenate([rows[:node_dev], blank], axis=0),
                    jnp.concatenate([blank, rows[node_dev:]], axis=0),
                ],
                axis=1,
            )
            for part in range(2):
                hot = jnp.concatenate(
                    [
                        node_row == input_ref[
                            pl.ds((2 * pair + side) * chunk + meta_base + level * 2 + part, 1), :
                        ]
                        for side in range(2)
                    ],
                    axis=0,
                )
                picked = lax.dot_general(
                    hot.astype(F32).astype(BF16), both, (((0,), (0,)), ((), ())),
                    preferred_element_type=F32,
                )
                for side in range(2):
                    slot_ref[
                        pl.ds(part * half * pitch + 2 * pair + side, half, stride=pitch), :
                    ] = picked[:, side * LANES : (side + 1) * LANES]
            return carry

        lax.fori_loop(0, owners // 2, body, 0, unroll=SPREAD_UNROLL)

    def slot_rows(dest):
        pieces = [
            slot_ref[pl.ds((rank * owners + dest) * pitch, owners), :]
            for rank in range(4)
        ]
        return jnp.concatenate(pieces, axis=0).astype(BF16)

    def gather(level):
        def body(dest, carry):
            base = level * (fields - 1) * owners + dest
            code = table_ref[pl.ds(base, 1), :]
            weight = table_ref[pl.ds(base + owners, 1), :]
            survival = table_ref[pl.ds(base + 2 * owners, 1), :]
            hit = pair_row == code.astype(MASK)
            scales = []
            for scale in (weight * survival, weight * ((1.0 - survival) * 0.25)):
                high = scale.astype(BF16).astype(F32)
                scales += [high, scale - high]
            chosen = jnp.concatenate(
                [
                    jnp.where(hit, scale.astype(MASK), jnp.zeros((), MASK)).astype(BF16)
                    for scale in scales
                ],
                axis=0,
            )
            product = jnp.dot(chosen, slot_rows(dest), preferred_element_type=F32)
            start = pl.multiple_of(dest * half, half)
            sums_ref[pl.ds(start, half), : 2 * LANES] = both_parts(
                product[:half] + product[half : 2 * half]
            )
            sums_ref[pl.ds(start, half), 2 * LANES :] = both_parts(
                product[2 * half : 3 * half] + product[3 * half :]
            )
            return carry

        lax.fori_loop(0, owners, body, 0, unroll=GATHER_UNROLL)

    def pair_sums(group):
        rows = GROUP * half
        start = pl.multiple_of(group * rows, rows)
        sums = jnp.dot(sums_ref[pl.ds(start, rows), :], settle, preferred_element_type=F32)
        first = [sums[item * half : item * half + node_dev] for item in range(GROUP)]
        second = [sums[item * half + node_dev : (item + 1) * half] for item in range(GROUP)]
        return jnp.concatenate(first, axis=0), jnp.concatenate(second, axis=0)

    group_nodes = GROUP * node_dev

    def finish():
        mask = lax.broadcasted_iota(jnp.int32, (group_nodes, LANES), 1) < LANES // 2

        def body(group, carry):
            first, second = pair_sums(group)
            store_current(pl.multiple_of(group * group_nodes, group_nodes), first * second, mask)
            return carry

        lax.fori_loop(0, owners // GROUP, body, 0, unroll=FINISH_UNROLL)

    def finish_last():
        lane = lax.broadcasted_iota(jnp.int32, (group_nodes, LANES), 1)

        def body(group, carry):
            first, second = pair_sums(group)
            scaled = scaled_ref[...]
            likelihood = 0.125 * jnp.dot(
                both_parts(first * second), over_states_twice, preferred_element_type=F32
            )
            logs = scaled * jnp.log(likelihood)
            high = logs.astype(BF16).astype(F32)
            middle = (logs - high).astype(BF16).astype(F32)
            packed = jnp.where(
                lane < site_own, high,
                jnp.where(
                    lane < 2 * site_own, middle,
                    jnp.where(lane < 3 * site_own, logs - high - middle, 0.0),
                ),
            )
            score_ref[pl.ds(group, 1), :] = lax.dot_general(
                jnp.ones((8, LANES), BF16), packed.astype(BF16), (((1,), (1,)), ((), ())),
                preferred_element_type=F32,
            )[:1]
            factor = scaled * 0.25 / likelihood
            first, second = second * factor, first * factor
            adjoint = jnp.concatenate(
                [
                    value[item * node_dev : (item + 1) * node_dev]
                    for item in range(GROUP)
                    for value in (first, second)
                ],
                axis=0,
            )
            parts = both_parts(adjoint)
            summed = both_parts(
                0.5 * jnp.dot(parts, over_states_twice, preferred_element_type=F32)
            )
            for item in range(GROUP):
                start = pl.multiple_of((group * GROUP + item) * 2 * half, 2 * half)
                adjoint_ref[pl.ds(start, half), :] = parts[item * half : (item + 1) * half]
                adjoint_ref[pl.ds(start + half, half), :] = summed[item * half : (item + 1) * half]
            return carry

        lax.fori_loop(0, owners // GROUP, body, 0, unroll=LAST_UNROLL)

    def edges(level):
        def body(dest, carry):
            base = level * (fields - 1) * owners + dest
            code = table_ref[pl.ds(base, 1), :]
            survival = table_ref[pl.ds(base + 2 * owners, 1), :]
            rows = slot_rows(dest)
            against = lax.dot_general(
                adjoint_ref[pl.ds(pl.multiple_of(dest * 2 * half, 2 * half), 2 * half), :],
                jnp.concatenate([rows, rows], axis=1),
                (((1,), (1,)), ((), ())), preferred_element_type=F32,
            )
            found = pair_wide == code
            edge = survival * jnp.sum(
                jnp.where(found, against[:half], 0.0), axis=0, keepdims=True
            ) + ((1.0 - survival) * 0.25) * jnp.sum(
                jnp.where(found, against[half:], 0.0), axis=0, keepdims=True
            )
            for part in range(2):
                term_ref[pl.ds(part * owners + dest, 1), :] = edge[
                    :, part * LANES : (part + 1) * LANES
                ]
            return carry

        lax.fori_loop(0, owners, body, 0, unroll=EDGE_UNROLL)

    for level in range(levels):
        spread(level)
        gather(level)
        if level < levels - 1:
            finish()
    finish_last()
    edges(levels - 1)

    score = score_ref[...]
    score_high = score.astype(BF16)
    score_rest = score - score_high.astype(F32)
    score_middle = score_rest.astype(BF16)
    score_low = (score_rest - score_middle.astype(F32)).astype(BF16)
    totals = [jnp.zeros((1, LANES), F32), jnp.zeros((1, LANES), F32)]
    for chunk in range(topo_ref.shape[0]):
        entry = topo_ref[chunk : chunk + 1, :]
        group_of = entry // group_nodes
        local_of = entry - group_of * group_nodes
        group_row = lax.broadcasted_iota(jnp.int32, (owners // GROUP, LANES), 0)
        group_hot = (group_row == group_of).astype(F32).astype(BF16)
        found = sum(
            lax.dot_general(piece, group_hot, (((0,), (0,)), ((), ())), preferred_element_type=F32)
            for piece in (score_high, score_middle, score_low)
        )
        row = lax.broadcasted_iota(jnp.int32, (group_nodes, LANES), 0)
        totals[chunk % 2] = totals[chunk % 2] + jnp.sum(
            jnp.where(row == local_of, found, 0.0), axis=0, keepdims=True
        )
    def place(row, block):
        turned = block.T
        out_ref[pl.ds(row, owners, stride=out_rows), : 2 * block.shape[0]] = jnp.concatenate(
            [turned[:owners], turned[owners:]], axis=1
        )

    for part in range(2):
        place(part, term_ref[part * owners : (part + 1) * owners, :])
    place(2, jnp.concatenate(totals + [jnp.zeros((6, LANES), F32)], axis=0))


def on_device(leaf_partials, dag_edges, weights, lengths, counts, topo_nodes):
    node_dev, states, site_dev = leaf_partials.shape
    levels, edge_dev, _ = dag_edges.shape
    owners = lax.axis_size("node")
    device = lax.axis_index("node")
    sites_all = site_dev * lax.axis_size("site")
    site_own = site_dev // owners
    ranks = 4
    slots = ranks * owners
    fields = 4
    topo_dev, use = topo_nodes.shape

    child = dag_edges[:, :, 0] - device * node_dev
    parents = dag_edges[:, :, 1]
    owner_of = parents // node_dev
    code = dag_edges[:, :, 2] * node_dev + parents - owner_of * node_dev
    earlier = jnp.arange(edge_dev)[:, None] < jnp.arange(edge_dev)[None, :]
    rank = jnp.sum(
        ((owner_of[:, :, None] == owner_of[:, None, :]) & earlier[None]).astype(jnp.int32), axis=1
    )
    slot = rank * owners + owner_of
    chosen = slot[:, None, :] == jnp.arange(slots)[None, :, None]
    values = jnp.stack(
        [
            (child + 1).astype(F32), (code + 1).astype(F32), weights,
            jnp.exp(lengths * (-4.0 / 3.0)),
        ]
    )
    by_slot = jnp.sum(jnp.where(chosen[None], values[:, :, None, :], 0.0), axis=3)
    halves = topo_dev // 2
    topo = topo_nodes.reshape(halves, 2, use).transpose(1, 2, 0).reshape(1, -1).astype(F32)
    meta = by_slot.reshape(fields * levels * 2, LANES)
    tail = -(-(meta.shape[0] + 1) // 8) * 8
    tail = jnp.concatenate(
        [meta, jnp.pad(topo, ((0, tail - meta.shape[0] - 1), (0, LANES - topo.shape[1])))], axis=0
    )
    chunk = 2 * site_own + tail.shape[0]
    peers = LANES // site_own
    packed = pl.pallas_call(
        functools.partial(pack_kernel, site_own=site_own, chunk=chunk),
        grid=(site_dev // LANES,),
        in_specs=[
            pl.BlockSpec((node_dev, states, LANES), lambda step: (0, 0, step)),
            pl.BlockSpec(tail.shape, lambda step: (0, 0)),
        ],
        out_specs=pl.BlockSpec((peers * chunk, LANES), lambda step: (step, 0)),
        out_shape=jax.ShapeDtypeStruct((owners * chunk, LANES), F32),
    )(leaf_partials, tail)
    received = lax.all_to_all(
        packed.reshape(owners, chunk, LANES), "node", split_axis=0, concat_axis=0, tiled=True
    ).reshape(owners * chunk, LANES)
    own_counts = lax.dynamic_slice_in_dim(counts, device * site_own, site_own)
    scaled = jnp.tile(own_counts.astype(F32) / sites_all, LANES // site_own)[None, :]

    out_rows = 8
    partial = pl.pallas_call(
        functools.partial(
            dag_kernel, levels=levels, owners=owners, node_dev=node_dev, site_own=site_own,
            states=states, fields=fields, chunk=chunk, out_rows=out_rows,
        ),
        out_shape=jax.ShapeDtypeStruct((owners * out_rows, LANES), F32),
        scratch_shapes=[
            pltpu.VMEM((owners * node_dev, LANES), BF16),
            pltpu.VMEM((slots * (owners + 1), LANES), F32),
            pltpu.VMEM((levels * (fields - 1) * owners, slots), F32),
            pltpu.VMEM((use * halves, LANES), jnp.int32),
            pltpu.VMEM((owners // GROUP, GROUP * node_dev), F32),
            pltpu.VMEM((2 * owners, LANES), F32),
            pltpu.VMEM((2 * owners * node_dev, 4 * LANES), BF16),
            pltpu.VMEM((4 * owners * node_dev, 2 * LANES), BF16),
        ],
        compiler_params=pltpu.CompilerParams(vmem_limit_bytes=56 * 1024 * 1024),
    )(received, scaled)
    shares = lax.all_to_all(
        partial.reshape(owners, out_rows, LANES), "node", split_axis=0, concat_axis=0, tiled=True
    )
    mine = lax.psum(jnp.sum(shares[:, : slots // LANES + 1], axis=0), "site").reshape(-1)
    uses = received.reshape(owners, chunk, LANES)[:, 2 * site_own + meta.shape[0], : topo_dev * use]
    multiplicity = jnp.sum(
        (uses.reshape(-1)[None, :] == parents[levels - 1].astype(F32)[:, None]).astype(F32), axis=1
    )
    edge_gradient = multiplicity * jnp.sum(
        jnp.where(slot[levels - 1][:, None] == jnp.arange(slots)[None, :], mine[None, :slots], 0.0),
        axis=1,
    )
    topology = mine[slots : slots + 16].reshape(2, 8)[:, :halves].T.reshape(-1)
    return (topology, edge_gradient)


def solution(mesh):
    return jax.shard_map(
        on_device,
        mesh=mesh,
        in_specs=(
            P("node", None, "site"),
            P(None, "node", None),
            P(None, "node"),
            P(None, "node"),
            P("site"),
            P("node", None),
        ),
        out_specs=(P("node"), P("node")),
        check_vma=False,
    )
```

```python
import functools

import jax
import jax.numpy as jnp
from jax import lax
from jax.experimental import pallas as pl
from jax.experimental.pallas import tpu as pltpu
from jax.sharding import PartitionSpec as P

F32 = jnp.float32
BF16 = jnp.bfloat16
MASK = F32
SPREAD_UNROLL = 8
GATHER_UNROLL = 8
FINISH_UNROLL = 2
LAST_UNROLL = 2
EDGE_UNROLL = 8
LEAF_UNROLL = 4
LANES = 128
GROUP = 4


def pack_kernel(leaf_ref, out_ref, *, site_own):
    states = leaf_ref.shape[1]
    chunk = states // 2 * site_own
    for pair in range(states // 2):
        rows = jnp.concatenate([leaf_ref[:, 2 * pair, :], leaf_ref[:, 2 * pair + 1, :]], axis=0).T
        for peer in range(LANES // site_own):
            out_ref[peer * chunk + pair * site_own : peer * chunk + (pair + 1) * site_own, :] = (
                rows[peer * site_own : (peer + 1) * site_own]
            )


def table_kernel(
    place_ref, *refs, levels, owners, fields, shares, share_rows, entries,
):
    share_refs, (child_ref, table_ref, topo_ref, meta_ref) = refs[:shares], refs[shares:]
    size = owners * share_rows
    for step in range(shares):
        origin = lax.rem(place_ref[0] + (shares - step), shares)
        meta_ref[pl.ds(pl.multiple_of(origin * size, size), size), :] = share_refs[step][...]

    def rows_of(row):
        return meta_ref[
            pl.ds(row // share_rows * size + row % share_rows, owners, stride=share_rows), :
        ]

    child_ref[...] = meta_ref[:size, :]
    for level in range(levels):
        for field in range(1, fields):
            for part in range(2):
                block = rows_of((field * levels + level) * 2 + part).T
                table_ref[
                    pl.ds((level * (fields - 1) + field - 1) * owners, owners),
                    part * LANES : (part + 1) * LANES,
                ] = jnp.concatenate([block[:owners], block[owners:]], axis=1)
    block = rows_of(fields * levels * 2).T
    topo_ref[...] = jnp.concatenate(
        [block[:entries], block[entries : 2 * entries]], axis=1
    ).astype(jnp.int32)


def two_parts(value):
    high = value.astype(BF16)
    return high, (value - high.astype(F32)).astype(BF16)


def both_parts(value):
    return jnp.concatenate(two_parts(value), axis=1)


def dag_kernel(
    input_ref, child_ref, table_ref, topo_ref, scaled_ref, out_ref,
    current_ref, slot_ref, score_ref, term_ref, sums_ref, adjoint_ref,
    *, levels, owners, node_dev, site_own, states, fields, out_rows,
):
    half = 2 * node_dev
    slots = 4 * owners
    chunk = states // 2 * site_own
    child_rows = child_ref.shape[0] // owners
    pitch = slot_ref.shape[0] // slots
    left = lax.broadcasted_iota(jnp.int32, (LANES, LANES), 1) < LANES // 2
    left_nodes = left[:node_dev]

    def store_current(start, value, mask):
        high = value.astype(BF16).astype(F32)
        current_ref[pl.ds(start, value.shape[0]), :] = jnp.where(
            mask, high, value - high
        ).astype(BF16)

    apart = jnp.abs(
        lax.broadcasted_iota(jnp.int32, (LANES, LANES), 0)
        - lax.broadcasted_iota(jnp.int32, (LANES, LANES), 1)
    )
    fold = (apart % (site_own * states) == 0).astype(F32).astype(BF16)
    over_states = (apart % site_own == 0).astype(F32).astype(BF16)
    over_states_twice = jnp.concatenate([over_states, over_states], axis=0)
    settle = jnp.concatenate([fold, fold, over_states_twice], axis=0)

    def load_leaves(pair, carry):
        first = pl.multiple_of(pair * 2 * chunk, chunk)
        pieces = []
        for block in range(states // 2):
            a = input_ref[pl.ds(first + block * site_own, site_own), :]
            b = input_ref[pl.ds(first + chunk + block * site_own, site_own), :]
            pieces.append(jnp.where(left[:site_own], a, pltpu.roll(b, LANES // 2, 1)))
            pieces.append(jnp.where(left[:site_own], pltpu.roll(a, LANES // 2, 1), b))
        stacked = jnp.concatenate(pieces + pieces, axis=0)
        store_current(pl.multiple_of(pair * LANES, LANES), stacked.T, left)
        return carry

    lax.fori_loop(0, owners // 2, load_leaves, 0, unroll=LEAF_UNROLL)

    node_row = lax.broadcasted_iota(jnp.int32, (node_dev, LANES), 0).astype(F32) + 1.0
    pair_row = (lax.broadcasted_iota(jnp.int32, (half, slots), 0).astype(F32) + 1.0).astype(MASK)
    blank = jnp.zeros((node_dev, LANES), BF16)
    pair_wide = lax.broadcasted_iota(jnp.int32, (half, slots), 0).astype(F32) + 1.0

    def spread(level):
        def body(pair, carry):
            rows = current_ref[pl.ds(pl.multiple_of(pair * LANES, LANES), LANES), :]
            both = jnp.concatenate(
                [
                    jnp.concatenate([rows[:node_dev], blank], axis=0),
                    jnp.concatenate([blank, rows[node_dev:]], axis=0),
                ],
                axis=1,
            )
            for part in range(2):
                hot = jnp.concatenate(
                    [
                        node_row == child_ref[
                            pl.ds((2 * pair + side) * child_rows + level * 2 + part, 1), :
                        ]
                        for side in range(2)
                    ],
                    axis=0,
                )
                picked = lax.dot_general(
                    hot.astype(F32).astype(BF16), both, (((0,), (0,)), ((), ())),
                    preferred_element_type=F32,
                )
                for side in range(2):
                    slot_ref[
                        pl.ds(part * half * pitch + 2 * pair + side, half, stride=pitch), :
                    ] = picked[:, side * LANES : (side + 1) * LANES]
            return carry

        lax.fori_loop(0, owners // 2, body, 0, unroll=SPREAD_UNROLL)

    def slot_rows(dest):
        pieces = [
            slot_ref[pl.ds((rank * owners + dest) * pitch, owners), :]
            for rank in range(4)
        ]
        return jnp.concatenate(pieces, axis=0).astype(BF16)

    def gather(level):
        def body(dest, carry):
            base = level * (fields - 1) * owners + dest
            code = table_ref[pl.ds(base, 1), :]
            weight = table_ref[pl.ds(base + owners, 1), :]
            survival = table_ref[pl.ds(base + 2 * owners, 1), :]
            hit = pair_row == code.astype(MASK)
            scales = []
            for scale in (weight * survival, weight * ((1.0 - survival) * 0.25)):
                high = scale.astype(BF16).astype(F32)
                scales += [high, scale - high]
            chosen = jnp.concatenate(
                [
                    jnp.where(hit, scale.astype(MASK), jnp.zeros((), MASK)).astype(BF16)
                    for scale in scales
                ],
                axis=0,
            )
            product = jnp.dot(chosen, slot_rows(dest), preferred_element_type=F32)
            start = pl.multiple_of(dest * half, half)
            sums_ref[pl.ds(start, half), : 2 * LANES] = both_parts(
                product[:half] + product[half : 2 * half]
            )
            sums_ref[pl.ds(start, half), 2 * LANES :] = both_parts(
                product[2 * half : 3 * half] + product[3 * half :]
            )
            return carry

        lax.fori_loop(0, owners, body, 0, unroll=GATHER_UNROLL)

    def pair_sums(group):
        rows = GROUP * half
        start = pl.multiple_of(group * rows, rows)
        sums = jnp.dot(sums_ref[pl.ds(start, rows), :], settle, preferred_element_type=F32)
        first = [sums[item * half : item * half + node_dev] for item in range(GROUP)]
        second = [sums[item * half + node_dev : (item + 1) * half] for item in range(GROUP)]
        return jnp.concatenate(first, axis=0), jnp.concatenate(second, axis=0)

    group_nodes = GROUP * node_dev

    def finish():
        mask = lax.broadcasted_iota(jnp.int32, (group_nodes, LANES), 1) < LANES // 2

        def body(group, carry):
            first, second = pair_sums(group)
            store_current(pl.multiple_of(group * group_nodes, group_nodes), first * second, mask)
            return carry

        lax.fori_loop(0, owners // GROUP, body, 0, unroll=FINISH_UNROLL)

    def finish_last():
        lane = lax.broadcasted_iota(jnp.int32, (group_nodes, LANES), 1)

        def body(group, carry):
            first, second = pair_sums(group)
            scaled = scaled_ref[...]
            likelihood = 0.125 * jnp.dot(
                both_parts(first * second), over_states_twice, preferred_element_type=F32
            )
            logs = scaled * jnp.log(likelihood)
            high = logs.astype(BF16).astype(F32)
            middle = (logs - high).astype(BF16).astype(F32)
            packed = jnp.where(
                lane < site_own, high,
                jnp.where(
                    lane < 2 * site_own, middle,
                    jnp.where(lane < 3 * site_own, logs - high - middle, 0.0),
                ),
            )
            score_ref[pl.ds(group, 1), :] = lax.dot_general(
                jnp.ones((8, LANES), BF16), packed.astype(BF16), (((1,), (1,)), ((), ())),
                preferred_element_type=F32,
            )[:1]
            factor = scaled * 0.25 / likelihood
            first, second = second * factor, first * factor
            adjoint = jnp.concatenate(
                [
                    value[item * node_dev : (item + 1) * node_dev]
                    for item in range(GROUP)
                    for value in (first, second)
                ],
                axis=0,
            )
            parts = both_parts(adjoint)
            summed = both_parts(
                0.5 * jnp.dot(parts, over_states_twice, preferred_element_type=F32)
            )
            for item in range(GROUP):
                start = pl.multiple_of((group * GROUP + item) * 2 * half, 2 * half)
                adjoint_ref[pl.ds(start, half), :] = parts[item * half : (item + 1) * half]
                adjoint_ref[pl.ds(start + half, half), :] = summed[item * half : (item + 1) * half]
            return carry

        lax.fori_loop(0, owners // GROUP, body, 0, unroll=LAST_UNROLL)

    def edges(level):
        def body(dest, carry):
            base = level * (fields - 1) * owners + dest
            code = table_ref[pl.ds(base, 1), :]
            survival = table_ref[pl.ds(base + 2 * owners, 1), :]
            rows = slot_rows(dest)
            against = lax.dot_general(
                adjoint_ref[pl.ds(pl.multiple_of(dest * 2 * half, 2 * half), 2 * half), :],
                jnp.concatenate([rows, rows], axis=1),
                (((1,), (1,)), ((), ())), preferred_element_type=F32,
            )
            found = pair_wide == code
            edge = survival * jnp.sum(
                jnp.where(found, against[:half], 0.0), axis=0, keepdims=True
            ) + ((1.0 - survival) * 0.25) * jnp.sum(
                jnp.where(found, against[half:], 0.0), axis=0, keepdims=True
            )
            for part in range(2):
                term_ref[pl.ds(part * owners + dest, 1), :] = edge[
                    :, part * LANES : (part + 1) * LANES
                ]
            return carry

        lax.fori_loop(0, owners, body, 0, unroll=EDGE_UNROLL)

    for level in range(levels):
        spread(level)
        gather(level)
        if level < levels - 1:
            finish()
    finish_last()
    edges(levels - 1)

    score = score_ref[...]
    score_high = score.astype(BF16)
    score_rest = score - score_high.astype(F32)
    score_middle = score_rest.astype(BF16)
    score_low = (score_rest - score_middle.astype(F32)).astype(BF16)
    totals = [jnp.zeros((1, LANES), F32), jnp.zeros((1, LANES), F32)]
    for chunk in range(topo_ref.shape[0]):
        entry = topo_ref[chunk : chunk + 1, :]
        group_of = entry // group_nodes
        local_of = entry - group_of * group_nodes
        group_row = lax.broadcasted_iota(jnp.int32, (owners // GROUP, LANES), 0)
        group_hot = (group_row == group_of).astype(F32).astype(BF16)
        found = sum(
            lax.dot_general(piece, group_hot, (((0,), (0,)), ((), ())), preferred_element_type=F32)
            for piece in (score_high, score_middle, score_low)
        )
        row = lax.broadcasted_iota(jnp.int32, (group_nodes, LANES), 0)
        totals[chunk % 2] = totals[chunk % 2] + jnp.sum(
            jnp.where(row == local_of, found, 0.0), axis=0, keepdims=True
        )
    def place(row, block):
        turned = block.T
        out_ref[pl.ds(row, owners, stride=out_rows), : 2 * block.shape[0]] = jnp.concatenate(
            [turned[:owners], turned[owners:]], axis=1
        )

    for part in range(2):
        place(part, term_ref[part * owners : (part + 1) * owners, :])
    place(2, jnp.concatenate(totals + [jnp.zeros((6, LANES), F32)], axis=0))


def on_device(leaf_partials, dag_edges, weights, lengths, counts, topo_nodes):
    node_dev, states, site_dev = leaf_partials.shape
    levels, edge_dev, _ = dag_edges.shape
    owners = lax.axis_size("node")
    device = lax.axis_index("node")
    sites_all = site_dev * lax.axis_size("site")
    site_own = site_dev // owners
    ranks = 4
    slots = ranks * owners
    fields = 4
    topo_dev, use = topo_nodes.shape

    child = dag_edges[:, :, 0] - device * node_dev
    parents = dag_edges[:, :, 1]
    owner_of = parents // node_dev
    code = dag_edges[:, :, 2] * node_dev + parents - owner_of * node_dev
    earlier = jnp.arange(edge_dev)[:, None] < jnp.arange(edge_dev)[None, :]
    rank = jnp.sum(
        ((owner_of[:, :, None] == owner_of[:, None, :]) & earlier[None]).astype(jnp.int32), axis=1
    )
    slot = rank * owners + owner_of
    chosen = slot[:, None, :] == jnp.arange(slots)[None, :, None]
    values = jnp.stack(
        [
            (child + 1).astype(F32), (code + 1).astype(F32), weights,
            jnp.exp(lengths * (-4.0 / 3.0)),
        ]
    )
    by_slot = jnp.sum(jnp.where(chosen[None], values[:, :, None, :], 0.0), axis=3)
    halves = topo_dev // 2
    topo = topo_nodes.reshape(halves, 2, use).transpose(1, 2, 0).reshape(1, -1).astype(F32)
    meta = by_slot.reshape(fields * levels * 2, LANES)
    shares = lax.axis_size("site")
    share_rows = -(-(meta.shape[0] + 1) // (8 * shares)) * 8
    place = lax.axis_index("site")
    meta = jnp.concatenate(
        [
            meta,
            jnp.pad(
                topo,
                ((0, share_rows * shares - meta.shape[0] - 1), (0, LANES - topo.shape[1])),
            ),
        ],
        axis=0,
    )
    share = lax.dynamic_slice_in_dim(meta, place * share_rows, share_rows)
    share = lax.all_to_all(
        jnp.broadcast_to(share[None], (owners, share_rows, LANES)), "node",
        split_axis=0, concat_axis=0, tiled=True,
    ).reshape(owners * share_rows, LANES)
    met = [share] + [
        lax.ppermute(share, "site", [(k, (k + step) % shares) for k in range(shares)])
        for step in range(1, shares)
    ]
    vmem = pl.BlockSpec(memory_space=pltpu.VMEM)
    entries = use * halves
    child_table, edge_table, topologies = pl.pallas_call(
        functools.partial(
            table_kernel, levels=levels, owners=owners, fields=fields, shares=shares,
            share_rows=share_rows, entries=entries,
        ),
        in_specs=[pl.BlockSpec(memory_space=pltpu.SMEM)] + [vmem] * shares,
        out_shape=[
            jax.ShapeDtypeStruct((owners * share_rows, LANES), F32),
            jax.ShapeDtypeStruct((levels * (fields - 1) * owners, slots), F32),
            jax.ShapeDtypeStruct((entries, LANES), jnp.int32),
        ],
        scratch_shapes=[pltpu.VMEM((owners * share_rows * shares, LANES), F32)],
    )(place.astype(jnp.int32).reshape(1), *met)

    chunk = states // 2 * site_own
    peers = LANES // site_own
    packed = pl.pallas_call(
        functools.partial(pack_kernel, site_own=site_own),
        grid=(site_dev // LANES,),
        in_specs=[pl.BlockSpec((node_dev, states, LANES), lambda step: (0, 0, step))],
        out_specs=pl.BlockSpec((peers * chunk, LANES), lambda step: (step, 0)),
        out_shape=jax.ShapeDtypeStruct((owners * chunk, LANES), F32),
    )(leaf_partials)
    received = lax.all_to_all(
        packed.reshape(owners, chunk, LANES), "node", split_axis=0, concat_axis=0, tiled=True
    ).reshape(owners * chunk, LANES)
    own_counts = lax.dynamic_slice_in_dim(counts, device * site_own, site_own)
    scaled = jnp.tile(own_counts.astype(F32) / sites_all, LANES // site_own)[None, :]

    out_rows = 8
    partial = pl.pallas_call(
        functools.partial(
            dag_kernel, levels=levels, owners=owners, node_dev=node_dev, site_own=site_own,
            states=states, fields=fields, out_rows=out_rows,
        ),
        out_shape=jax.ShapeDtypeStruct((owners * out_rows, LANES), F32),
        scratch_shapes=[
            pltpu.VMEM((owners * node_dev, LANES), BF16),
            pltpu.VMEM((slots * (owners + 1), LANES), F32),
            pltpu.VMEM((owners // GROUP, GROUP * node_dev), F32),
            pltpu.VMEM((2 * owners, LANES), F32),
            pltpu.VMEM((2 * owners * node_dev, 4 * LANES), BF16),
            pltpu.VMEM((4 * owners * node_dev, 2 * LANES), BF16),
        ],
        compiler_params=pltpu.CompilerParams(vmem_limit_bytes=56 * 1024 * 1024),
    )(received, child_table, edge_table, topologies, scaled)
    shares = lax.all_to_all(
        partial.reshape(owners, out_rows, LANES), "node", split_axis=0, concat_axis=0, tiled=True
    )
    mine = lax.psum(jnp.sum(shares[:, : slots // LANES + 1], axis=0), "site").reshape(-1)
    multiplicity = jnp.sum(
        (topologies.reshape(-1)[None, :] == parents[levels - 1][:, None]).astype(F32), axis=1
    )
    edge_gradient = multiplicity * jnp.sum(
        jnp.where(slot[levels - 1][:, None] == jnp.arange(slots)[None, :], mine[None, :slots], 0.0),
        axis=1,
    )
    topology = mine[slots : slots + 16].reshape(2, 8)[:, :halves].T.reshape(-1)
    return (topology, edge_gradient)


def solution(mesh):
    return jax.shard_map(
        on_device,
        mesh=mesh,
        in_specs=(
            P("node", None, "site"),
            P(None, "node", None),
            P(None, "node"),
            P(None, "node"),
            P("site"),
            P("node", None),
        ),
        out_specs=(P("node"), P("node")),
        check_vma=False,
    )
```

```python
import functools

import jax
import jax.numpy as jnp
from jax import lax
from jax.experimental import pallas as pl
from jax.experimental.pallas import tpu as pltpu
from jax.sharding import PartitionSpec as P

F32 = jnp.float32
BF16 = jnp.bfloat16
SPREAD_UNROLL = 8
GATHER_UNROLL = 8
FINISH_UNROLL = 2
LAST_UNROLL = 2
EDGE_UNROLL = 8
LEAF_UNROLL = 4
LANES = 128
GROUP = 4


def pack_kernel(leaf_ref, out_ref, *, site_own):
    states = leaf_ref.shape[1]
    chunk = states // 2 * site_own
    for pair in range(states // 2):
        rows = jnp.concatenate([leaf_ref[:, 2 * pair, :], leaf_ref[:, 2 * pair + 1, :]], axis=0).T
        for peer in range(LANES // site_own):
            out_ref[peer * chunk + pair * site_own : peer * chunk + (pair + 1) * site_own, :] = (
                rows[peer * site_own : (peer + 1) * site_own]
            )


def table_kernel(
    place_ref, *refs, levels, owners, fields, shares, share_rows, entries,
):
    share_refs, (child_ref, table_ref, topo_ref, meta_ref) = refs[:shares], refs[shares:]
    size = owners * share_rows
    for step in range(shares):
        origin = lax.rem(place_ref[0] + (shares - step), shares)
        meta_ref[pl.ds(pl.multiple_of(origin * size, size), size), :] = share_refs[step][...]

    def rows_of(row):
        return meta_ref[
            pl.ds(row // share_rows * size + row % share_rows, owners, stride=share_rows), :
        ]

    child_ref[...] = meta_ref[:size, :]
    for level in range(levels):
        for field in range(1, fields):
            for part in range(2):
                block = rows_of((field * levels + level) * 2 + part).T
                table_ref[
                    pl.ds((level * (fields - 1) + field - 1) * owners, owners),
                    part * LANES : (part + 1) * LANES,
                ] = jnp.concatenate([block[:owners], block[owners:]], axis=1)
    block = rows_of(fields * levels * 2).T
    topo_ref[...] = jnp.concatenate(
        [block[:entries], block[entries : 2 * entries]], axis=1
    ).astype(jnp.int32)


def scale_kernel(table_ref, out_ref, *, owners, fields, per_step):
    step = pl.program_id(0)
    level = step * per_step // owners
    slots = table_ref.shape[1]
    row = lax.broadcasted_iota(jnp.int32, (8, slots), 0)
    rank = lax.broadcasted_iota(jnp.int32, (8, LANES), 0)
    left = lax.broadcasted_iota(jnp.int32, (8, LANES), 1) < LANES // 2
    sides = jnp.where(
        (left & (rank < 3)) | (~left & (rank >= 3) & (rank < 6)), 1.0, 0.0
    ).astype(BF16)
    for item in range(per_step):
        base = level * (fields - 1) * owners + (step * per_step - level * owners) + item
        weight = table_ref[pl.ds(base + owners, 1), :]
        survival = table_ref[pl.ds(base + 2 * owners, 1), :]
        stacked = jnp.zeros((8, slots), F32)
        for side, scale in enumerate((weight * survival, weight * ((1.0 - survival) * 0.25))):
            for part in range(3):
                high = scale.astype(BF16).astype(F32)
                stacked = jnp.where(row == 3 * side + part, high, stacked)
                scale = scale - high
        out_ref[item * slots : (item + 1) * slots, :] = lax.dot_general(
            stacked.astype(BF16), sides, (((0,), (0,)), ((), ())), preferred_element_type=F32
        )


def two_parts(value):
    high = value.astype(BF16)
    return high, (value - high.astype(F32)).astype(BF16)


def both_parts(value):
    return jnp.concatenate(two_parts(value), axis=1)


def dag_kernel(
    input_ref, child_ref, table_ref, topo_ref, scaled_ref, scale_ref, out_ref,
    current_ref, slot_ref, score_ref, term_ref, sums_ref, adjoint_ref, weighted_ref, factor_ref,
    arrived,
    *, levels, owners, node_dev, site_own, states, fields, out_rows,
):
    half = 2 * node_dev
    slots = 4 * owners
    chunk = states // 2 * site_own
    child_rows = child_ref.shape[0] // owners
    pitch = slot_ref.shape[0] // slots
    size = owners * slots
    left = lax.broadcasted_iota(jnp.int32, (LANES, LANES), 1) < LANES // 2

    def fetch(level):
        return pltpu.make_async_copy(
            scale_ref.at[pl.ds(level * size, size), :], factor_ref.at[level % 2],
            arrived.at[level % 2],
        )

    for level in range(min(2, levels)):
        fetch(level).start()

    def store_current(source, value):
        high, low = two_parts(value)
        start = pl.multiple_of(source * half, half)
        current_ref[pl.ds(start, node_dev), :] = high
        current_ref[pl.ds(start + node_dev, node_dev), :] = low

    from_lane = lax.broadcasted_iota(jnp.int32, (LANES, LANES), 0)
    to_lane = lax.broadcasted_iota(jnp.int32, (LANES, LANES), 1)
    apart = jnp.abs(from_lane - to_lane)
    over_states = apart % site_own == 0
    settle = (
        (apart % (site_own * states) == 0) | (over_states & (from_lane >= LANES // 2))
    ).astype(F32).astype(BF16)
    settle = jnp.concatenate([settle, settle], axis=0)
    over_states = over_states.astype(F32).astype(BF16)
    over_states_twice = jnp.concatenate([over_states, over_states], axis=0)

    def load_leaves(pair, carry):
        first = pl.multiple_of(pair * 2 * chunk, chunk)
        pieces = []
        for block in range(states // 2):
            a = input_ref[pl.ds(first + block * site_own, site_own), :]
            b = input_ref[pl.ds(first + chunk + block * site_own, site_own), :]
            pieces.append(jnp.where(left[:site_own], a, pltpu.roll(b, LANES // 2, 1)))
            pieces.append(jnp.where(left[:site_own], pltpu.roll(a, LANES // 2, 1), b))
        stacked = jnp.concatenate(pieces + pieces, axis=0)
        turned = stacked.T
        store_current(2 * pair, turned[:node_dev])
        store_current(2 * pair + 1, turned[node_dev:])
        return carry

    lax.fori_loop(0, owners // 2, load_leaves, 0, unroll=LEAF_UNROLL)

    node_row = lax.broadcasted_iota(jnp.int32, (node_dev, LANES), 0).astype(F32) + 1.0
    pair_row = lax.broadcasted_iota(jnp.int32, (half, slots), 0).astype(F32) + 1.0
    blank = jnp.zeros((half, LANES), BF16)

    def spread(level):
        def body(pair, carry):
            rows = current_ref[pl.ds(pl.multiple_of(pair * 2 * half, 2 * half), 2 * half), :]
            both = jnp.concatenate(
                [
                    jnp.concatenate([rows[:half], blank], axis=0),
                    jnp.concatenate([blank, rows[half:]], axis=0),
                ],
                axis=1,
            )
            for part in range(2):
                hot = []
                for side in range(2):
                    child = child_ref[
                        pl.ds((2 * pair + side) * child_rows + level * 2 + part, 1), :
                    ]
                    hot += [(node_row == child).astype(F32).astype(BF16)] * 2
                picked = lax.dot_general(
                    jnp.concatenate(hot, axis=0), both, (((0,), (0,)), ((), ())),
                    preferred_element_type=F32,
                )
                for side in range(2):
                    slot_ref[
                        pl.ds(part * half * pitch + 2 * pair + side, half, stride=pitch), :
                    ] = picked[:, side * LANES : (side + 1) * LANES]
            return carry

        lax.fori_loop(0, owners // 2, body, 0, unroll=SPREAD_UNROLL)

    def code_of(level, dest):
        return table_ref[pl.ds(level * (fields - 1) * owners + dest, 1), :]

    def gather(level, last):
        fetch(level).wait()

        def body(dest, carry):
            rows = jnp.concatenate(
                [
                    slot_ref[pl.ds((rank * owners + dest) * pitch, owners), :]
                    for rank in range(4)
                ],
                axis=0,
            )
            factor = factor_ref[
                level % 2, pl.ds(pl.multiple_of(dest * slots, slots), slots), :
            ]
            weighted = both_parts(rows * factor)
            if last:
                weighted_ref[pl.ds(pl.multiple_of(dest * slots, slots), slots), :] = weighted
            hit = (pair_row == code_of(level, dest)).astype(F32).astype(BF16)
            product = jnp.dot(hit, weighted, preferred_element_type=F32)
            sums_ref[pl.ds(pl.multiple_of(dest * half, half), half), :] = both_parts(
                product[:, :LANES] + product[:, LANES:]
            )
            return carry

        lax.fori_loop(0, owners, body, 0, unroll=GATHER_UNROLL)
        if level + 2 < levels:
            fetch(level + 2).start()

    def pair_sums(group):
        rows = GROUP * half
        start = pl.multiple_of(group * rows, rows)
        sums = jnp.dot(sums_ref[pl.ds(start, rows), :], settle, preferred_element_type=F32)
        first = [sums[item * half : item * half + node_dev] for item in range(GROUP)]
        second = [sums[item * half + node_dev : (item + 1) * half] for item in range(GROUP)]
        return jnp.concatenate(first, axis=0), jnp.concatenate(second, axis=0)

    group_nodes = GROUP * node_dev

    def finish():
        def body(group, carry):
            first, second = pair_sums(group)
            value = first * second
            for item in range(GROUP):
                store_current(
                    group * GROUP + item, value[item * node_dev : (item + 1) * node_dev]
                )
            return carry

        lax.fori_loop(0, owners // GROUP, body, 0, unroll=FINISH_UNROLL)

    def finish_last():
        lane = lax.broadcasted_iota(jnp.int32, (group_nodes, LANES), 1)
        wide_left = lax.broadcasted_iota(jnp.int32, (GROUP * half, LANES), 1) < LANES // 2

        def body(group, carry):
            first, second = pair_sums(group)
            scaled = scaled_ref[...]
            likelihood = 0.125 * jnp.dot(
                both_parts(first * second), over_states_twice, preferred_element_type=F32
            )
            logs = scaled * jnp.log(likelihood)
            high = logs.astype(BF16).astype(F32)
            middle = (logs - high).astype(BF16).astype(F32)
            packed = jnp.where(
                lane < site_own, high,
                jnp.where(
                    lane < 2 * site_own, middle,
                    jnp.where(lane < 3 * site_own, logs - high - middle, 0.0),
                ),
            )
            score_ref[pl.ds(group, 1), :] = lax.dot_general(
                jnp.ones((8, LANES), BF16), packed.astype(BF16), (((1,), (1,)), ((), ())),
                preferred_element_type=F32,
            )[:1]
            factor = scaled * 0.25 / likelihood
            first, second = second * factor, first * factor
            adjoint = jnp.concatenate(
                [
                    value[item * node_dev : (item + 1) * node_dev]
                    for item in range(GROUP)
                    for value in (first, second)
                ],
                axis=0,
            )
            summed = 0.5 * jnp.dot(
                both_parts(adjoint), over_states_twice, preferred_element_type=F32
            )
            start = pl.multiple_of(group * GROUP * half, GROUP * half)
            adjoint_ref[pl.ds(start, GROUP * half), :] = both_parts(
                jnp.where(wide_left, adjoint, summed)
            )
            return carry

        lax.fori_loop(0, owners // GROUP, body, 0, unroll=LAST_UNROLL)

    def edges(level):
        def body(dest, carry):
            parts = adjoint_ref[pl.ds(pl.multiple_of(dest * half, half), half), :]
            high = parts[:, :LANES]
            against = lax.dot_general(
                jnp.concatenate(
                    [
                        jnp.concatenate([high, high], axis=1),
                        jnp.concatenate([parts[:, LANES:], jnp.zeros_like(high)], axis=1),
                    ],
                    axis=0,
                ),
                weighted_ref[pl.ds(pl.multiple_of(dest * slots, slots), slots), :],
                (((1,), (1,)), ((), ())), preferred_element_type=F32,
            )
            edge = jnp.sum(
                jnp.where(
                    pair_row == code_of(level, dest), against[:half] + against[half:], 0.0
                ),
                axis=0, keepdims=True,
            )
            for part in range(2):
                term_ref[pl.ds(part * owners + dest, 1), :] = edge[
                    :, part * LANES : (part + 1) * LANES
                ]
            return carry

        lax.fori_loop(0, owners, body, 0, unroll=EDGE_UNROLL)

    for level in range(levels):
        spread(level)
        gather(level, level == levels - 1)
        if level < levels - 1:
            finish()
    finish_last()
    edges(levels - 1)

    score = score_ref[...]
    score_high = score.astype(BF16)
    score_rest = score - score_high.astype(F32)
    score_middle = score_rest.astype(BF16)
    score_low = (score_rest - score_middle.astype(F32)).astype(BF16)
    totals = [jnp.zeros((1, LANES), F32), jnp.zeros((1, LANES), F32)]
    for chunk in range(topo_ref.shape[0]):
        entry = topo_ref[chunk : chunk + 1, :]
        group_of = entry // group_nodes
        local_of = entry - group_of * group_nodes
        group_row = lax.broadcasted_iota(jnp.int32, (owners // GROUP, LANES), 0)
        group_hot = (group_row == group_of).astype(F32).astype(BF16)
        found = sum(
            lax.dot_general(piece, group_hot, (((0,), (0,)), ((), ())), preferred_element_type=F32)
            for piece in (score_high, score_middle, score_low)
        )
        row = lax.broadcasted_iota(jnp.int32, (group_nodes, LANES), 0)
        totals[chunk % 2] = totals[chunk % 2] + jnp.sum(
            jnp.where(row == local_of, found, 0.0), axis=0, keepdims=True
        )
    def place(row, block):
        turned = block.T
        out_ref[pl.ds(row, owners, stride=out_rows), : 2 * block.shape[0]] = jnp.concatenate(
            [turned[:owners], turned[owners:]], axis=1
        )

    for part in range(2):
        place(part, term_ref[part * owners : (part + 1) * owners, :])
    place(2, jnp.concatenate(totals + [jnp.zeros((6, LANES), F32)], axis=0))


def on_device(leaf_partials, dag_edges, weights, lengths, counts, topo_nodes):
    node_dev, states, site_dev = leaf_partials.shape
    levels, edge_dev, _ = dag_edges.shape
    owners = lax.axis_size("node")
    device = lax.axis_index("node")
    sites_all = site_dev * lax.axis_size("site")
    site_own = site_dev // owners
    ranks = 4
    slots = ranks * owners
    fields = 4
    topo_dev, use = topo_nodes.shape

    child = dag_edges[:, :, 0] - device * node_dev
    parents = dag_edges[:, :, 1]
    owner_of = parents // node_dev
    code = dag_edges[:, :, 2] * node_dev + parents - owner_of * node_dev
    earlier = jnp.arange(edge_dev)[:, None] < jnp.arange(edge_dev)[None, :]
    rank = jnp.sum(
        ((owner_of[:, :, None] == owner_of[:, None, :]) & earlier[None]).astype(jnp.int32), axis=1
    )
    slot = rank * owners + owner_of
    chosen = slot[:, None, :] == jnp.arange(slots)[None, :, None]
    values = jnp.stack(
        [
            (child + 1).astype(F32), (code + 1).astype(F32), weights,
            jnp.exp(lengths * (-4.0 / 3.0)),
        ]
    )
    by_slot = jnp.sum(jnp.where(chosen[None], values[:, :, None, :], 0.0), axis=3)
    halves = topo_dev // 2
    topo = topo_nodes.reshape(halves, 2, use).transpose(1, 2, 0).reshape(1, -1).astype(F32)
    meta = by_slot.reshape(fields * levels * 2, LANES)
    shares = lax.axis_size("site")
    share_rows = -(-(meta.shape[0] + 1) // (8 * shares)) * 8
    place = lax.axis_index("site")
    meta = jnp.concatenate(
        [
            meta,
            jnp.pad(
                topo,
                ((0, share_rows * shares - meta.shape[0] - 1), (0, LANES - topo.shape[1])),
            ),
        ],
        axis=0,
    )
    share = lax.dynamic_slice_in_dim(meta, place * share_rows, share_rows)
    share = lax.all_to_all(
        jnp.broadcast_to(share[None], (owners, share_rows, LANES)), "node",
        split_axis=0, concat_axis=0, tiled=True,
    ).reshape(owners * share_rows, LANES)
    met = [share] + [
        lax.ppermute(share, "site", [(k, (k + step) % shares) for k in range(shares)])
        for step in range(1, shares)
    ]
    vmem = pl.BlockSpec(memory_space=pltpu.VMEM)
    entries = use * halves
    child_table, edge_table, topologies = pl.pallas_call(
        functools.partial(
            table_kernel, levels=levels, owners=owners, fields=fields, shares=shares,
            share_rows=share_rows, entries=entries,
        ),
        in_specs=[pl.BlockSpec(memory_space=pltpu.SMEM)] + [vmem] * shares,
        out_shape=[
            jax.ShapeDtypeStruct((owners * share_rows, LANES), F32),
            jax.ShapeDtypeStruct((levels * (fields - 1) * owners, slots), F32),
            jax.ShapeDtypeStruct((entries, LANES), jnp.int32),
        ],
        scratch_shapes=[pltpu.VMEM((owners * share_rows * shares, LANES), F32)],
    )(place.astype(jnp.int32).reshape(1), *met)

    chunk = states // 2 * site_own
    peers = LANES // site_own
    packed = pl.pallas_call(
        functools.partial(pack_kernel, site_own=site_own),
        grid=(site_dev // LANES,),
        in_specs=[pl.BlockSpec((node_dev, states, LANES), lambda step: (0, 0, step))],
        out_specs=pl.BlockSpec((peers * chunk, LANES), lambda step: (step, 0)),
        out_shape=jax.ShapeDtypeStruct((owners * chunk, LANES), F32),
    )(leaf_partials)
    received = lax.all_to_all(
        packed.reshape(owners, chunk, LANES), "node", split_axis=0, concat_axis=0, tiled=True
    ).reshape(owners * chunk, LANES)
    own_counts = lax.dynamic_slice_in_dim(counts, device * site_own, site_own)
    scaled = jnp.tile(own_counts.astype(F32) / sites_all, LANES // site_own)[None, :]

    per_step = 8
    scales = pl.pallas_call(
        functools.partial(scale_kernel, owners=owners, fields=fields, per_step=per_step),
        grid=(levels * owners // per_step,),
        in_specs=[pl.BlockSpec(edge_table.shape, lambda step: (0, 0))],
        out_specs=pl.BlockSpec((per_step * slots, LANES), lambda step: (step, 0)),
        out_shape=jax.ShapeDtypeStruct((levels * owners * slots, LANES), F32),
    )(edge_table)

    out_rows = 8
    partial = pl.pallas_call(
        functools.partial(
            dag_kernel, levels=levels, owners=owners, node_dev=node_dev, site_own=site_own,
            states=states, fields=fields, out_rows=out_rows,
        ),
        in_specs=[vmem] * 5 + [pl.BlockSpec(memory_space=pl.ANY)],
        out_shape=jax.ShapeDtypeStruct((owners * out_rows, LANES), F32),
        scratch_shapes=[
            pltpu.VMEM((2 * owners * node_dev, LANES), BF16),
            pltpu.VMEM((slots * (owners + 1), LANES), F32),
            pltpu.VMEM((owners // GROUP, GROUP * node_dev), F32),
            pltpu.VMEM((2 * owners, LANES), F32),
            pltpu.VMEM((2 * owners * node_dev, 2 * LANES), BF16),
            pltpu.VMEM((2 * owners * node_dev, 2 * LANES), BF16),
            pltpu.VMEM((owners * slots, 2 * LANES), BF16),
            pltpu.VMEM((2, owners * slots, LANES), F32),
            pltpu.SemaphoreType.DMA((2,)),
        ],
        compiler_params=pltpu.CompilerParams(vmem_limit_bytes=56 * 1024 * 1024),
    )(received, child_table, edge_table, topologies, scaled, scales)
    shares = lax.all_to_all(
        partial.reshape(owners, out_rows, LANES), "node", split_axis=0, concat_axis=0, tiled=True
    )
    mine = lax.psum(jnp.sum(shares[:, : slots // LANES + 1], axis=0), "site").reshape(-1)
    multiplicity = jnp.sum(
        (topologies.reshape(-1)[None, :] == parents[levels - 1][:, None]).astype(F32), axis=1
    )
    edge_gradient = multiplicity / weights[levels - 1] * jnp.sum(
        jnp.where(slot[levels - 1][:, None] == jnp.arange(slots)[None, :], mine[None, :slots], 0.0),
        axis=1,
    )
    topology = mine[slots : slots + 16].reshape(2, 8)[:, :halves].T.reshape(-1)
    return (topology, edge_gradient)


def solution(mesh):
    return jax.shard_map(
        on_device,
        mesh=mesh,
        in_specs=(
            P("node", None, "site"),
            P(None, "node", None),
            P(None, "node"),
            P(None, "node"),
            P("site"),
            P("node", None),
        ),
        out_specs=(P("node"), P("node")),
        check_vma=False,
    )
```

```python
import functools

import jax
import jax.numpy as jnp
from jax import lax
from jax.experimental import pallas as pl
from jax.experimental.pallas import tpu as pltpu
from jax.sharding import PartitionSpec as P

F32 = jnp.float32
BF16 = jnp.bfloat16
SPREAD_UNROLL = 8
GATHER_UNROLL = 8
FINISH_UNROLL = 4
LAST_UNROLL = 4
EDGE_UNROLL = 8
LEAF_UNROLL = 4
LANES = 128
GROUP = 4


def pack_kernel(leaf_ref, out_ref, *, site_own):
    states = leaf_ref.shape[1]
    chunk = states // 2 * site_own
    for pair in range(states // 2):
        rows = jnp.concatenate([leaf_ref[:, 2 * pair, :], leaf_ref[:, 2 * pair + 1, :]], axis=0).T
        for peer in range(LANES // site_own):
            out_ref[peer * chunk + pair * site_own : peer * chunk + (pair + 1) * site_own, :] = (
                rows[peer * site_own : (peer + 1) * site_own]
            )


def slot_kernel(
    where_ref, dag_ref, weight_ref, length_ref, topo_ref, share_ref, slot_ref, meta_ref,
    *, levels, owners, node_dev, fields, share_rows,
):
    edges = weight_ref.shape[1]
    slots = 4 * owners

    def rows(count):
        return lax.broadcasted_iota(jnp.int32, (count, edges), 0)

    earlier = rows(edges) < lax.broadcasted_iota(jnp.int32, (edges, edges), 1)
    earlier = earlier.astype(F32).astype(BF16)
    meta_ref[...] = jnp.zeros(meta_ref.shape, F32)
    field_row = rows(8)
    for level in range(levels):
        child = dag_ref[level : level + 1, :] - where_ref[0] * node_dev
        parent = dag_ref[levels + level : levels + level + 1, :]
        rotation = dag_ref[2 * levels + level : 2 * levels + level + 1, :]
        owner_of = parent // node_dev
        code = rotation * node_dev + parent - owner_of * node_dev
        goes = (rows(owners) == owner_of).astype(F32)
        before = jnp.dot(goes.astype(BF16), earlier, preferred_element_type=F32)
        rank = jnp.sum(goes * before, axis=0, keepdims=True)
        slot = rank.astype(jnp.int32) * owners + owner_of
        slot_ref[level : level + 1, :] = slot
        values = jnp.zeros((8, edges), F32)
        for field, value in enumerate(
            (
                (child + 1).astype(F32), (code + 1).astype(F32), weight_ref[level : level + 1, :],
                jnp.exp(length_ref[level : level + 1, :] * (-4.0 / 3.0)),
            )
        ):
            values = jnp.where(field_row == field, value, values)
        parts = []
        for _ in range(3):
            parts.append(values.astype(BF16).astype(F32))
            values = values - parts[-1]
        found = lax.dot_general(
            jnp.concatenate(parts, axis=0).astype(BF16),
            (rows(slots) == slot).astype(F32).astype(BF16),
            (((1,), (1,)), ((), ())), preferred_element_type=F32,
        )
        found = found[:8] + found[8:16] + found[16:]
        for field in range(fields):
            for part in range(2):
                row = (field * levels + level) * 2 + part
                meta_ref[row : row + 1, :] = found[
                    field : field + 1, part * LANES : (part + 1) * LANES
                ]
    row = fields * levels * 2
    meta_ref[row : row + 1, : topo_ref.shape[1]] = topo_ref[...].astype(F32)
    share = meta_ref[pl.ds(pl.multiple_of(where_ref[1] * share_rows, share_rows), share_rows), :]
    for owner in range(owners):
        share_ref[owner * share_rows : (owner + 1) * share_rows, :] = share


def table_kernel(
    place_ref, *refs, levels, owners, fields, shares, share_rows, entries,
):
    share_refs, (child_ref, table_ref, topo_ref, meta_ref) = refs[:shares], refs[shares:]
    size = owners * share_rows
    for step in range(shares):
        origin = lax.rem(place_ref[0] + (shares - step), shares)
        meta_ref[pl.ds(pl.multiple_of(origin * size, size), size), :] = share_refs[step][...]

    def rows_of(row):
        return meta_ref[
            pl.ds(row // share_rows * size + row % share_rows, owners, stride=share_rows), :
        ]

    child_ref[...] = meta_ref[:size, :]
    for level in range(levels):
        for field in range(1, fields):
            for part in range(2):
                block = rows_of((field * levels + level) * 2 + part).T
                table_ref[
                    pl.ds((level * (fields - 1) + field - 1) * owners, owners),
                    part * LANES : (part + 1) * LANES,
                ] = jnp.concatenate([block[:owners], block[owners:]], axis=1)
    block = rows_of(fields * levels * 2).T
    use = entries // 2
    for part in range(2):
        start = 2 * part * use
        topo_ref[part * use : (part + 1) * use, :] = jnp.concatenate(
            [block[start : start + use], block[start + use : start + 2 * use]], axis=1
        ).astype(jnp.int32)


def two_parts(value):
    high = value.astype(BF16)
    return high, (value - high.astype(F32)).astype(BF16)


def both_parts(value):
    return jnp.concatenate(two_parts(value), axis=1)


def dag_kernel(
    input_ref, child_ref, table_ref, topo_ref, scaled_ref, out_ref,
    current_ref, slot_ref, score_ref, term_ref, sums_ref, adjoint_ref, weighted_ref,
    *, levels, owners, node_dev, site_own, states, fields, out_rows,
):
    half = 2 * node_dev
    slots = 4 * owners
    chunk = states // 2 * site_own
    child_rows = child_ref.shape[0] // owners
    pitch = slot_ref.shape[0] // slots
    left = lax.broadcasted_iota(jnp.int32, (LANES, LANES), 1) < LANES // 2

    def store_current(source, value):
        high, low = two_parts(value)
        start = pl.multiple_of(source * half, half)
        current_ref[pl.ds(start, node_dev), :] = high
        current_ref[pl.ds(start + node_dev, node_dev), :] = low

    from_lane = lax.broadcasted_iota(jnp.int32, (LANES, LANES), 0)
    to_lane = lax.broadcasted_iota(jnp.int32, (LANES, LANES), 1)
    apart = jnp.abs(from_lane - to_lane)
    over_states = apart % site_own == 0
    settle = (
        (apart % (site_own * states) == 0) | (over_states & (from_lane >= LANES // 2))
    ).astype(F32).astype(BF16)
    settle = jnp.concatenate([settle, settle], axis=0)
    over_states = over_states.astype(F32).astype(BF16)
    over_states_twice = jnp.concatenate([over_states, over_states], axis=0)

    def load_leaves(pair, carry):
        first = pl.multiple_of(pair * 2 * chunk, chunk)
        pieces = []
        for block in range(states // 2):
            a = input_ref[pl.ds(first + block * site_own, site_own), :]
            b = input_ref[pl.ds(first + chunk + block * site_own, site_own), :]
            pieces.append(jnp.where(left[:site_own], a, pltpu.roll(b, LANES // 2, 1)))
            pieces.append(jnp.where(left[:site_own], pltpu.roll(a, LANES // 2, 1), b))
        stacked = jnp.concatenate(pieces + pieces, axis=0)
        turned = stacked.T
        store_current(2 * pair, turned[:node_dev])
        store_current(2 * pair + 1, turned[node_dev:])
        return carry

    lax.fori_loop(0, owners // 2, load_leaves, 0, unroll=LEAF_UNROLL)

    node_row = lax.broadcasted_iota(jnp.int32, (node_dev, LANES), 0).astype(F32) + 1.0
    pair_row = lax.broadcasted_iota(jnp.int32, (half, slots), 0).astype(F32) + 1.0
    blank = jnp.zeros((half, LANES), BF16)

    def spread(level):
        def body(pair, carry):
            rows = current_ref[pl.ds(pl.multiple_of(pair * 2 * half, 2 * half), 2 * half), :]
            both = jnp.concatenate(
                [
                    jnp.concatenate([rows[:half], blank], axis=0),
                    jnp.concatenate([blank, rows[half:]], axis=0),
                ],
                axis=1,
            )
            for part in range(2):
                hot = []
                for side in range(2):
                    child = child_ref[
                        pl.ds((2 * pair + side) * child_rows + level * 2 + part, 1), :
                    ]
                    hot += [(node_row == child).astype(F32).astype(BF16)] * 2
                picked = lax.dot_general(
                    jnp.concatenate(hot, axis=0), both, (((0,), (0,)), ((), ())),
                    preferred_element_type=F32,
                )
                for side in range(2):
                    slot_ref[
                        pl.ds(part * half * pitch + 2 * pair + side, half, stride=pitch), :
                    ] = picked[:, side * LANES : (side + 1) * LANES]
            return carry

        lax.fori_loop(0, owners // 2, body, 0, unroll=SPREAD_UNROLL)

    def code_of(level, dest):
        return table_ref[pl.ds(level * (fields - 1) * owners + dest, 1), :]

    part_row = lax.broadcasted_iota(jnp.int32, (8, slots), 0)
    part_rank = lax.broadcasted_iota(jnp.int32, (8, LANES), 0)
    part_left = lax.broadcasted_iota(jnp.int32, (8, LANES), 1) < LANES // 2
    sides = jnp.where(
        (part_left & (part_rank < 3)) | (~part_left & (part_rank >= 3) & (part_rank < 6)), 1.0, 0.0
    ).astype(BF16)

    def factor_of(level, dest):
        base = level * (fields - 1) * owners + dest
        weight = table_ref[pl.ds(base + owners, 1), :]
        survival = table_ref[pl.ds(base + 2 * owners, 1), :]
        stacked = jnp.zeros((8, slots), F32)
        for side, scale in enumerate((weight * survival, weight * ((1.0 - survival) * 0.25))):
            for part in range(3):
                high = scale.astype(BF16).astype(F32)
                stacked = jnp.where(part_row == 3 * side + part, high, stacked)
                scale = scale - high
        return lax.dot_general(
            stacked.astype(BF16), sides, (((0,), (0,)), ((), ())), preferred_element_type=F32
        )

    def gather(level, last):
        def body(dest, carry):
            rows = jnp.concatenate(
                [
                    slot_ref[pl.ds((rank * owners + dest) * pitch, owners), :]
                    for rank in range(4)
                ],
                axis=0,
            )
            factor = factor_of(level, dest)
            weighted = both_parts(rows * factor)
            if last:
                weighted_ref[pl.ds(pl.multiple_of(dest * slots, slots), slots), :] = weighted
            hit = (pair_row == code_of(level, dest)).astype(F32).astype(BF16)
            product = jnp.dot(hit, weighted, preferred_element_type=F32)
            sums_ref[pl.ds(pl.multiple_of(dest * half, half), half), :] = both_parts(
                product[:, :LANES] + product[:, LANES:]
            )
            return carry

        lax.fori_loop(0, owners, body, 0, unroll=GATHER_UNROLL)

    def pair_sums(group):
        rows = GROUP * half
        start = pl.multiple_of(group * rows, rows)
        sums = jnp.dot(sums_ref[pl.ds(start, rows), :], settle, preferred_element_type=F32)
        first = [sums[item * half : item * half + node_dev] for item in range(GROUP)]
        second = [sums[item * half + node_dev : (item + 1) * half] for item in range(GROUP)]
        return jnp.concatenate(first, axis=0), jnp.concatenate(second, axis=0)

    group_nodes = GROUP * node_dev

    def finish():
        def body(group, carry):
            first, second = pair_sums(group)
            value = first * second
            for item in range(GROUP):
                store_current(
                    group * GROUP + item, value[item * node_dev : (item + 1) * node_dev]
                )
            return carry

        lax.fori_loop(0, owners // GROUP, body, 0, unroll=FINISH_UNROLL)

    def finish_last():
        lane = lax.broadcasted_iota(jnp.int32, (group_nodes, LANES), 1)
        wide_left = lax.broadcasted_iota(jnp.int32, (GROUP * half, LANES), 1) < LANES // 2

        def body(group, carry):
            first, second = pair_sums(group)
            scaled = scaled_ref[...]
            likelihood = 0.125 * jnp.dot(
                both_parts(first * second), over_states_twice, preferred_element_type=F32
            )
            logs = scaled * jnp.log(likelihood)
            high = logs.astype(BF16).astype(F32)
            middle = (logs - high).astype(BF16).astype(F32)
            packed = jnp.where(
                lane < site_own, high,
                jnp.where(
                    lane < 2 * site_own, middle,
                    jnp.where(lane < 3 * site_own, logs - high - middle, 0.0),
                ),
            )
            score_ref[pl.ds(group, 1), :] = lax.dot_general(
                jnp.ones((8, LANES), BF16), packed.astype(BF16), (((1,), (1,)), ((), ())),
                preferred_element_type=F32,
            )[:1]
            factor = scaled * 0.25 / likelihood
            first, second = second * factor, first * factor
            adjoint = jnp.concatenate(
                [
                    value[item * node_dev : (item + 1) * node_dev]
                    for item in range(GROUP)
                    for value in (first, second)
                ],
                axis=0,
            )
            summed = 0.5 * jnp.dot(
                both_parts(adjoint), over_states_twice, preferred_element_type=F32
            )
            start = pl.multiple_of(group * GROUP * half, GROUP * half)
            adjoint_ref[pl.ds(start, GROUP * half), :] = both_parts(
                jnp.where(wide_left, adjoint, summed)
            )
            return carry

        lax.fori_loop(0, owners // GROUP, body, 0, unroll=LAST_UNROLL)

    def edges(level):
        def body(dest, carry):
            parts = adjoint_ref[pl.ds(pl.multiple_of(dest * half, half), half), :]
            high = parts[:, :LANES]
            against = lax.dot_general(
                jnp.concatenate(
                    [
                        jnp.concatenate([high, high], axis=1),
                        jnp.concatenate([parts[:, LANES:], jnp.zeros_like(high)], axis=1),
                    ],
                    axis=0,
                ),
                weighted_ref[pl.ds(pl.multiple_of(dest * slots, slots), slots), :],
                (((1,), (1,)), ((), ())), preferred_element_type=F32,
            )
            edge = jnp.sum(
                jnp.where(
                    pair_row == code_of(level, dest), against[:half] + against[half:], 0.0
                ),
                axis=0, keepdims=True,
            )
            for part in range(2):
                term_ref[pl.ds(part * owners + dest, 1), :] = edge[
                    :, part * LANES : (part + 1) * LANES
                ]
            return carry

        lax.fori_loop(0, owners, body, 0, unroll=EDGE_UNROLL)

    for level in range(levels):
        spread(level)
        gather(level, level == levels - 1)
        if level < levels - 1:
            finish()
    finish_last()
    edges(levels - 1)

    score = score_ref[...]
    score_high = score.astype(BF16)
    score_rest = score - score_high.astype(F32)
    score_middle = score_rest.astype(BF16)
    score_low = (score_rest - score_middle.astype(F32)).astype(BF16)
    totals = [jnp.zeros((1, LANES), F32), jnp.zeros((1, LANES), F32)]
    for chunk in range(topo_ref.shape[0]):
        entry = topo_ref[chunk : chunk + 1, :]
        group_of = entry // group_nodes
        local_of = entry - group_of * group_nodes
        group_row = lax.broadcasted_iota(jnp.int32, (owners // GROUP, LANES), 0)
        group_hot = (group_row == group_of).astype(F32).astype(BF16)
        found = sum(
            lax.dot_general(piece, group_hot, (((0,), (0,)), ((), ())), preferred_element_type=F32)
            for piece in (score_high, score_middle, score_low)
        )
        row = lax.broadcasted_iota(jnp.int32, (group_nodes, LANES), 0)
        totals[chunk * 2 // topo_ref.shape[0]] = totals[chunk * 2 // topo_ref.shape[0]] + jnp.sum(
            jnp.where(row == local_of, found, 0.0), axis=0, keepdims=True
        )
    def place(row, block):
        turned = block.T
        out_ref[pl.ds(row, owners, stride=out_rows), : 2 * block.shape[0]] = jnp.concatenate(
            [turned[:owners], turned[owners:]], axis=1
        )

    for part in range(2):
        place(part, term_ref[part * owners : (part + 1) * owners, :])
    place(2, jnp.concatenate(totals + [jnp.zeros((6, LANES), F32)], axis=0))


def on_device(leaf_partials, dag_edges, weights, lengths, counts, topo_nodes):
    node_dev, states, site_dev = leaf_partials.shape
    levels, edge_dev, _ = dag_edges.shape
    owners = lax.axis_size("node")
    device = lax.axis_index("node")
    sites_all = site_dev * lax.axis_size("site")
    site_own = site_dev // owners
    ranks = 4
    slots = ranks * owners
    fields = 4
    topo_dev, use = topo_nodes.shape

    halves = topo_dev // 2
    vmem = pl.BlockSpec(memory_space=pltpu.VMEM)
    smem = pl.BlockSpec(memory_space=pltpu.SMEM)
    shares = lax.axis_size("site")
    share_rows = -(-(fields * levels * 2 + 1) // (8 * shares)) * 8
    place = lax.axis_index("site")
    share, slot = pl.pallas_call(
        functools.partial(
            slot_kernel, levels=levels, owners=owners, node_dev=node_dev, fields=fields,
            share_rows=share_rows,
        ),
        in_specs=[smem] + [vmem] * 4,
        out_shape=[
            jax.ShapeDtypeStruct((owners * share_rows, LANES), F32),
            jax.ShapeDtypeStruct((levels, edge_dev), jnp.int32),
        ],
        scratch_shapes=[pltpu.VMEM((share_rows * shares, LANES), F32)],
    )(
        jnp.stack([device, place]).astype(jnp.int32),
        dag_edges.transpose(2, 0, 1).reshape(3 * levels, edge_dev), weights, lengths,
        topo_nodes.reshape(1, -1),
    )
    share = lax.all_to_all(
        share.reshape(owners, share_rows, LANES), "node",
        split_axis=0, concat_axis=0, tiled=True,
    ).reshape(owners * share_rows, LANES)
    met = [share] + [
        lax.ppermute(share, "site", [(k, (k + step) % shares) for k in range(shares)])
        for step in range(1, shares)
    ]
    entries = use * halves
    child_table, edge_table, topologies = pl.pallas_call(
        functools.partial(
            table_kernel, levels=levels, owners=owners, fields=fields, shares=shares,
            share_rows=share_rows, entries=entries,
        ),
        in_specs=[smem] + [vmem] * shares,
        out_shape=[
            jax.ShapeDtypeStruct((owners * share_rows, LANES), F32),
            jax.ShapeDtypeStruct((levels * (fields - 1) * owners, slots), F32),
            jax.ShapeDtypeStruct((entries, LANES), jnp.int32),
        ],
        scratch_shapes=[pltpu.VMEM((owners * share_rows * shares, LANES), F32)],
        compiler_params=pltpu.CompilerParams(vmem_limit_bytes=8 * 1024 * 1024),
    )(place.astype(jnp.int32).reshape(1), *met)

    chunk = states // 2 * site_own
    peers = LANES // site_own
    packed = pl.pallas_call(
        functools.partial(pack_kernel, site_own=site_own),
        grid=(site_dev // LANES,),
        in_specs=[pl.BlockSpec((node_dev, states, LANES), lambda step: (0, 0, step))],
        out_specs=pl.BlockSpec((peers * chunk, LANES), lambda step: (step, 0)),
        out_shape=jax.ShapeDtypeStruct((owners * chunk, LANES), F32),
    )(leaf_partials)
    received = lax.all_to_all(
        packed.reshape(owners, chunk, LANES), "node", split_axis=0, concat_axis=0, tiled=True
    ).reshape(owners * chunk, LANES)
    own_counts = lax.dynamic_slice_in_dim(counts, device * site_own, site_own)
    scaled = jnp.tile(own_counts.astype(F32) / sites_all, LANES // site_own)[None, :]

    out_rows = 8
    partial = pl.pallas_call(
        functools.partial(
            dag_kernel, levels=levels, owners=owners, node_dev=node_dev, site_own=site_own,
            states=states, fields=fields, out_rows=out_rows,
        ),
        in_specs=[vmem] * 5,
        out_shape=jax.ShapeDtypeStruct((owners * out_rows, LANES), F32),
        scratch_shapes=[
            pltpu.VMEM((2 * owners * node_dev, LANES), BF16),
            pltpu.VMEM((slots * (owners + 1), LANES), F32),
            pltpu.VMEM((owners // GROUP, GROUP * node_dev), F32),
            pltpu.VMEM((2 * owners, LANES), F32),
            pltpu.VMEM((2 * owners * node_dev, 2 * LANES), BF16),
            pltpu.VMEM((2 * owners * node_dev, 2 * LANES), BF16),
            pltpu.VMEM((owners * slots, 2 * LANES), BF16),
        ],
        compiler_params=pltpu.CompilerParams(vmem_limit_bytes=40 * 1024 * 1024),
    )(received, child_table, edge_table, topologies, scaled)
    shares = lax.all_to_all(
        partial.reshape(owners, out_rows, LANES), "node", split_axis=0, concat_axis=0, tiled=True
    )
    mine = lax.psum(jnp.sum(shares[:, : slots // LANES + 1], axis=0), "site").reshape(-1)
    multiplicity = jnp.sum(
        (topologies.reshape(-1)[None, :] == dag_edges[levels - 1, :, 1][:, None]).astype(F32), axis=1
    )
    edge_gradient = multiplicity / weights[levels - 1] * jnp.sum(
        jnp.where(slot[levels - 1][:, None] == jnp.arange(slots)[None, :], mine[None, :slots], 0.0),
        axis=1,
    )
    topology = mine[slots : slots + 16].reshape(2, 8)[:, :halves].T.reshape(-1)
    return (topology, edge_gradient)


def solution(mesh):
    return jax.shard_map(
        on_device,
        mesh=mesh,
        in_specs=(
            P("node", None, "site"),
            P(None, "node", None),
            P(None, "node"),
            P(None, "node"),
            P("site"),
            P("node", None),
        ),
        out_specs=(P("node"), P("node")),
        check_vma=False,
    )
```

```python
import functools

import jax
import jax.numpy as jnp
from jax import lax
from jax.experimental import pallas as pl
from jax.experimental.pallas import tpu as pltpu
from jax.sharding import PartitionSpec as P

F32 = jnp.float32
BF16 = jnp.bfloat16
SPREAD_UNROLL = 8
GATHER_UNROLL = 8
FINISH_UNROLL = 4
LAST_UNROLL = 4
EDGE_UNROLL = 8
LEAF_UNROLL = 4
LANES = 128
GROUP = 4


def pack_kernel(leaf_ref, out_ref, *, site_own):
    states = leaf_ref.shape[1]
    chunk = states // 2 * site_own
    for pair in range(states // 2):
        rows = jnp.concatenate([leaf_ref[:, 2 * pair, :], leaf_ref[:, 2 * pair + 1, :]], axis=0).T
        for peer in range(LANES // site_own):
            out_ref[peer * chunk + pair * site_own : peer * chunk + (pair + 1) * site_own, :] = (
                rows[peer * site_own : (peer + 1) * site_own]
            )


def slot_kernel(
    dag_ref, weight_ref, length_ref, topo_ref, share_ref, slot_ref, meta_ref,
    *, levels, owners, node_dev, fields, share_rows,
):
    edges = weight_ref.shape[1]
    slots = 4 * owners

    def rows(count):
        return lax.broadcasted_iota(jnp.int32, (count, edges), 0)

    earlier = rows(edges) < lax.broadcasted_iota(jnp.int32, (edges, edges), 1)
    earlier = earlier.astype(F32).astype(BF16)
    meta_ref[...] = jnp.zeros(meta_ref.shape, F32)
    field_row = rows(8)
    for level in range(levels):
        child = dag_ref[0, level : level + 1, :] - lax.axis_index("node") * node_dev
        parent = dag_ref[1, level : level + 1, :]
        rotation = dag_ref[2, level : level + 1, :]
        owner_of = parent // node_dev
        code = rotation * node_dev + parent - owner_of * node_dev
        goes = (rows(owners) == owner_of).astype(F32)
        before = jnp.dot(goes.astype(BF16), earlier, preferred_element_type=F32)
        rank = jnp.sum(goes * before, axis=0, keepdims=True)
        slot = rank.astype(jnp.int32) * owners + owner_of
        slot_ref[level : level + 1, :] = slot
        values = jnp.zeros((8, edges), F32)
        for field, value in enumerate(
            (
                (child + 1).astype(F32), (code + 1).astype(F32), weight_ref[level : level + 1, :],
                jnp.exp(length_ref[level : level + 1, :] * (-4.0 / 3.0)),
            )
        ):
            values = jnp.where(field_row == field, value, values)
        parts = []
        for _ in range(3):
            parts.append(values.astype(BF16).astype(F32))
            values = values - parts[-1]
        found = lax.dot_general(
            jnp.concatenate(parts, axis=0).astype(BF16),
            (rows(slots) == slot).astype(F32).astype(BF16),
            (((1,), (1,)), ((), ())), preferred_element_type=F32,
        )
        found = found[:8] + found[8:16] + found[16:]
        for field in range(fields):
            for part in range(2):
                row = (field * levels + level) * 2 + part
                meta_ref[row : row + 1, :] = found[
                    field : field + 1, part * LANES : (part + 1) * LANES
                ]
    row = fields * levels * 2
    use = topo_ref.shape[1]
    for topology in range(topo_ref.shape[0]):
        meta_ref[row : row + 1, topology * use : (topology + 1) * use] = topo_ref[
            topology : topology + 1, :
        ].astype(F32)
    place = lax.axis_index("site")
    share = meta_ref[pl.ds(pl.multiple_of(place * share_rows, share_rows), share_rows), :]
    for owner in range(owners):
        share_ref[owner * share_rows : (owner + 1) * share_rows, :] = share


def table_kernel(
    *refs, levels, owners, fields, shares, share_rows, entries,
):
    share_refs, (child_ref, table_ref, topo_ref, meta_ref) = refs[:shares], refs[shares:]
    size = owners * share_rows
    for step in range(shares):
        origin = lax.rem(lax.axis_index("site") + (shares - step), shares)
        meta_ref[pl.ds(pl.multiple_of(origin * size, size), size), :] = share_refs[step][...]

    def rows_of(row):
        return meta_ref[
            pl.ds(row // share_rows * size + row % share_rows, owners, stride=share_rows), :
        ]

    child_ref[...] = meta_ref[:size, :]
    for level in range(levels):
        for field in range(1, fields):
            for part in range(2):
                block = rows_of((field * levels + level) * 2 + part).T
                table_ref[
                    pl.ds((level * (fields - 1) + field - 1) * owners, owners),
                    part * LANES : (part + 1) * LANES,
                ] = jnp.concatenate([block[:owners], block[owners:]], axis=1)
    block = rows_of(fields * levels * 2).T
    use = entries // 2
    for part in range(2):
        start = 2 * part * use
        topo_ref[part * use : (part + 1) * use, :] = jnp.concatenate(
            [block[start : start + use], block[start + use : start + 2 * use]], axis=1
        ).astype(jnp.int32)


def two_parts(value):
    high = value.astype(BF16)
    return high, (value - high.astype(F32)).astype(BF16)


def both_parts(value):
    return jnp.concatenate(two_parts(value), axis=1)


def dag_kernel(
    input_ref, child_ref, table_ref, topo_ref, scaled_ref, out_ref,
    current_ref, slot_ref, score_ref, term_ref, sums_ref, adjoint_ref, weighted_ref,
    *, levels, owners, node_dev, site_own, states, fields, out_rows,
):
    half = 2 * node_dev
    slots = 4 * owners
    chunk = states // 2 * site_own
    child_rows = child_ref.shape[0] // owners
    pitch = slot_ref.shape[0] // slots
    left = lax.broadcasted_iota(jnp.int32, (LANES, LANES), 1) < LANES // 2

    def store_current(source, value):
        high, low = two_parts(value)
        start = pl.multiple_of(source * half, half)
        current_ref[pl.ds(start, node_dev), :] = high
        current_ref[pl.ds(start + node_dev, node_dev), :] = low

    from_lane = lax.broadcasted_iota(jnp.int32, (LANES, LANES), 0)
    to_lane = lax.broadcasted_iota(jnp.int32, (LANES, LANES), 1)
    apart = jnp.abs(from_lane - to_lane)
    over_states = apart % site_own == 0
    settle = (
        (apart % (site_own * states) == 0) | (over_states & (from_lane >= LANES // 2))
    ).astype(F32).astype(BF16)
    settle = jnp.concatenate([settle, settle], axis=0)
    over_states = over_states.astype(F32).astype(BF16)
    over_states_twice = jnp.concatenate([over_states, over_states], axis=0)

    def load_leaves(pair, carry):
        first = pl.multiple_of(pair * 2 * chunk, chunk)
        pieces = []
        for block in range(states // 2):
            a = input_ref[pl.ds(first + block * site_own, site_own), :]
            b = input_ref[pl.ds(first + chunk + block * site_own, site_own), :]
            pieces.append(jnp.where(left[:site_own], a, pltpu.roll(b, LANES // 2, 1)))
            pieces.append(jnp.where(left[:site_own], pltpu.roll(a, LANES // 2, 1), b))
        stacked = jnp.concatenate(pieces + pieces, axis=0)
        turned = stacked.T
        store_current(2 * pair, turned[:node_dev])
        store_current(2 * pair + 1, turned[node_dev:])
        return carry

    lax.fori_loop(0, owners // 2, load_leaves, 0, unroll=LEAF_UNROLL)

    node_row = lax.broadcasted_iota(jnp.int32, (node_dev, LANES), 0).astype(F32) + 1.0
    pair_row = lax.broadcasted_iota(jnp.int32, (half, slots), 0).astype(F32) + 1.0
    blank = jnp.zeros((half, LANES), BF16)

    def spread(level):
        def body(pair, carry):
            rows = current_ref[pl.ds(pl.multiple_of(pair * 2 * half, 2 * half), 2 * half), :]
            both = jnp.concatenate(
                [
                    jnp.concatenate([rows[:half], blank], axis=0),
                    jnp.concatenate([blank, rows[half:]], axis=0),
                ],
                axis=1,
            )
            for part in range(2):
                hot = []
                for side in range(2):
                    child = child_ref[
                        pl.ds((2 * pair + side) * child_rows + level * 2 + part, 1), :
                    ]
                    hot += [(node_row == child).astype(F32).astype(BF16)] * 2
                picked = lax.dot_general(
                    jnp.concatenate(hot, axis=0), both, (((0,), (0,)), ((), ())),
                    preferred_element_type=F32,
                )
                for side in range(2):
                    slot_ref[
                        pl.ds(part * half * pitch + 2 * pair + side, half, stride=pitch), :
                    ] = picked[:, side * LANES : (side + 1) * LANES]
            return carry

        lax.fori_loop(0, owners // 2, body, 0, unroll=SPREAD_UNROLL)

    def code_of(level, dest):
        return table_ref[pl.ds(level * (fields - 1) * owners + dest, 1), :]

    part_row = lax.broadcasted_iota(jnp.int32, (16, slots), 0)
    part_rank = lax.broadcasted_iota(jnp.int32, (16, 2 * LANES), 0)
    part_lane = lax.broadcasted_iota(jnp.int32, (16, 2 * LANES), 1)
    part_within = part_rank % 8
    part_left = part_lane % LANES < LANES // 2
    sides = jnp.where(
        (part_rank // 8 == part_lane // LANES)
        & (
            (part_left & (part_within < 3))
            | (~part_left & (part_within >= 3) & (part_within < 6))
        ),
        1.0, 0.0,
    ).astype(BF16)

    def factors_of(level, pair):
        stacked = jnp.zeros((16, slots), F32)
        for item in range(2):
            base = level * (fields - 1) * owners + 2 * pair + item
            weight = table_ref[pl.ds(base + owners, 1), :]
            survival = table_ref[pl.ds(base + 2 * owners, 1), :]
            for side, scale in enumerate(
                (weight * survival, weight * ((1.0 - survival) * 0.25))
            ):
                for part in range(3):
                    high = scale.astype(BF16).astype(F32)
                    stacked = jnp.where(part_row == 8 * item + 3 * side + part, high, stacked)
                    scale = scale - high
        return lax.dot_general(
            stacked.astype(BF16), sides, (((0,), (0,)), ((), ())), preferred_element_type=F32
        )

    def gather(level, last):
        def body(pair, carry):
            factors = factors_of(level, pair)
            for item in range(2):
                dest = 2 * pair + item
                rows = jnp.concatenate(
                    [
                        slot_ref[pl.ds((rank * owners + dest) * pitch, owners), :]
                        for rank in range(4)
                    ],
                    axis=0,
                )
                weighted = both_parts(rows * factors[:, item * LANES : (item + 1) * LANES])
                if last:
                    weighted_ref[
                        pl.ds(pl.multiple_of(dest * slots, slots), slots), :
                    ] = weighted
                hit = (pair_row == code_of(level, dest)).astype(F32).astype(BF16)
                product = jnp.dot(hit, weighted, preferred_element_type=F32)
                sums_ref[pl.ds(pl.multiple_of(dest * half, half), half), :] = both_parts(
                    product[:, :LANES] + product[:, LANES:]
                )
            return carry

        lax.fori_loop(0, owners // 2, body, 0, unroll=GATHER_UNROLL // 2)

    def pair_sums(group):
        rows = GROUP * half
        start = pl.multiple_of(group * rows, rows)
        sums = jnp.dot(sums_ref[pl.ds(start, rows), :], settle, preferred_element_type=F32)
        first = [sums[item * half : item * half + node_dev] for item in range(GROUP)]
        second = [sums[item * half + node_dev : (item + 1) * half] for item in range(GROUP)]
        return jnp.concatenate(first, axis=0), jnp.concatenate(second, axis=0)

    group_nodes = GROUP * node_dev

    def finish():
        def body(group, carry):
            first, second = pair_sums(group)
            value = first * second
            for item in range(GROUP):
                store_current(
                    group * GROUP + item, value[item * node_dev : (item + 1) * node_dev]
                )
            return carry

        lax.fori_loop(0, owners // GROUP, body, 0, unroll=FINISH_UNROLL)

    def finish_last():
        lane = lax.broadcasted_iota(jnp.int32, (group_nodes, LANES), 1)
        wide_left = lax.broadcasted_iota(jnp.int32, (GROUP * half, LANES), 1) < LANES // 2

        def body(group, carry):
            first, second = pair_sums(group)
            scaled = scaled_ref[...]
            likelihood = 0.125 * jnp.dot(
                both_parts(first * second), over_states_twice, preferred_element_type=F32
            )
            logs = scaled * jnp.log(likelihood)
            high = logs.astype(BF16).astype(F32)
            middle = (logs - high).astype(BF16).astype(F32)
            packed = jnp.where(
                lane < site_own, high,
                jnp.where(
                    lane < 2 * site_own, middle,
                    jnp.where(lane < 3 * site_own, logs - high - middle, 0.0),
                ),
            )
            score_ref[pl.ds(group, 1), :] = lax.dot_general(
                jnp.ones((8, LANES), BF16), packed.astype(BF16), (((1,), (1,)), ((), ())),
                preferred_element_type=F32,
            )[:1]
            factor = scaled * 0.25 / likelihood
            first, second = second * factor, first * factor
            adjoint = jnp.concatenate(
                [
                    value[item * node_dev : (item + 1) * node_dev]
                    for item in range(GROUP)
                    for value in (first, second)
                ],
                axis=0,
            )
            summed = 0.5 * jnp.dot(
                both_parts(adjoint), over_states_twice, preferred_element_type=F32
            )
            start = pl.multiple_of(group * GROUP * half, GROUP * half)
            adjoint_ref[pl.ds(start, GROUP * half), :] = both_parts(
                jnp.where(wide_left, adjoint, summed)
            )
            return carry

        lax.fori_loop(0, owners // GROUP, body, 0, unroll=LAST_UNROLL)

    def edges(level):
        def body(dest, carry):
            parts = adjoint_ref[pl.ds(pl.multiple_of(dest * half, half), half), :]
            high = parts[:, :LANES]
            against = lax.dot_general(
                jnp.concatenate(
                    [
                        jnp.concatenate([high, high], axis=1),
                        jnp.concatenate([parts[:, LANES:], jnp.zeros_like(high)], axis=1),
                    ],
                    axis=0,
                ),
                weighted_ref[pl.ds(pl.multiple_of(dest * slots, slots), slots), :],
                (((1,), (1,)), ((), ())), preferred_element_type=F32,
            )
            edge = jnp.sum(
                jnp.where(
                    pair_row == code_of(level, dest), against[:half] + against[half:], 0.0
                ),
                axis=0, keepdims=True,
            )
            for part in range(2):
                term_ref[pl.ds(part * owners + dest, 1), :] = edge[
                    :, part * LANES : (part + 1) * LANES
                ]
            return carry

        lax.fori_loop(0, owners, body, 0, unroll=EDGE_UNROLL)

    for level in range(levels):
        spread(level)
        gather(level, level == levels - 1)
        if level < levels - 1:
            finish()
    finish_last()
    edges(levels - 1)

    score = score_ref[...]
    score_high = score.astype(BF16)
    score_rest = score - score_high.astype(F32)
    score_middle = score_rest.astype(BF16)
    score_low = (score_rest - score_middle.astype(F32)).astype(BF16)
    totals = [jnp.zeros((1, LANES), F32), jnp.zeros((1, LANES), F32)]
    for chunk in range(topo_ref.shape[0]):
        entry = topo_ref[chunk : chunk + 1, :]
        group_of = entry // group_nodes
        local_of = entry - group_of * group_nodes
        group_row = lax.broadcasted_iota(jnp.int32, (owners // GROUP, LANES), 0)
        group_hot = (group_row == group_of).astype(F32).astype(BF16)
        found = sum(
            lax.dot_general(piece, group_hot, (((0,), (0,)), ((), ())), preferred_element_type=F32)
            for piece in (score_high, score_middle, score_low)
        )
        row = lax.broadcasted_iota(jnp.int32, (group_nodes, LANES), 0)
        totals[chunk * 2 // topo_ref.shape[0]] = totals[chunk * 2 // topo_ref.shape[0]] + jnp.sum(
            jnp.where(row == local_of, found, 0.0), axis=0, keepdims=True
        )
    def place(row, block):
        turned = block.T
        out_ref[pl.ds(row, owners, stride=out_rows), : 2 * block.shape[0]] = jnp.concatenate(
            [turned[:owners], turned[owners:]], axis=1
        )

    for part in range(2):
        place(part, term_ref[part * owners : (part + 1) * owners, :])
    place(2, jnp.concatenate(totals + [jnp.zeros((6, LANES), F32)], axis=0))


def on_device(leaf_partials, dag_edges, weights, lengths, counts, topo_nodes):
    node_dev, states, site_dev = leaf_partials.shape
    levels, edge_dev, _ = dag_edges.shape
    owners = lax.axis_size("node")
    device = lax.axis_index("node")
    sites_all = site_dev * lax.axis_size("site")
    site_own = site_dev // owners
    ranks = 4
    slots = ranks * owners
    fields = 4
    topo_dev, use = topo_nodes.shape

    halves = topo_dev // 2
    vmem = pl.BlockSpec(memory_space=pltpu.VMEM)
    shares = lax.axis_size("site")
    share_rows = -(-(fields * levels * 2 + 1) // (8 * shares)) * 8
    share, slot = pl.pallas_call(
        functools.partial(
            slot_kernel, levels=levels, owners=owners, node_dev=node_dev, fields=fields,
            share_rows=share_rows,
        ),
        in_specs=[vmem] * 4,
        out_shape=[
            jax.ShapeDtypeStruct((owners * share_rows, LANES), F32),
            jax.ShapeDtypeStruct((levels, edge_dev), jnp.int32),
        ],
        scratch_shapes=[pltpu.VMEM((share_rows * shares, LANES), F32)],
    )(
        dag_edges.transpose(2, 0, 1), weights, lengths, topo_nodes
    )
    share = lax.all_to_all(
        share.reshape(owners, share_rows, LANES), "node",
        split_axis=0, concat_axis=0, tiled=True,
    ).reshape(owners * share_rows, LANES)
    met = [share] + [
        lax.ppermute(share, "site", [(k, (k + step) % shares) for k in range(shares)])
        for step in range(1, shares)
    ]
    entries = use * halves
    child_table, edge_table, topologies = pl.pallas_call(
        functools.partial(
            table_kernel, levels=levels, owners=owners, fields=fields, shares=shares,
            share_rows=share_rows, entries=entries,
        ),
        in_specs=[vmem] * shares,
        out_shape=[
            jax.ShapeDtypeStruct((owners * share_rows, LANES), F32),
            jax.ShapeDtypeStruct((levels * (fields - 1) * owners, slots), F32),
            jax.ShapeDtypeStruct((entries, LANES), jnp.int32),
        ],
        scratch_shapes=[pltpu.VMEM((owners * share_rows * shares, LANES), F32)],
        compiler_params=pltpu.CompilerParams(vmem_limit_bytes=8 * 1024 * 1024),
    )(*met)

    chunk = states // 2 * site_own
    peers = LANES // site_own
    packed = pl.pallas_call(
        functools.partial(pack_kernel, site_own=site_own),
        grid=(site_dev // LANES,),
        in_specs=[pl.BlockSpec((node_dev, states, LANES), lambda step: (0, 0, step))],
        out_specs=pl.BlockSpec((peers * chunk, LANES), lambda step: (step, 0)),
        out_shape=jax.ShapeDtypeStruct((owners * chunk, LANES), F32),
    )(leaf_partials)
    received = lax.all_to_all(
        packed.reshape(owners, chunk, LANES), "node", split_axis=0, concat_axis=0, tiled=True
    ).reshape(owners * chunk, LANES)
    own_counts = lax.dynamic_slice_in_dim(counts, device * site_own, site_own)
    scaled = jnp.tile(own_counts.astype(F32) / sites_all, LANES // site_own)[None, :]

    out_rows = 8
    partial = pl.pallas_call(
        functools.partial(
            dag_kernel, levels=levels, owners=owners, node_dev=node_dev, site_own=site_own,
            states=states, fields=fields, out_rows=out_rows,
        ),
        in_specs=[vmem] * 5,
        out_shape=jax.ShapeDtypeStruct((owners * out_rows, LANES), F32),
        scratch_shapes=[
            pltpu.VMEM((2 * owners * node_dev, LANES), BF16),
            pltpu.VMEM((slots * (owners + 1), LANES), F32),
            pltpu.VMEM((owners // GROUP, GROUP * node_dev), F32),
            pltpu.VMEM((2 * owners, LANES), F32),
            pltpu.VMEM((2 * owners * node_dev, 2 * LANES), BF16),
            pltpu.VMEM((2 * owners * node_dev, 2 * LANES), BF16),
            pltpu.VMEM((owners * slots, 2 * LANES), BF16),
        ],
        compiler_params=pltpu.CompilerParams(vmem_limit_bytes=40 * 1024 * 1024),
    )(received, child_table, edge_table, topologies, scaled)
    shares = lax.all_to_all(
        partial.reshape(owners, out_rows, LANES), "node", split_axis=0, concat_axis=0, tiled=True
    )
    mine = lax.psum(jnp.sum(shares[:, : slots // LANES + 1], axis=0), "site").reshape(-1)
    multiplicity = jnp.sum(
        (topologies.reshape(-1)[None, :] == dag_edges[levels - 1, :, 1][:, None]).astype(F32), axis=1
    )
    edge_gradient = multiplicity / weights[levels - 1] * jnp.sum(
        jnp.where(slot[levels - 1][:, None] == jnp.arange(slots)[None, :], mine[None, :slots], 0.0),
        axis=1,
    )
    topology = mine[slots : slots + 16].reshape(2, 8)[:, :halves].T.reshape(-1)
    return (topology, edge_gradient)


def solution(mesh):
    return jax.shard_map(
        on_device,
        mesh=mesh,
        in_specs=(
            P("node", None, "site"),
            P(None, "node", None),
            P(None, "node"),
            P(None, "node"),
            P("site"),
            P("node", None),
        ),
        out_specs=(P("node"), P("node")),
        check_vma=False,
    )
```

```python
import functools

import jax
import jax.numpy as jnp
from jax import lax
from jax.experimental import pallas as pl
from jax.experimental.pallas import tpu as pltpu
from jax.sharding import PartitionSpec as P

F32 = jnp.float32
BF16 = jnp.bfloat16
SPREAD_UNROLL = 8
GATHER_UNROLL = 8
FINISH_UNROLL = 4
LAST_UNROLL = 4
EDGE_UNROLL = 8
LEAF_UNROLL = 4
LANES = 128
GROUP = 4


def pack_kernel(leaf_ref, out_ref, *, site_own):
    states = leaf_ref.shape[1]
    chunk = states // 2 * site_own
    for pair in range(states // 2):
        rows = jnp.concatenate([leaf_ref[:, 2 * pair, :], leaf_ref[:, 2 * pair + 1, :]], axis=0).T
        for peer in range(LANES // site_own):
            out_ref[peer * chunk + pair * site_own : peer * chunk + (pair + 1) * site_own, :] = (
                rows[peer * site_own : (peer + 1) * site_own]
            )


def slot_kernel(
    dag_ref, weight_ref, length_ref, topo_ref, meta_ref, slot_ref,
    *, levels, owners, node_dev, fields,
):
    edges = weight_ref.shape[1]
    slots = 4 * owners

    def rows(count):
        return lax.broadcasted_iota(jnp.int32, (count, edges), 0)

    earlier = rows(edges) < lax.broadcasted_iota(jnp.int32, (edges, edges), 1)
    earlier = earlier.astype(F32).astype(BF16)
    meta_ref[...] = jnp.zeros(meta_ref.shape, F32)
    field_row = rows(8)
    for level in range(levels):
        child = dag_ref[0, level : level + 1, :] - lax.axis_index("node") * node_dev
        parent = dag_ref[1, level : level + 1, :]
        rotation = dag_ref[2, level : level + 1, :]
        owner_of = parent // node_dev
        code = rotation * node_dev + parent - owner_of * node_dev
        goes = (rows(owners) == owner_of).astype(F32)
        before = jnp.dot(goes.astype(BF16), earlier, preferred_element_type=F32)
        rank = jnp.sum(goes * before, axis=0, keepdims=True)
        slot = rank.astype(jnp.int32) * owners + owner_of
        slot_ref[level : level + 1, :] = slot
        values = jnp.zeros((8, edges), F32)
        for field, value in enumerate(
            (
                (child + 1).astype(F32), (code + 1).astype(F32), weight_ref[level : level + 1, :],
                jnp.exp(length_ref[level : level + 1, :] * (-4.0 / 3.0)),
            )
        ):
            values = jnp.where(field_row == field, value, values)
        parts = []
        for _ in range(3):
            parts.append(values.astype(BF16).astype(F32))
            values = values - parts[-1]
        found = lax.dot_general(
            jnp.concatenate(parts, axis=0).astype(BF16),
            (rows(slots) == slot).astype(F32).astype(BF16),
            (((1,), (1,)), ((), ())), preferred_element_type=F32,
        )
        found = found[:8] + found[8:16] + found[16:]
        for field in range(fields):
            for part in range(2):
                row = (field * levels + level) * 2 + part
                meta_ref[row : row + 1, :] = found[
                    field : field + 1, part * LANES : (part + 1) * LANES
                ]
    row = fields * levels * 2
    use = topo_ref.shape[1]
    for topology in range(topo_ref.shape[0]):
        meta_ref[row : row + 1, topology * use : (topology + 1) * use] = topo_ref[
            topology : topology + 1, :
        ].astype(F32)


def table_kernel(
    met_ref, child_ref, table_ref, topo_ref, meta_ref,
    *, levels, owners, fields, meta_rows, entries, strides,
):
    device = lax.axis_index("node")
    pitch = meta_ref.shape[0] // owners
    child_rows = child_ref.shape[0] // owners
    for place in range(owners):
        origin = device
        for bit, stride in enumerate(strides):
            if place >> bit & 1:
                origin = lax.bitwise_xor(origin, jnp.int32(stride))
        block = met_ref[place * meta_rows : (place + 1) * meta_rows, :]
        meta_ref[pl.ds(pl.multiple_of(origin * pitch, 8), meta_rows), :] = block
        child_ref[pl.ds(pl.multiple_of(origin * child_rows, 8), child_rows), :] = block[
            :child_rows
        ]

    def rows_of(row):
        return meta_ref[pl.ds(row, owners, stride=pitch), :]

    for level in range(levels):
        for field in range(1, fields):
            for part in range(2):
                block = rows_of((field * levels + level) * 2 + part).T
                table_ref[
                    pl.ds((level * (fields - 1) + field - 1) * owners, owners),
                    part * LANES : (part + 1) * LANES,
                ] = jnp.concatenate([block[:owners], block[owners:]], axis=1)
    block = rows_of(fields * levels * 2).T
    use = entries // 2
    for part in range(2):
        start = 2 * part * use
        topo_ref[part * use : (part + 1) * use, :] = jnp.concatenate(
            [block[start : start + use], block[start + use : start + 2 * use]], axis=1
        ).astype(jnp.int32)


def two_parts(value):
    high = value.astype(BF16)
    return high, (value - high.astype(F32)).astype(BF16)


def both_parts(value):
    return jnp.concatenate(two_parts(value), axis=1)


def dag_kernel(
    input_ref, child_ref, table_ref, topo_ref, scaled_ref, out_ref,
    current_ref, slot_ref, score_ref, term_ref, sums_ref, adjoint_ref, weighted_ref,
    *, levels, owners, node_dev, site_own, states, fields, out_rows,
):
    half = 2 * node_dev
    slots = 4 * owners
    chunk = states // 2 * site_own
    child_rows = child_ref.shape[0] // owners
    pitch = slot_ref.shape[0] // slots
    left = lax.broadcasted_iota(jnp.int32, (LANES, LANES), 1) < LANES // 2

    def store_current(source, value):
        high, low = two_parts(value)
        start = pl.multiple_of(source * half, half)
        current_ref[pl.ds(start, node_dev), :] = high
        current_ref[pl.ds(start + node_dev, node_dev), :] = low

    from_lane = lax.broadcasted_iota(jnp.int32, (LANES, LANES), 0)
    to_lane = lax.broadcasted_iota(jnp.int32, (LANES, LANES), 1)
    apart = jnp.abs(from_lane - to_lane)
    over_states = apart % site_own == 0
    settle = (
        (apart % (site_own * states) == 0) | (over_states & (from_lane >= LANES // 2))
    ).astype(F32).astype(BF16)
    settle = jnp.concatenate([settle, settle], axis=0)
    over_states = over_states.astype(F32).astype(BF16)
    over_states_twice = jnp.concatenate([over_states, over_states], axis=0)

    def load_leaves(pair, carry):
        first = pl.multiple_of(pair * 2 * chunk, chunk)
        pieces = []
        for block in range(states // 2):
            a = input_ref[pl.ds(first + block * site_own, site_own), :]
            b = input_ref[pl.ds(first + chunk + block * site_own, site_own), :]
            pieces.append(jnp.where(left[:site_own], a, pltpu.roll(b, LANES // 2, 1)))
            pieces.append(jnp.where(left[:site_own], pltpu.roll(a, LANES // 2, 1), b))
        stacked = jnp.concatenate(pieces + pieces, axis=0)
        turned = stacked.T
        store_current(2 * pair, turned[:node_dev])
        store_current(2 * pair + 1, turned[node_dev:])
        return carry

    lax.fori_loop(0, owners // 2, load_leaves, 0, unroll=LEAF_UNROLL)

    node_row = lax.broadcasted_iota(jnp.int32, (node_dev, LANES), 0).astype(F32) + 1.0
    pair_row = lax.broadcasted_iota(jnp.int32, (half, slots), 0).astype(F32) + 1.0
    blank = jnp.zeros((half, LANES), BF16)

    def spread(level):
        def body(pair, carry):
            rows = current_ref[pl.ds(pl.multiple_of(pair * 2 * half, 2 * half), 2 * half), :]
            both = jnp.concatenate(
                [
                    jnp.concatenate([rows[:half], blank], axis=0),
                    jnp.concatenate([blank, rows[half:]], axis=0),
                ],
                axis=1,
            )
            for part in range(2):
                hot = []
                for side in range(2):
                    child = child_ref[
                        pl.ds((2 * pair + side) * child_rows + level * 2 + part, 1), :
                    ]
                    hot += [(node_row == child).astype(F32).astype(BF16)] * 2
                picked = lax.dot_general(
                    jnp.concatenate(hot, axis=0), both, (((0,), (0,)), ((), ())),
                    preferred_element_type=F32,
                )
                for side in range(2):
                    slot_ref[
                        pl.ds(part * half * pitch + 2 * pair + side, half, stride=pitch), :
                    ] = picked[:, side * LANES : (side + 1) * LANES]
            return carry

        lax.fori_loop(0, owners // 2, body, 0, unroll=SPREAD_UNROLL)

    def code_of(level, dest):
        return table_ref[pl.ds(level * (fields - 1) * owners + dest, 1), :]

    part_row = lax.broadcasted_iota(jnp.int32, (8, slots), 0)
    part_rank = lax.broadcasted_iota(jnp.int32, (8, LANES), 0)
    part_left = lax.broadcasted_iota(jnp.int32, (8, LANES), 1) < LANES // 2
    sides = jnp.where(
        (part_left & (part_rank < 3)) | (~part_left & (part_rank >= 3) & (part_rank < 6)), 1.0, 0.0
    ).astype(BF16)

    def factor_of(level, dest):
        base = level * (fields - 1) * owners + dest
        weight = table_ref[pl.ds(base + owners, 1), :]
        survival = table_ref[pl.ds(base + 2 * owners, 1), :]
        stacked = jnp.zeros((8, slots), F32)
        for side, scale in enumerate((weight * survival, weight * ((1.0 - survival) * 0.25))):
            for part in range(3):
                high = scale.astype(BF16).astype(F32)
                stacked = jnp.where(part_row == 3 * side + part, high, stacked)
                scale = scale - high
        return lax.dot_general(
            stacked.astype(BF16), sides, (((0,), (0,)), ((), ())), preferred_element_type=F32
        )

    def gather(level, last):
        def body(dest, carry):
            rows = jnp.concatenate(
                [
                    slot_ref[pl.ds((rank * owners + dest) * pitch, owners), :]
                    for rank in range(4)
                ],
                axis=0,
            )
            factor = factor_of(level, dest)
            weighted = both_parts(rows * factor)
            if last:
                weighted_ref[pl.ds(pl.multiple_of(dest * slots, slots), slots), :] = weighted
            hit = (pair_row == code_of(level, dest)).astype(F32).astype(BF16)
            product = jnp.dot(hit, weighted, preferred_element_type=F32)
            sums_ref[pl.ds(pl.multiple_of(dest * half, half), half), :] = both_parts(
                product[:, :LANES] + product[:, LANES:]
            )
            return carry

        lax.fori_loop(0, owners, body, 0, unroll=GATHER_UNROLL)

    def pair_sums(group):
        rows = GROUP * half
        start = pl.multiple_of(group * rows, rows)
        sums = jnp.dot(sums_ref[pl.ds(start, rows), :], settle, preferred_element_type=F32)
        first = [sums[item * half : item * half + node_dev] for item in range(GROUP)]
        second = [sums[item * half + node_dev : (item + 1) * half] for item in range(GROUP)]
        return jnp.concatenate(first, axis=0), jnp.concatenate(second, axis=0)

    group_nodes = GROUP * node_dev

    def finish():
        def body(group, carry):
            first, second = pair_sums(group)
            value = first * second
            for item in range(GROUP):
                store_current(
                    group * GROUP + item, value[item * node_dev : (item + 1) * node_dev]
                )
            return carry

        lax.fori_loop(0, owners // GROUP, body, 0, unroll=FINISH_UNROLL)

    def finish_last():
        lane = lax.broadcasted_iota(jnp.int32, (group_nodes, LANES), 1)
        wide_left = lax.broadcasted_iota(jnp.int32, (GROUP * half, LANES), 1) < LANES // 2

        def body(group, carry):
            first, second = pair_sums(group)
            scaled = scaled_ref[...]
            likelihood = 0.125 * jnp.dot(
                both_parts(first * second), over_states_twice, preferred_element_type=F32
            )
            logs = scaled * jnp.log(likelihood)
            high = logs.astype(BF16).astype(F32)
            middle = (logs - high).astype(BF16).astype(F32)
            packed = jnp.where(
                lane < site_own, high,
                jnp.where(
                    lane < 2 * site_own, middle,
                    jnp.where(lane < 3 * site_own, logs - high - middle, 0.0),
                ),
            )
            score_ref[pl.ds(group, 1), :] = lax.dot_general(
                jnp.ones((8, LANES), BF16), packed.astype(BF16), (((1,), (1,)), ((), ())),
                preferred_element_type=F32,
            )[:1]
            factor = scaled * 0.25 / likelihood
            first, second = second * factor, first * factor
            adjoint = jnp.concatenate(
                [
                    value[item * node_dev : (item + 1) * node_dev]
                    for item in range(GROUP)
                    for value in (first, second)
                ],
                axis=0,
            )
            summed = 0.5 * jnp.dot(
                both_parts(adjoint), over_states_twice, preferred_element_type=F32
            )
            start = pl.multiple_of(group * GROUP * half, GROUP * half)
            adjoint_ref[pl.ds(start, GROUP * half), :] = both_parts(
                jnp.where(wide_left, adjoint, summed)
            )
            return carry

        lax.fori_loop(0, owners // GROUP, body, 0, unroll=LAST_UNROLL)

    def edges(level):
        def body(dest, carry):
            parts = adjoint_ref[pl.ds(pl.multiple_of(dest * half, half), half), :]
            high = parts[:, :LANES]
            against = lax.dot_general(
                jnp.concatenate(
                    [
                        jnp.concatenate([high, high], axis=1),
                        jnp.concatenate([parts[:, LANES:], jnp.zeros_like(high)], axis=1),
                    ],
                    axis=0,
                ),
                weighted_ref[pl.ds(pl.multiple_of(dest * slots, slots), slots), :],
                (((1,), (1,)), ((), ())), preferred_element_type=F32,
            )
            edge = jnp.sum(
                jnp.where(
                    pair_row == code_of(level, dest), against[:half] + against[half:], 0.0
                ),
                axis=0, keepdims=True,
            )
            for part in range(2):
                term_ref[pl.ds(part * owners + dest, 1), :] = edge[
                    :, part * LANES : (part + 1) * LANES
                ]
            return carry

        lax.fori_loop(0, owners, body, 0, unroll=EDGE_UNROLL)

    for level in range(levels):
        spread(level)
        gather(level, level == levels - 1)
        if level < levels - 1:
            finish()
    finish_last()
    edges(levels - 1)

    score = score_ref[...]
    score_high = score.astype(BF16)
    score_rest = score - score_high.astype(F32)
    score_middle = score_rest.astype(BF16)
    score_low = (score_rest - score_middle.astype(F32)).astype(BF16)
    totals = [jnp.zeros((1, LANES), F32), jnp.zeros((1, LANES), F32)]
    for chunk in range(topo_ref.shape[0]):
        entry = topo_ref[chunk : chunk + 1, :]
        group_of = entry // group_nodes
        local_of = entry - group_of * group_nodes
        group_row = lax.broadcasted_iota(jnp.int32, (owners // GROUP, LANES), 0)
        group_hot = (group_row == group_of).astype(F32).astype(BF16)
        found = sum(
            lax.dot_general(piece, group_hot, (((0,), (0,)), ((), ())), preferred_element_type=F32)
            for piece in (score_high, score_middle, score_low)
        )
        row = lax.broadcasted_iota(jnp.int32, (group_nodes, LANES), 0)
        totals[chunk * 2 // topo_ref.shape[0]] = totals[chunk * 2 // topo_ref.shape[0]] + jnp.sum(
            jnp.where(row == local_of, found, 0.0), axis=0, keepdims=True
        )
    def place(row, block):
        turned = block.T
        out_ref[pl.ds(row, owners, stride=out_rows), : 2 * block.shape[0]] = jnp.concatenate(
            [turned[:owners], turned[owners:]], axis=1
        )

    for part in range(2):
        place(part, term_ref[part * owners : (part + 1) * owners, :])
    place(2, jnp.concatenate(totals + [jnp.zeros((6, LANES), F32)], axis=0))


def on_device(leaf_partials, dag_edges, weights, lengths, counts, topo_nodes):
    node_dev, states, site_dev = leaf_partials.shape
    levels, edge_dev, _ = dag_edges.shape
    owners = lax.axis_size("node")
    device = lax.axis_index("node")
    sites_all = site_dev * lax.axis_size("site")
    site_own = site_dev // owners
    ranks = 4
    slots = ranks * owners
    fields = 4
    topo_dev, use = topo_nodes.shape

    halves = topo_dev // 2
    vmem = pl.BlockSpec(memory_space=pltpu.VMEM)
    meta_rows = -(-(fields * levels * 2 + 1) // 8) * 8
    met, slot = pl.pallas_call(
        functools.partial(
            slot_kernel, levels=levels, owners=owners, node_dev=node_dev, fields=fields
        ),
        in_specs=[vmem] * 4,
        out_shape=[
            jax.ShapeDtypeStruct((meta_rows, LANES), F32),
            jax.ShapeDtypeStruct((levels, edge_dev), jnp.int32),
        ],
    )(dag_edges.transpose(2, 0, 1), weights, lengths, topo_nodes)

    def exchange(tables, stride):
        other = lax.ppermute(tables, "node", [(k, k ^ stride) for k in range(owners)])
        return jnp.concatenate([tables, other], axis=0)

    strides = [1 << bit for bit in reversed(range(owners.bit_length() - 1))]
    for stride in strides[: len(strides) // 2]:
        met = exchange(met, stride)

    chunk = states // 2 * site_own
    peers = LANES // site_own
    packed = pl.pallas_call(
        functools.partial(pack_kernel, site_own=site_own),
        grid=(site_dev // LANES,),
        in_specs=[pl.BlockSpec((node_dev, states, LANES), lambda step: (0, 0, step))],
        out_specs=pl.BlockSpec((peers * chunk, LANES), lambda step: (step, 0)),
        out_shape=jax.ShapeDtypeStruct((owners * chunk, LANES), F32),
    )(leaf_partials)
    packed, met = lax.optimization_barrier((packed, met))
    received = lax.all_to_all(
        packed.reshape(owners, chunk, LANES), "node", split_axis=0, concat_axis=0, tiled=True
    ).reshape(owners * chunk, LANES)
    for stride in strides[len(strides) // 2 :]:
        met = exchange(met, stride)
    entries = use * halves
    child_table, edge_table, topologies = pl.pallas_call(
        functools.partial(
            table_kernel, levels=levels, owners=owners, fields=fields, meta_rows=meta_rows,
            entries=entries, strides=strides,
        ),
        in_specs=[vmem],
        out_shape=[
            jax.ShapeDtypeStruct((owners * 8, LANES), F32),
            jax.ShapeDtypeStruct((levels * (fields - 1) * owners, slots), F32),
            jax.ShapeDtypeStruct((entries, LANES), jnp.int32),
        ],
        scratch_shapes=[pltpu.VMEM((owners * (meta_rows + 8), LANES), F32)],
        compiler_params=pltpu.CompilerParams(vmem_limit_bytes=8 * 1024 * 1024),
    )(met)
    own_counts = lax.dynamic_slice_in_dim(counts, device * site_own, site_own)
    scaled = jnp.tile(own_counts.astype(F32) / sites_all, LANES // site_own)[None, :]

    out_rows = 8
    partial = pl.pallas_call(
        functools.partial(
            dag_kernel, levels=levels, owners=owners, node_dev=node_dev, site_own=site_own,
            states=states, fields=fields, out_rows=out_rows,
        ),
        in_specs=[vmem] * 5,
        out_shape=jax.ShapeDtypeStruct((owners * out_rows, LANES), F32),
        scratch_shapes=[
            pltpu.VMEM((2 * owners * node_dev, LANES), BF16),
            pltpu.VMEM((slots * (owners + 1), LANES), F32),
            pltpu.VMEM((owners // GROUP, GROUP * node_dev), F32),
            pltpu.VMEM((2 * owners, LANES), F32),
            pltpu.VMEM((2 * owners * node_dev, 2 * LANES), BF16),
            pltpu.VMEM((2 * owners * node_dev, 2 * LANES), BF16),
            pltpu.VMEM((owners * slots, 2 * LANES), BF16),
        ],
        compiler_params=pltpu.CompilerParams(vmem_limit_bytes=40 * 1024 * 1024),
    )(received, child_table, edge_table, topologies, scaled)
    shares = lax.all_to_all(
        partial.reshape(owners, out_rows, LANES), "node", split_axis=0, concat_axis=0, tiled=True
    )
    mine = lax.psum(jnp.sum(shares[:, : slots // LANES + 1], axis=0), "site").reshape(-1)
    multiplicity = jnp.sum(
        (topologies.reshape(-1)[None, :] == dag_edges[levels - 1, :, 1][:, None]).astype(F32), axis=1
    )
    edge_gradient = multiplicity / weights[levels - 1] * jnp.sum(
        jnp.where(slot[levels - 1][:, None] == jnp.arange(slots)[None, :], mine[None, :slots], 0.0),
        axis=1,
    )
    topology = mine[slots : slots + 16].reshape(2, 8)[:, :halves].T.reshape(-1)
    return (topology, edge_gradient)


def solution(mesh):
    return jax.shard_map(
        on_device,
        mesh=mesh,
        in_specs=(
            P("node", None, "site"),
            P(None, "node", None),
            P(None, "node"),
            P(None, "node"),
            P("site"),
            P("node", None),
        ),
        out_specs=(P("node"), P("node")),
        check_vma=False,
    )
```

```python
import functools

import jax
import jax.numpy as jnp
from jax import lax
from jax.experimental import pallas as pl
from jax.experimental.pallas import tpu as pltpu
from jax.sharding import PartitionSpec as P

F32 = jnp.float32
BF16 = jnp.bfloat16
SPREAD_UNROLL = 16
GATHER_UNROLL = 32
FINISH_UNROLL = 8
LAST_UNROLL = 8
EDGE_UNROLL = 16
LEAF_UNROLL = 8
LANES = 128
GROUP = 4


def pack_kernel(leaf_ref, out_ref, *, site_own):
    states = leaf_ref.shape[1]
    chunk = states // 2 * site_own
    for pair in range(states // 2):
        rows = jnp.concatenate([leaf_ref[:, 2 * pair, :], leaf_ref[:, 2 * pair + 1, :]], axis=0).T
        for peer in range(LANES // site_own):
            out_ref[peer * chunk + pair * site_own : peer * chunk + (pair + 1) * site_own, :] = (
                rows[peer * site_own : (peer + 1) * site_own]
            )


def slot_kernel(
    dag_ref, weight_ref, length_ref, topo_ref, share_ref, slot_ref, meta_ref,
    *, levels, owners, node_dev, fields, share_rows,
):
    edges = weight_ref.shape[1]
    slots = 4 * owners

    def rows(count):
        return lax.broadcasted_iota(jnp.int32, (count, edges), 0)

    earlier = rows(edges) < lax.broadcasted_iota(jnp.int32, (edges, edges), 1)
    earlier = earlier.astype(F32).astype(BF16)
    meta_ref[...] = jnp.zeros(meta_ref.shape, F32)
    field_row = rows(8)
    for level in range(levels):
        child = dag_ref[0, level : level + 1, :] - lax.axis_index("node") * node_dev
        parent = dag_ref[1, level : level + 1, :]
        rotation = dag_ref[2, level : level + 1, :]
        owner_of = parent // node_dev
        code = rotation * node_dev + parent - owner_of * node_dev
        goes = (rows(owners) == owner_of).astype(F32)
        before = jnp.dot(goes.astype(BF16), earlier, preferred_element_type=F32)
        rank = jnp.sum(goes * before, axis=0, keepdims=True)
        slot = rank.astype(jnp.int32) * owners + owner_of
        slot_ref[level : level + 1, :] = slot
        values = jnp.zeros((8, edges), F32)
        for field, value in enumerate(
            (
                (child + 1).astype(F32), (code + 1).astype(F32), weight_ref[level : level + 1, :],
                jnp.exp(length_ref[level : level + 1, :] * (-4.0 / 3.0)),
            )
        ):
            values = jnp.where(field_row == field, value, values)
        parts = []
        for _ in range(3):
            parts.append(values.astype(BF16).astype(F32))
            values = values - parts[-1]
        found = lax.dot_general(
            jnp.concatenate(parts, axis=0).astype(BF16),
            (rows(slots) == slot).astype(F32).astype(BF16),
            (((1,), (1,)), ((), ())), preferred_element_type=F32,
        )
        found = found[:8] + found[8:16] + found[16:]
        for field in range(fields):
            for part in range(2):
                row = (field * levels + level) * 2 + part
                meta_ref[row : row + 1, :] = found[
                    field : field + 1, part * LANES : (part + 1) * LANES
                ]
    row = fields * levels * 2
    use = topo_ref.shape[1]
    for topology in range(topo_ref.shape[0]):
        meta_ref[row : row + 1, topology * use : (topology + 1) * use] = topo_ref[
            topology : topology + 1, :
        ].astype(F32)
    place = lax.axis_index("site")
    share = meta_ref[pl.ds(pl.multiple_of(place * share_rows, share_rows), share_rows), :]
    for owner in range(owners):
        share_ref[owner * share_rows : (owner + 1) * share_rows, :] = share


def table_kernel(
    *refs, levels, owners, fields, shares, share_rows, entries,
):
    share_refs, (child_ref, table_ref, topo_ref, meta_ref) = refs[:shares], refs[shares:]
    size = owners * share_rows
    for step in range(shares):
        origin = lax.rem(lax.axis_index("site") + (shares - step), shares)
        meta_ref[pl.ds(pl.multiple_of(origin * size, size), size), :] = share_refs[step][...]

    def rows_of(row):
        return meta_ref[
            pl.ds(row // share_rows * size + row % share_rows, owners, stride=share_rows), :
        ]

    child_ref[...] = meta_ref[:size, :]
    for level in range(levels):
        for field in range(1, fields):
            for part in range(2):
                block = rows_of((field * levels + level) * 2 + part).T
                table_ref[
                    pl.ds((level * (fields - 1) + field - 1) * owners, owners),
                    part * LANES : (part + 1) * LANES,
                ] = jnp.concatenate([block[:owners], block[owners:]], axis=1)
    block = rows_of(fields * levels * 2).T
    use = entries // 2
    for part in range(2):
        start = 2 * part * use
        topo_ref[part * use : (part + 1) * use, :] = jnp.concatenate(
            [block[start : start + use], block[start + use : start + 2 * use]], axis=1
        ).astype(jnp.int32)


def two_parts(value):
    high = value.astype(BF16)
    return high, (value - high.astype(F32)).astype(BF16)


def both_parts(value):
    return jnp.concatenate(two_parts(value), axis=1)


def dag_kernel(
    input_ref, child_ref, table_ref, topo_ref, scaled_ref, out_ref,
    current_ref, slot_ref, score_ref, term_ref, sums_ref, adjoint_ref, weighted_ref,
    *, levels, owners, node_dev, site_own, states, fields, out_rows,
):
    half = 2 * node_dev
    slots = 4 * owners
    chunk = states // 2 * site_own
    child_rows = child_ref.shape[0] // owners
    pitch = slot_ref.shape[0] // slots
    left = lax.broadcasted_iota(jnp.int32, (LANES, LANES), 1) < LANES // 2

    def store_current(source, value):
        high, low = two_parts(value)
        start = pl.multiple_of(source * half, half)
        current_ref[pl.ds(start, node_dev), :] = high
        current_ref[pl.ds(start + node_dev, node_dev), :] = low

    from_lane = lax.broadcasted_iota(jnp.int32, (LANES, LANES), 0)
    to_lane = lax.broadcasted_iota(jnp.int32, (LANES, LANES), 1)
    apart = jnp.abs(from_lane - to_lane)
    over_states = apart % site_own == 0
    settle = (
        (apart % (site_own * states) == 0) | (over_states & (from_lane >= LANES // 2))
    ).astype(F32).astype(BF16)
    settle = jnp.concatenate([settle, settle], axis=0)
    over_states = over_states.astype(F32).astype(BF16)
    over_states_twice = jnp.concatenate([over_states, over_states], axis=0)

    def load_leaves(pair, carry):
        first = pl.multiple_of(pair * 2 * chunk, chunk)
        pieces = []
        for block in range(states // 2):
            a = input_ref[pl.ds(first + block * site_own, site_own), :]
            b = input_ref[pl.ds(first + chunk + block * site_own, site_own), :]
            pieces.append(jnp.where(left[:site_own], a, pltpu.roll(b, LANES // 2, 1)))
            pieces.append(jnp.where(left[:site_own], pltpu.roll(a, LANES // 2, 1), b))
        stacked = jnp.concatenate(pieces + pieces, axis=0)
        turned = stacked.T
        store_current(2 * pair, turned[:node_dev])
        store_current(2 * pair + 1, turned[node_dev:])
        return carry

    lax.fori_loop(0, owners // 2, load_leaves, 0, unroll=LEAF_UNROLL)

    node_row = lax.broadcasted_iota(jnp.int32, (node_dev, LANES), 0).astype(F32) + 1.0
    pair_row = lax.broadcasted_iota(jnp.int32, (half, slots), 0).astype(F32) + 1.0
    blank = jnp.zeros((half, LANES), BF16)

    def spread(level):
        def body(pair, carry):
            rows = current_ref[pl.ds(pl.multiple_of(pair * 2 * half, 2 * half), 2 * half), :]
            both = jnp.concatenate(
                [
                    jnp.concatenate([rows[:half], blank], axis=0),
                    jnp.concatenate([blank, rows[half:]], axis=0),
                ],
                axis=1,
            )
            for part in range(2):
                hot = []
                for side in range(2):
                    child = child_ref[
                        pl.ds((2 * pair + side) * child_rows + level * 2 + part, 1), :
                    ]
                    hot += [(node_row == child).astype(F32).astype(BF16)] * 2
                picked = lax.dot_general(
                    jnp.concatenate(hot, axis=0), both, (((0,), (0,)), ((), ())),
                    preferred_element_type=F32,
                )
                for side in range(2):
                    slot_ref[
                        pl.ds(part * half * pitch + 2 * pair + side, half, stride=pitch), :
                    ] = picked[:, side * LANES : (side + 1) * LANES]
            return carry

        lax.fori_loop(0, owners // 2, body, 0, unroll=SPREAD_UNROLL)

    def code_of(level, dest):
        return table_ref[pl.ds(level * (fields - 1) * owners + dest, 1), :]

    part_row = lax.broadcasted_iota(jnp.int32, (8, slots), 0)
    part_rank = lax.broadcasted_iota(jnp.int32, (8, LANES), 0)
    part_left = lax.broadcasted_iota(jnp.int32, (8, LANES), 1) < LANES // 2
    sides = jnp.where(
        (part_left & (part_rank < 3)) | (~part_left & (part_rank >= 3) & (part_rank < 6)), 1.0, 0.0
    ).astype(BF16)

    def factor_of(level, dest):
        base = level * (fields - 1) * owners + dest
        weight = table_ref[pl.ds(base + owners, 1), :]
        survival = table_ref[pl.ds(base + 2 * owners, 1), :]
        stacked = jnp.zeros((8, slots), F32)
        for side, scale in enumerate((weight * survival, weight * ((1.0 - survival) * 0.25))):
            for part in range(3):
                high = scale.astype(BF16).astype(F32)
                stacked = jnp.where(part_row == 3 * side + part, high, stacked)
                scale = scale - high
        return lax.dot_general(
            stacked.astype(BF16), sides, (((0,), (0,)), ((), ())), preferred_element_type=F32
        )

    def gather(level, last):
        def body(dest, carry):
            rows = jnp.concatenate(
                [
                    slot_ref[pl.ds((rank * owners + dest) * pitch, owners), :]
                    for rank in range(4)
                ],
                axis=0,
            )
            factor = factor_of(level, dest)
            weighted = both_parts(rows * factor)
            if last:
                weighted_ref[pl.ds(pl.multiple_of(dest * slots, slots), slots), :] = weighted
            hit = (pair_row == code_of(level, dest)).astype(F32).astype(BF16)
            product = jnp.dot(hit, weighted, preferred_element_type=F32)
            sums_ref[pl.ds(pl.multiple_of(dest * half, half), half), :] = both_parts(
                product[:, :LANES] + product[:, LANES:]
            )
            return carry

        lax.fori_loop(0, owners, body, 0, unroll=GATHER_UNROLL)

    def pair_sums(group):
        rows = GROUP * half
        start = pl.multiple_of(group * rows, rows)
        sums = jnp.dot(sums_ref[pl.ds(start, rows), :], settle, preferred_element_type=F32)
        first = [sums[item * half : item * half + node_dev] for item in range(GROUP)]
        second = [sums[item * half + node_dev : (item + 1) * half] for item in range(GROUP)]
        return jnp.concatenate(first, axis=0), jnp.concatenate(second, axis=0)

    group_nodes = GROUP * node_dev

    def finish():
        def body(group, carry):
            first, second = pair_sums(group)
            value = first * second
            for item in range(GROUP):
                store_current(
                    group * GROUP + item, value[item * node_dev : (item + 1) * node_dev]
                )
            return carry

        lax.fori_loop(0, owners // GROUP, body, 0, unroll=FINISH_UNROLL)

    def finish_last():
        lane = lax.broadcasted_iota(jnp.int32, (group_nodes, LANES), 1)
        wide_left = lax.broadcasted_iota(jnp.int32, (GROUP * half, LANES), 1) < LANES // 2

        def body(group, carry):
            first, second = pair_sums(group)
            scaled = scaled_ref[...]
            likelihood = 0.125 * jnp.dot(
                both_parts(first * second), over_states_twice, preferred_element_type=F32
            )
            logs = scaled * jnp.log(likelihood)
            high = logs.astype(BF16).astype(F32)
            middle = (logs - high).astype(BF16).astype(F32)
            packed = jnp.where(
                lane < site_own, high,
                jnp.where(
                    lane < 2 * site_own, middle,
                    jnp.where(lane < 3 * site_own, logs - high - middle, 0.0),
                ),
            )
            score_ref[pl.ds(group, 1), :] = lax.dot_general(
                jnp.ones((8, LANES), BF16), packed.astype(BF16), (((1,), (1,)), ((), ())),
                preferred_element_type=F32,
            )[:1]
            factor = scaled * 0.25 / likelihood
            first, second = second * factor, first * factor
            adjoint = jnp.concatenate(
                [
                    value[item * node_dev : (item + 1) * node_dev]
                    for item in range(GROUP)
                    for value in (first, second)
                ],
                axis=0,
            )
            summed = 0.5 * jnp.dot(
                both_parts(adjoint), over_states_twice, preferred_element_type=F32
            )
            start = pl.multiple_of(group * GROUP * half, GROUP * half)
            adjoint_ref[pl.ds(start, GROUP * half), :] = both_parts(
                jnp.where(wide_left, adjoint, summed)
            )
            return carry

        lax.fori_loop(0, owners // GROUP, body, 0, unroll=LAST_UNROLL)

    def edges(level):
        def body(dest, carry):
            parts = adjoint_ref[pl.ds(pl.multiple_of(dest * half, half), half), :]
            high = parts[:, :LANES]
            against = lax.dot_general(
                jnp.concatenate(
                    [
                        jnp.concatenate([high, high], axis=1),
                        jnp.concatenate([parts[:, LANES:], jnp.zeros_like(high)], axis=1),
                    ],
                    axis=0,
                ),
                weighted_ref[pl.ds(pl.multiple_of(dest * slots, slots), slots), :],
                (((1,), (1,)), ((), ())), preferred_element_type=F32,
            )
            edge = jnp.sum(
                jnp.where(
                    pair_row == code_of(level, dest), against[:half] + against[half:], 0.0
                ),
                axis=0, keepdims=True,
            )
            for part in range(2):
                term_ref[pl.ds(part * owners + dest, 1), :] = edge[
                    :, part * LANES : (part + 1) * LANES
                ]
            return carry

        lax.fori_loop(0, owners, body, 0, unroll=EDGE_UNROLL)

    for level in range(levels):
        spread(level)
        gather(level, level == levels - 1)
        if level < levels - 1:
            finish()
    finish_last()
    edges(levels - 1)

    score = score_ref[...]
    score_high = score.astype(BF16)
    score_rest = score - score_high.astype(F32)
    score_middle = score_rest.astype(BF16)
    score_low = (score_rest - score_middle.astype(F32)).astype(BF16)
    totals = [jnp.zeros((1, LANES), F32), jnp.zeros((1, LANES), F32)]
    for chunk in range(topo_ref.shape[0]):
        entry = topo_ref[chunk : chunk + 1, :]
        group_of = entry // group_nodes
        local_of = entry - group_of * group_nodes
        group_row = lax.broadcasted_iota(jnp.int32, (owners // GROUP, LANES), 0)
        group_hot = (group_row == group_of).astype(F32).astype(BF16)
        found = sum(
            lax.dot_general(piece, group_hot, (((0,), (0,)), ((), ())), preferred_element_type=F32)
            for piece in (score_high, score_middle, score_low)
        )
        row = lax.broadcasted_iota(jnp.int32, (group_nodes, LANES), 0)
        totals[chunk * 2 // topo_ref.shape[0]] = totals[chunk * 2 // topo_ref.shape[0]] + jnp.sum(
            jnp.where(row == local_of, found, 0.0), axis=0, keepdims=True
        )
    def place(row, block):
        turned = block.T
        out_ref[pl.ds(row, owners, stride=out_rows), : 2 * block.shape[0]] = jnp.concatenate(
            [turned[:owners], turned[owners:]], axis=1
        )

    for part in range(2):
        place(part, term_ref[part * owners : (part + 1) * owners, :])
    place(2, jnp.concatenate(totals + [jnp.zeros((6, LANES), F32)], axis=0))


def on_device(leaf_partials, dag_edges, weights, lengths, counts, topo_nodes):
    node_dev, states, site_dev = leaf_partials.shape
    levels, edge_dev, _ = dag_edges.shape
    owners = lax.axis_size("node")
    device = lax.axis_index("node")
    sites_all = site_dev * lax.axis_size("site")
    site_own = site_dev // owners
    ranks = 4
    slots = ranks * owners
    fields = 4
    topo_dev, use = topo_nodes.shape

    halves = topo_dev // 2
    vmem = pl.BlockSpec(memory_space=pltpu.VMEM)
    shares = lax.axis_size("site")
    share_rows = -(-(fields * levels * 2 + 1) // (8 * shares)) * 8
    share, slot = pl.pallas_call(
        functools.partial(
            slot_kernel, levels=levels, owners=owners, node_dev=node_dev, fields=fields,
            share_rows=share_rows,
        ),
        in_specs=[vmem] * 4,
        out_shape=[
            jax.ShapeDtypeStruct((owners * share_rows, LANES), F32),
            jax.ShapeDtypeStruct((levels, edge_dev), jnp.int32),
        ],
        scratch_shapes=[pltpu.VMEM((share_rows * shares, LANES), F32)],
    )(
        dag_edges.transpose(2, 0, 1), weights, lengths, topo_nodes
    )
    share = lax.all_to_all(
        share.reshape(owners, share_rows, LANES), "node",
        split_axis=0, concat_axis=0, tiled=True,
    ).reshape(owners * share_rows, LANES)
    met = [share] + [
        lax.ppermute(share, "site", [(k, (k + step) % shares) for k in range(shares)])
        for step in range(1, shares)
    ]
    entries = use * halves
    child_table, edge_table, topologies = pl.pallas_call(
        functools.partial(
            table_kernel, levels=levels, owners=owners, fields=fields, shares=shares,
            share_rows=share_rows, entries=entries,
        ),
        in_specs=[vmem] * shares,
        out_shape=[
            jax.ShapeDtypeStruct((owners * share_rows, LANES), F32),
            jax.ShapeDtypeStruct((levels * (fields - 1) * owners, slots), F32),
            jax.ShapeDtypeStruct((entries, LANES), jnp.int32),
        ],
        scratch_shapes=[pltpu.VMEM((owners * share_rows * shares, LANES), F32)],
        compiler_params=pltpu.CompilerParams(vmem_limit_bytes=8 * 1024 * 1024),
    )(*met)

    chunk = states // 2 * site_own
    peers = LANES // site_own
    packed = pl.pallas_call(
        functools.partial(pack_kernel, site_own=site_own),
        grid=(site_dev // LANES,),
        in_specs=[pl.BlockSpec((node_dev, states, LANES), lambda step: (0, 0, step))],
        out_specs=pl.BlockSpec((peers * chunk, LANES), lambda step: (step, 0)),
        out_shape=jax.ShapeDtypeStruct((owners * chunk, LANES), F32),
    )(leaf_partials)
    received = lax.all_to_all(
        packed.reshape(owners, chunk, LANES), "node", split_axis=0, concat_axis=0, tiled=True
    ).reshape(owners * chunk, LANES)
    own_counts = lax.dynamic_slice_in_dim(counts, device * site_own, site_own)
    scaled = jnp.tile(own_counts.astype(F32) / sites_all, LANES // site_own)[None, :]

    out_rows = 8
    partial = pl.pallas_call(
        functools.partial(
            dag_kernel, levels=levels, owners=owners, node_dev=node_dev, site_own=site_own,
            states=states, fields=fields, out_rows=out_rows,
        ),
        in_specs=[vmem] * 5,
        out_shape=jax.ShapeDtypeStruct((owners * out_rows, LANES), F32),
        scratch_shapes=[
            pltpu.VMEM((2 * owners * node_dev, LANES), BF16),
            pltpu.VMEM((slots * (owners + 1), LANES), F32),
            pltpu.VMEM((owners // GROUP, GROUP * node_dev), F32),
            pltpu.VMEM((2 * owners, LANES), F32),
            pltpu.VMEM((2 * owners * node_dev, 2 * LANES), BF16),
            pltpu.VMEM((2 * owners * node_dev, 2 * LANES), BF16),
            pltpu.VMEM((owners * slots, 2 * LANES), BF16),
        ],
        compiler_params=pltpu.CompilerParams(vmem_limit_bytes=40 * 1024 * 1024),
    )(received, child_table, edge_table, topologies, scaled)
    shares = lax.all_to_all(
        partial.reshape(owners, out_rows, LANES), "node", split_axis=0, concat_axis=0, tiled=True
    )
    mine = lax.psum(jnp.sum(shares[:, : slots // LANES + 1], axis=0), "site").reshape(-1)
    multiplicity = jnp.sum(
        (topologies.reshape(-1)[None, :] == dag_edges[levels - 1, :, 1][:, None]).astype(F32), axis=1
    )
    edge_gradient = multiplicity / weights[levels - 1] * jnp.sum(
        jnp.where(slot[levels - 1][:, None] == jnp.arange(slots)[None, :], mine[None, :slots], 0.0),
        axis=1,
    )
    topology = mine[slots : slots + 16].reshape(2, 8)[:, :halves].T.reshape(-1)
    return (topology, edge_gradient)


def solution(mesh):
    return jax.shard_map(
        on_device,
        mesh=mesh,
        in_specs=(
            P("node", None, "site"),
            P(None, "node", None),
            P(None, "node"),
            P(None, "node"),
            P("site"),
            P("node", None),
        ),
        out_specs=(P("node"), P("node")),
        check_vma=False,
    )
```

```python
import functools

import jax
import jax.numpy as jnp
from jax import lax
from jax.experimental import pallas as pl
from jax.experimental.pallas import tpu as pltpu
from jax.sharding import PartitionSpec as P

F32 = jnp.float32
BF16 = jnp.bfloat16
SPREAD_UNROLL = 32
GATHER_UNROLL = 32
FINISH_UNROLL = 8
LAST_UNROLL = 8
EDGE_UNROLL = 32
LEAF_UNROLL = 8
LANES = 128
GROUP = 4


def pack_kernel(leaf_ref, out_ref, *, site_own):
    states = leaf_ref.shape[1]
    chunk = states // 2 * site_own
    for pair in range(states // 2):
        rows = jnp.concatenate([leaf_ref[:, 2 * pair, :], leaf_ref[:, 2 * pair + 1, :]], axis=0).T
        for peer in range(LANES // site_own):
            out_ref[peer * chunk + pair * site_own : peer * chunk + (pair + 1) * site_own, :] = (
                rows[peer * site_own : (peer + 1) * site_own]
            )


def slot_kernel(
    dag_ref, weight_ref, length_ref, topo_ref, share_ref, slot_ref, meta_ref,
    *, levels, owners, node_dev, fields, share_rows,
):
    edges = weight_ref.shape[1]
    slots = 4 * owners

    def rows(count):
        return lax.broadcasted_iota(jnp.int32, (count, edges), 0)

    earlier = rows(edges) < lax.broadcasted_iota(jnp.int32, (edges, edges), 1)
    earlier = earlier.astype(F32).astype(BF16)
    meta_ref[...] = jnp.zeros(meta_ref.shape, F32)
    field_row = rows(8)
    for level in range(levels):
        child = dag_ref[0, level : level + 1, :] - lax.axis_index("node") * node_dev
        parent = dag_ref[1, level : level + 1, :]
        rotation = dag_ref[2, level : level + 1, :]
        owner_of = parent // node_dev
        code = rotation * node_dev + parent - owner_of * node_dev
        goes = (rows(owners) == owner_of).astype(F32)
        before = jnp.dot(goes.astype(BF16), earlier, preferred_element_type=F32)
        rank = jnp.sum(goes * before, axis=0, keepdims=True)
        slot = rank.astype(jnp.int32) * owners + owner_of
        slot_ref[level : level + 1, :] = slot
        values = jnp.zeros((8, edges), F32)
        for field, value in enumerate(
            (
                (child + 1).astype(F32), (code + 1).astype(F32), weight_ref[level : level + 1, :],
                jnp.exp(length_ref[level : level + 1, :] * (-4.0 / 3.0)),
            )
        ):
            values = jnp.where(field_row == field, value, values)
        parts = []
        for _ in range(3):
            parts.append(values.astype(BF16).astype(F32))
            values = values - parts[-1]
        found = lax.dot_general(
            jnp.concatenate(parts, axis=0).astype(BF16),
            (rows(slots) == slot).astype(F32).astype(BF16),
            (((1,), (1,)), ((), ())), preferred_element_type=F32,
        )
        found = found[:8] + found[8:16] + found[16:]
        for field in range(fields):
            for part in range(2):
                row = (field * levels + level) * 2 + part
                meta_ref[row : row + 1, :] = found[
                    field : field + 1, part * LANES : (part + 1) * LANES
                ]
    row = fields * levels * 2
    use = topo_ref.shape[1]
    for topology in range(topo_ref.shape[0]):
        meta_ref[row : row + 1, topology * use : (topology + 1) * use] = topo_ref[
            topology : topology + 1, :
        ].astype(F32)
    place = lax.axis_index("site")
    share = meta_ref[pl.ds(pl.multiple_of(place * share_rows, share_rows), share_rows), :]
    for owner in range(owners):
        share_ref[owner * share_rows : (owner + 1) * share_rows, :] = share


def table_kernel(
    *refs, levels, owners, fields, shares, share_rows, entries,
):
    share_refs, (child_ref, table_ref, topo_ref, meta_ref) = refs[:shares], refs[shares:]
    size = owners * share_rows
    for step in range(shares):
        origin = lax.rem(lax.axis_index("site") + (shares - step), shares)
        meta_ref[pl.ds(pl.multiple_of(origin * size, size), size), :] = share_refs[step][...]

    def rows_of(row):
        return meta_ref[
            pl.ds(row // share_rows * size + row % share_rows, owners, stride=share_rows), :
        ]

    child_ref[...] = meta_ref[:size, :]
    for level in range(levels):
        for field in range(1, fields):
            for part in range(2):
                block = rows_of((field * levels + level) * 2 + part).T
                table_ref[
                    pl.ds((level * (fields - 1) + field - 1) * owners, owners),
                    part * LANES : (part + 1) * LANES,
                ] = jnp.concatenate([block[:owners], block[owners:]], axis=1)
    block = rows_of(fields * levels * 2).T
    use = entries // 2
    for part in range(2):
        start = 2 * part * use
        topo_ref[part * use : (part + 1) * use, :] = jnp.concatenate(
            [block[start : start + use], block[start + use : start + 2 * use]], axis=1
        ).astype(jnp.int32)


def two_parts(value):
    high = value.astype(BF16)
    return high, (value - high.astype(F32)).astype(BF16)


def both_parts(value):
    return jnp.concatenate(two_parts(value), axis=1)


def dag_kernel(
    input_ref, child_ref, table_ref, topo_ref, scaled_ref, out_ref,
    current_ref, slot_ref, score_ref, term_ref, sums_ref, adjoint_ref, weighted_ref,
    *, levels, owners, node_dev, site_own, states, fields, out_rows,
):
    half = 2 * node_dev
    slots = 4 * owners
    chunk = states // 2 * site_own
    child_rows = child_ref.shape[0] // owners
    pitch = slot_ref.shape[0] // slots
    left = lax.broadcasted_iota(jnp.int32, (LANES, LANES), 1) < LANES // 2

    def store_current(source, value):
        high, low = two_parts(value)
        start = pl.multiple_of(source * half, half)
        current_ref[pl.ds(start, node_dev), :] = high
        current_ref[pl.ds(start + node_dev, node_dev), :] = low

    from_lane = lax.broadcasted_iota(jnp.int32, (LANES, LANES), 0)
    to_lane = lax.broadcasted_iota(jnp.int32, (LANES, LANES), 1)
    apart = jnp.abs(from_lane - to_lane)
    over_states = apart % site_own == 0
    settle = (
        (apart % (site_own * states) == 0) | (over_states & (from_lane >= LANES // 2))
    ).astype(F32).astype(BF16)
    settle = jnp.concatenate([settle, settle], axis=0)
    over_states = over_states.astype(F32).astype(BF16)
    over_states_twice = jnp.concatenate([over_states, over_states], axis=0)

    def load_leaves(pair, carry):
        first = pl.multiple_of(pair * 2 * chunk, chunk)
        pieces = []
        for block in range(states // 2):
            a = input_ref[pl.ds(first + block * site_own, site_own), :]
            b = input_ref[pl.ds(first + chunk + block * site_own, site_own), :]
            pieces.append(jnp.where(left[:site_own], a, pltpu.roll(b, LANES // 2, 1)))
            pieces.append(jnp.where(left[:site_own], pltpu.roll(a, LANES // 2, 1), b))
        stacked = jnp.concatenate(pieces + pieces, axis=0)
        turned = stacked.T
        store_current(2 * pair, turned[:node_dev])
        store_current(2 * pair + 1, turned[node_dev:])
        return carry

    lax.fori_loop(0, owners // 2, load_leaves, 0, unroll=LEAF_UNROLL)

    node_row = lax.broadcasted_iota(jnp.int32, (node_dev, LANES), 0).astype(F32) + 1.0
    pair_row = lax.broadcasted_iota(jnp.int32, (half, slots), 0).astype(F32) + 1.0
    blank = jnp.zeros((half, LANES), BF16)

    def spread(level):
        def body(pair, carry):
            rows = current_ref[pl.ds(pl.multiple_of(pair * 2 * half, 2 * half), 2 * half), :]
            both = jnp.concatenate(
                [
                    jnp.concatenate([rows[:half], blank], axis=0),
                    jnp.concatenate([blank, rows[half:]], axis=0),
                ],
                axis=1,
            )
            for part in range(2):
                hot = []
                for side in range(2):
                    child = child_ref[
                        pl.ds((2 * pair + side) * child_rows + level * 2 + part, 1), :
                    ]
                    hot += [(node_row == child).astype(F32).astype(BF16)] * 2
                picked = lax.dot_general(
                    jnp.concatenate(hot, axis=0), both, (((0,), (0,)), ((), ())),
                    preferred_element_type=F32,
                )
                for side in range(2):
                    slot_ref[
                        pl.ds(part * half * pitch + 2 * pair + side, half, stride=pitch), :
                    ] = picked[:, side * LANES : (side + 1) * LANES]
            return carry

        lax.fori_loop(0, owners // 2, body, 0, unroll=SPREAD_UNROLL)

    def code_of(level, dest):
        return table_ref[pl.ds(level * (fields - 1) * owners + dest, 1), :]

    part_row = lax.broadcasted_iota(jnp.int32, (8, slots), 0)
    part_rank = lax.broadcasted_iota(jnp.int32, (8, LANES), 0)
    part_left = lax.broadcasted_iota(jnp.int32, (8, LANES), 1) < LANES // 2
    sides = jnp.where(
        (part_left & (part_rank < 3)) | (~part_left & (part_rank >= 3) & (part_rank < 6)), 1.0, 0.0
    ).astype(BF16)

    def factor_of(level, dest):
        base = level * (fields - 1) * owners + dest
        weight = table_ref[pl.ds(base + owners, 1), :]
        survival = table_ref[pl.ds(base + 2 * owners, 1), :]
        stacked = jnp.zeros((8, slots), F32)
        for side, scale in enumerate((weight * survival, weight * ((1.0 - survival) * 0.25))):
            for part in range(3):
                high = scale.astype(BF16).astype(F32)
                stacked = jnp.where(part_row == 3 * side + part, high, stacked)
                scale = scale - high
        return lax.dot_general(
            stacked.astype(BF16), sides, (((0,), (0,)), ((), ())), preferred_element_type=F32
        )

    def gather(level, last):
        def body(dest, carry):
            rows = jnp.concatenate(
                [
                    slot_ref[pl.ds((rank * owners + dest) * pitch, owners), :]
                    for rank in range(4)
                ],
                axis=0,
            )
            factor = factor_of(level, dest)
            weighted = both_parts(rows * factor)
            if last:
                weighted_ref[pl.ds(pl.multiple_of(dest * slots, slots), slots), :] = weighted
            hit = (pair_row == code_of(level, dest)).astype(F32).astype(BF16)
            product = jnp.dot(hit, weighted, preferred_element_type=F32)
            sums_ref[pl.ds(pl.multiple_of(dest * half, half), half), :] = both_parts(
                product[:, :LANES] + product[:, LANES:]
            )
            return carry

        lax.fori_loop(0, owners, body, 0, unroll=GATHER_UNROLL)

    def pair_sums(group):
        rows = GROUP * half
        start = pl.multiple_of(group * rows, rows)
        sums = jnp.dot(sums_ref[pl.ds(start, rows), :], settle, preferred_element_type=F32)
        first = [sums[item * half : item * half + node_dev] for item in range(GROUP)]
        second = [sums[item * half + node_dev : (item + 1) * half] for item in range(GROUP)]
        return jnp.concatenate(first, axis=0), jnp.concatenate(second, axis=0)

    group_nodes = GROUP * node_dev

    def finish():
        def body(group, carry):
            first, second = pair_sums(group)
            value = first * second
            for item in range(GROUP):
                store_current(
                    group * GROUP + item, value[item * node_dev : (item + 1) * node_dev]
                )
            return carry

        lax.fori_loop(0, owners // GROUP, body, 0, unroll=FINISH_UNROLL)

    def finish_last():
        lane = lax.broadcasted_iota(jnp.int32, (group_nodes, LANES), 1)
        wide_left = lax.broadcasted_iota(jnp.int32, (GROUP * half, LANES), 1) < LANES // 2

        def body(group, carry):
            first, second = pair_sums(group)
            scaled = scaled_ref[...]
            likelihood = 0.125 * jnp.dot(
                both_parts(first * second), over_states_twice, preferred_element_type=F32
            )
            logs = scaled * jnp.log(likelihood)
            high = logs.astype(BF16).astype(F32)
            middle = (logs - high).astype(BF16).astype(F32)
            packed = jnp.where(
                lane < site_own, high,
                jnp.where(
                    lane < 2 * site_own, middle,
                    jnp.where(lane < 3 * site_own, logs - high - middle, 0.0),
                ),
            )
            score_ref[pl.ds(group, 1), :] = lax.dot_general(
                jnp.ones((8, LANES), BF16), packed.astype(BF16), (((1,), (1,)), ((), ())),
                preferred_element_type=F32,
            )[:1]
            factor = scaled * 0.25 / likelihood
            first, second = second * factor, first * factor
            adjoint = jnp.concatenate(
                [
                    value[item * node_dev : (item + 1) * node_dev]
                    for item in range(GROUP)
                    for value in (first, second)
                ],
                axis=0,
            )
            summed = 0.5 * jnp.dot(
                both_parts(adjoint), over_states_twice, preferred_element_type=F32
            )
            start = pl.multiple_of(group * GROUP * half, GROUP * half)
            adjoint_ref[pl.ds(start, GROUP * half), :] = both_parts(
                jnp.where(wide_left, adjoint, summed)
            )
            return carry

        lax.fori_loop(0, owners // GROUP, body, 0, unroll=LAST_UNROLL)

    def edges(level):
        def body(dest, carry):
            parts = adjoint_ref[pl.ds(pl.multiple_of(dest * half, half), half), :]
            high = parts[:, :LANES]
            against = lax.dot_general(
                jnp.concatenate(
                    [
                        jnp.concatenate([high, high], axis=1),
                        jnp.concatenate([parts[:, LANES:], jnp.zeros_like(high)], axis=1),
                    ],
                    axis=0,
                ),
                weighted_ref[pl.ds(pl.multiple_of(dest * slots, slots), slots), :],
                (((1,), (1,)), ((), ())), preferred_element_type=F32,
            )
            edge = jnp.sum(
                jnp.where(
                    pair_row == code_of(level, dest), against[:half] + against[half:], 0.0
                ),
                axis=0, keepdims=True,
            )
            for part in range(2):
                term_ref[pl.ds(part * owners + dest, 1), :] = edge[
                    :, part * LANES : (part + 1) * LANES
                ]
            return carry

        lax.fori_loop(0, owners, body, 0, unroll=EDGE_UNROLL)

    for level in range(levels):
        spread(level)
        gather(level, level == levels - 1)
        if level < levels - 1:
            finish()
    finish_last()
    edges(levels - 1)

    score = score_ref[...]
    score_high = score.astype(BF16)
    score_rest = score - score_high.astype(F32)
    score_middle = score_rest.astype(BF16)
    score_low = (score_rest - score_middle.astype(F32)).astype(BF16)
    totals = [jnp.zeros((1, LANES), F32), jnp.zeros((1, LANES), F32)]
    for chunk in range(topo_ref.shape[0]):
        entry = topo_ref[chunk : chunk + 1, :]
        group_of = entry // group_nodes
        local_of = entry - group_of * group_nodes
        group_row = lax.broadcasted_iota(jnp.int32, (owners // GROUP, LANES), 0)
        group_hot = (group_row == group_of).astype(F32).astype(BF16)
        found = sum(
            lax.dot_general(piece, group_hot, (((0,), (0,)), ((), ())), preferred_element_type=F32)
            for piece in (score_high, score_middle, score_low)
        )
        row = lax.broadcasted_iota(jnp.int32, (group_nodes, LANES), 0)
        totals[chunk * 2 // topo_ref.shape[0]] = totals[chunk * 2 // topo_ref.shape[0]] + jnp.sum(
            jnp.where(row == local_of, found, 0.0), axis=0, keepdims=True
        )
    def place(row, block):
        turned = block.T
        out_ref[pl.ds(row, owners, stride=out_rows), : 2 * block.shape[0]] = jnp.concatenate(
            [turned[:owners], turned[owners:]], axis=1
        )

    for part in range(2):
        place(part, term_ref[part * owners : (part + 1) * owners, :])
    place(2, jnp.concatenate(totals + [jnp.zeros((6, LANES), F32)], axis=0))


def on_device(leaf_partials, dag_edges, weights, lengths, counts, topo_nodes):
    node_dev, states, site_dev = leaf_partials.shape
    levels, edge_dev, _ = dag_edges.shape
    owners = lax.axis_size("node")
    device = lax.axis_index("node")
    sites_all = site_dev * lax.axis_size("site")
    site_own = site_dev // owners
    ranks = 4
    slots = ranks * owners
    fields = 4
    topo_dev, use = topo_nodes.shape

    halves = topo_dev // 2
    vmem = pl.BlockSpec(memory_space=pltpu.VMEM)
    shares = lax.axis_size("site")
    share_rows = -(-(fields * levels * 2 + 1) // (8 * shares)) * 8
    share, slot = pl.pallas_call(
        functools.partial(
            slot_kernel, levels=levels, owners=owners, node_dev=node_dev, fields=fields,
            share_rows=share_rows,
        ),
        in_specs=[vmem] * 4,
        out_shape=[
            jax.ShapeDtypeStruct((owners * share_rows, LANES), F32),
            jax.ShapeDtypeStruct((levels, edge_dev), jnp.int32),
        ],
        scratch_shapes=[pltpu.VMEM((share_rows * shares, LANES), F32)],
    )(
        dag_edges.transpose(2, 0, 1), weights, lengths, topo_nodes
    )
    share = lax.all_to_all(
        share.reshape(owners, share_rows, LANES), "node",
        split_axis=0, concat_axis=0, tiled=True,
    ).reshape(owners * share_rows, LANES)
    met = [share] + [
        lax.ppermute(share, "site", [(k, (k + step) % shares) for k in range(shares)])
        for step in range(1, shares)
    ]
    entries = use * halves
    child_table, edge_table, topologies = pl.pallas_call(
        functools.partial(
            table_kernel, levels=levels, owners=owners, fields=fields, shares=shares,
            share_rows=share_rows, entries=entries,
        ),
        in_specs=[vmem] * shares,
        out_shape=[
            jax.ShapeDtypeStruct((owners * share_rows, LANES), F32),
            jax.ShapeDtypeStruct((levels * (fields - 1) * owners, slots), F32),
            jax.ShapeDtypeStruct((entries, LANES), jnp.int32),
        ],
        scratch_shapes=[pltpu.VMEM((owners * share_rows * shares, LANES), F32)],
        compiler_params=pltpu.CompilerParams(vmem_limit_bytes=8 * 1024 * 1024),
    )(*met)

    chunk = states // 2 * site_own
    peers = LANES // site_own
    packed = pl.pallas_call(
        functools.partial(pack_kernel, site_own=site_own),
        grid=(site_dev // LANES,),
        in_specs=[pl.BlockSpec((node_dev, states, LANES), lambda step: (0, 0, step))],
        out_specs=pl.BlockSpec((peers * chunk, LANES), lambda step: (step, 0)),
        out_shape=jax.ShapeDtypeStruct((owners * chunk, LANES), F32),
    )(leaf_partials)
    received = lax.all_to_all(
        packed.reshape(owners, chunk, LANES), "node", split_axis=0, concat_axis=0, tiled=True
    ).reshape(owners * chunk, LANES)
    own_counts = lax.dynamic_slice_in_dim(counts, device * site_own, site_own)
    scaled = jnp.tile(own_counts.astype(F32) / sites_all, LANES // site_own)[None, :]

    out_rows = 8
    partial = pl.pallas_call(
        functools.partial(
            dag_kernel, levels=levels, owners=owners, node_dev=node_dev, site_own=site_own,
            states=states, fields=fields, out_rows=out_rows,
        ),
        in_specs=[vmem] * 5,
        out_shape=jax.ShapeDtypeStruct((owners * out_rows, LANES), F32),
        scratch_shapes=[
            pltpu.VMEM((2 * owners * node_dev, LANES), BF16),
            pltpu.VMEM((slots * (owners + 1), LANES), F32),
            pltpu.VMEM((owners // GROUP, GROUP * node_dev), F32),
            pltpu.VMEM((2 * owners, LANES), F32),
            pltpu.VMEM((2 * owners * node_dev, 2 * LANES), BF16),
            pltpu.VMEM((2 * owners * node_dev, 2 * LANES), BF16),
            pltpu.VMEM((owners * slots, 2 * LANES), BF16),
        ],
        compiler_params=pltpu.CompilerParams(vmem_limit_bytes=40 * 1024 * 1024),
    )(received, child_table, edge_table, topologies, scaled)
    shares = lax.all_to_all(
        partial.reshape(owners, out_rows, LANES), "node", split_axis=0, concat_axis=0, tiled=True
    )
    mine = jnp.sum(shares[:, : slots // LANES + 1], axis=0)
    sites = lax.axis_size("site")
    for bit in range(sites.bit_length() - 1):
        mine = mine + lax.ppermute(mine, "site", [(k, k ^ (1 << bit)) for k in range(sites)])
    mine = mine.reshape(-1)
    multiplicity = jnp.sum(
        (topologies.reshape(-1)[None, :] == dag_edges[levels - 1, :, 1][:, None]).astype(F32), axis=1
    )
    scale = multiplicity / weights[levels - 1]
    edge_gradient = jnp.sum(
        jnp.where(
            slot[levels - 1][:, None] == jnp.arange(slots)[None, :],
            mine[None, :slots] * scale[:, None], 0.0,
        ),
        axis=1,
    )
    topology = mine[slots : slots + 16].reshape(2, 8)[:, :halves].T.reshape(-1)
    return (topology, edge_gradient)


def solution(mesh):
    return jax.shard_map(
        on_device,
        mesh=mesh,
        in_specs=(
            P("node", None, "site"),
            P(None, "node", None),
            P(None, "node"),
            P(None, "node"),
            P("site"),
            P("node", None),
        ),
        out_specs=(P("node"), P("node")),
        check_vma=False,
    )
```
